32 devices in a mesh: blk: 32 (over z, y, x, core).
Axes of the slice: x: 2, y: 2, z: 4, core: 2. Of those that a mesh axis runs over, the one named last changes fastest.
Arguments:
- populations: float32 [1024, 19, 512], P('blk'), may hold values from 0 to 1, as said below
- coarse_faces: float32 [64, 2, 19, 64], P('blk'), may hold values from 0 to 1, as said below
- neighbors: int32 [1024, 6], P('blk'), may hold values from -1 to 1023, as said below
- interface: int32 [1024, 2], P('blk'), may hold values from -1 to 63, as said below
- solid: int32 [1024, 512], P('blk'), may hold values from 0 to 1, as said below
Outputs:
- advanced: float32 [1024, 19, 512], P('blk')
The draws below stay inside these ranges and needn't reach their ends.
Inputs may be any that keep to these rules, and one draw needn't show every extreme that they name: `populations`: every entry is positive. `coarse_faces`: every entry is positive. `neighbors`: Symmetric: a is across face d of b exactly when b is across the opposite face of a. Blocks b with equal b // 32 share an owner. A block across a y or z face has the same owner; one across the +x (-x) face has the same owner or the next (previous) one. For each owner and each x direction at most 16 of its blocks have a neighbour with another owner, and some owner reaches 16 in each direction. The +y face of a block with interface[b, 0] >= 0 is -1 here. interface[b, 0] is owned by the next owner: interface[b, 0] // 2 == b // 32 + 1. interface[b, 1] is the quadrant, 0 to 3. Each pair of coarse block and quadrant appears at most once. `solid`: only cells with all three coordinates in 1..6 are wall cells.
All inputs are finite; a program needn't handle non-finite values.
Results may differ from the reference program's by a relative error of at most 0.0001.
Values sent between devices are 32-bit elements; how exact they have to be, the bound alone decides.
No kernel may reach another device: no remote copies, remote signals or barrier semaphores. Data moves between devices by JAX's collectives and lax.ppermute only.
A program may use at most 64 MiB of HBM per device.

```python
import jax
import jax.numpy as jnp
import numpy as np
from jax import lax

SIDE = 4
CROSS = 16
SLICES_DEV = 2
Q = 19
CELLS = 512
FACE = 64
BLK_DEV = 32
CB_DEV = 2
BLOCKS = 1024
CBLOCKS = 64
N_BLK = 32


velocity_draw = np.array([[0, 0, 0], [1, 0, 0], [-1, 0, 0], [0, 1, 0], [0, -1, 0], [0, 0, 1], [0, 0, -1], [1, 1, 0], [-1, -1, 0], [1, -1, 0], [-1, 1, 0], [1, 0, 1], [-1, 0, -1], [1, 0, -1], [-1, 0, 1], [0, 1, 1], [0, -1, -1], [0, 1, -1], [0, -1, 1]], dtype=np.float32)


weight_draw = np.array([1.0 / 3.0] + [1.0 / 18.0] * 6 + [1.0 / 36.0] * 12, dtype=np.float32)


def near_state(key, leading, cells):
    key_rho, key_vel, key_noise = jax.random.split(key, 3)
    density = 1.0 + 0.1 * jax.random.uniform(key_rho, (leading, 1, cells), jnp.float32, -1.0, 1.0)
    velocity = 0.04 * jnp.clip(jax.random.normal(key_vel, (leading, 3, cells), jnp.float32), -2.5, 2.5)
    noise = 0.3 * jax.random.uniform(key_noise, (leading, 19, cells), jnp.float32, -1.0, 1.0)
    vel_table = jnp.asarray(velocity_draw)
    project = vel_table[None, :, 0:1] * velocity[:, 0:1, :] + vel_table[None, :, 1:2] * velocity[:, 1:2, :] + vel_table[None, :, 2:3] * velocity[:, 2:3, :]
    square = jnp.sum(velocity * velocity, axis=1, keepdims=True)
    balance = jnp.asarray(weight_draw)[None, :, None] * density * (1.0 + 3.0 * project + 4.5 * project * project - 1.5 * square)
    return balance * (1.0 + noise)


def draw_populations(key, part):
    return near_state(jax.random.fold_in(key, 21), BLOCKS, CELLS)


def draw_coarse_faces(key, part):
    start_state = near_state(jax.random.fold_in(key, 22), CBLOCKS, FACE)
    end_state = near_state(jax.random.fold_in(key, 23), CBLOCKS, FACE)
    return jnp.stack([start_state, end_state], axis=1)


def behind(keep, step):
    return jnp.concatenate([jnp.zeros((step,), dtype=bool), keep[:-step]])


def geometry(key):
    owners = BLOCKS // BLK_DEV
    positions = jnp.arange(BLOCKS, dtype=jnp.int32)
    device_of = positions // BLK_DEV
    local_pos = positions % BLK_DEV
    slice_of = local_pos // CROSS
    cross_y = local_pos % CROSS // SIDE
    cross_z = local_pos % SIDE
    shuffles = jax.vmap(lambda sub_key: jax.random.permutation(sub_key, BLK_DEV))(jax.random.split(jax.random.fold_in(key, 11), owners))
    block_id = device_of * BLK_DEV + shuffles.reshape(-1).astype(jnp.int32)
    keep_x = jax.random.randint(jax.random.fold_in(key, 12), (BLOCKS,), 0, 8) != 0
    forced_owner = jax.random.randint(jax.random.fold_in(key, 13), (), 0, owners - 1)
    keep_x = (keep_x | (device_of == forced_owner) & (slice_of == SLICES_DEV - 1)) & (positions + CROSS < BLOCKS)
    keep_y = (jax.random.randint(jax.random.fold_in(key, 14), (BLOCKS,), 0, 8) != 0) & (cross_y < SIDE - 1)
    keep_z = (jax.random.randint(jax.random.fold_in(key, 15), (BLOCKS,), 0, 8) != 0) & (cross_z < SIDE - 1)
    plus_x = jnp.where(keep_x, positions + CROSS, -1)
    minus_x = jnp.where(behind(keep_x, CROSS), positions - CROSS, -1)
    plus_y = jnp.where(keep_y, positions + SIDE, -1)
    minus_y = jnp.where(behind(keep_y, SIDE), positions - SIDE, -1)
    plus_z = jnp.where(keep_z, positions + 1, -1)
    minus_z = jnp.where(behind(keep_z, 1), positions - 1, -1)
    by_pos = jnp.stack([plus_x, minus_x, plus_y, minus_y, plus_z, minus_z], axis=1)
    as_ids = jnp.where(by_pos >= 0, block_id[jnp.clip(by_pos, 0, BLOCKS - 1)], -1)
    neighbor_table = jnp.zeros((BLOCKS, 6), jnp.int32).at[block_id].set(as_ids.astype(jnp.int32))
    coarse_shuffle = jax.vmap(lambda sub_key: jax.random.permutation(sub_key, CB_DEV))(jax.random.split(jax.random.fold_in(key, 16), owners))
    coarse_local = slice_of // 2 * (SIDE // 2) + cross_z // 2
    upper_owner = jnp.minimum(device_of + 1, owners - 1)
    coarse_id = upper_owner * CB_DEV + coarse_shuffle[upper_owner, coarse_local].astype(jnp.int32)
    quadrant = 2 * (slice_of % 2) + cross_z % 2
    linked = (jax.random.randint(jax.random.fold_in(key, 17), (BLOCKS,), 0, 4) != 0) | (quadrant == 0)
    has_link = (cross_y == SIDE - 1) & linked & (device_of < owners - 1)
    link_pos = jnp.stack([jnp.where(has_link, coarse_id, -1), quadrant], axis=1).astype(jnp.int32)
    interface_table = jnp.zeros((BLOCKS, 2), jnp.int32).at[block_id].set(link_pos)
    return (neighbor_table, interface_table)


def draw_neighbors(key, part):
    return geometry(key)[0]


def draw_interface(key, part):
    return geometry(key)[1]


def draw_solid(key, part):
    cells = jnp.arange(CELLS, dtype=jnp.int32)
    coord_i = cells // 64
    coord_j = cells // 8 % 8
    coord_k = cells % 8
    inner = (coord_i >= 1) & (coord_i <= 6) & (coord_j >= 1) & (coord_j <= 6) & (coord_k >= 1) & (coord_k <= 6)
    marks = jax.random.randint(jax.random.fold_in(key, 31), (BLOCKS, CELLS), 0, 16) == 0
    return (marks & inner[None, :]).astype(jnp.int32)


def setup_inputs(seed: int = 0) -> dict:
    keys = jax.random.split(jax.random.key(seed), 6)
    return {
        "populations": draw_populations(jax.random.fold_in(keys[5], 71), 0),
        "coarse_faces": draw_coarse_faces(jax.random.fold_in(keys[5], 71), 0),
        "neighbors": draw_neighbors(jax.random.fold_in(keys[5], 71), 0),
        "interface": draw_interface(jax.random.fold_in(keys[5], 71), 0),
        "solid": draw_solid(jax.random.fold_in(keys[5], 71), 0),
    }


def velocity_list():
    return [[0, 0, 0], [1, 0, 0], [-1, 0, 0], [0, 1, 0], [0, -1, 0], [0, 0, 1], [0, 0, -1],
            [1, 1, 0], [-1, -1, 0], [1, -1, 0], [-1, 1, 0], [1, 0, 1], [-1, 0, -1], [1, 0, -1],
            [-1, 0, 1], [0, 1, 1], [0, -1, -1], [0, 1, -1], [0, -1, 1]]


def opposite_list():
    return [0, 2, 1, 4, 3, 6, 5, 8, 7, 10, 9, 12, 11, 14, 13, 16, 15, 18, 17]


def build_relax():
    velocity_set = np.array(velocity_list())
    shear_rate = 1.0 / 0.6
    vel_x = velocity_set[:, 0] * 1.0
    vel_y = velocity_set[:, 1] * 1.0
    vel_z = velocity_set[:, 2] * 1.0
    speed_sq = vel_x * vel_x + vel_y * vel_y + vel_z * vel_z
    moment_rows = [np.ones(19), 19.0 * speed_sq - 30.0, (21.0 * speed_sq * speed_sq - 53.0 * speed_sq + 24.0) / 2.0,
                   vel_x, (5.0 * speed_sq - 9.0) * vel_x, vel_y, (5.0 * speed_sq - 9.0) * vel_y,
                   vel_z, (5.0 * speed_sq - 9.0) * vel_z, 3.0 * vel_x * vel_x - speed_sq,
                   (3.0 * speed_sq - 5.0) * (3.0 * vel_x * vel_x - speed_sq), vel_y * vel_y - vel_z * vel_z,
                   (3.0 * speed_sq - 5.0) * (vel_y * vel_y - vel_z * vel_z), vel_x * vel_y, vel_y * vel_z,
                   vel_x * vel_z, (vel_y * vel_y - vel_z * vel_z) * vel_x, (vel_z * vel_z - vel_x * vel_x) * vel_y,
                   (vel_x * vel_x - vel_y * vel_y) * vel_z]
    moments = np.stack(moment_rows)
    relax_rates = np.array([0.0, 1.19, 1.4, 0.0, 1.2, 0.0, 1.2, 0.0, 1.2, shear_rate, 1.4, shear_rate, 1.4,
                            shear_rate, shear_rate, shear_rate, 1.98, 1.98, 1.98])
    row_norms = np.sum(moments * moments, axis=1)
    return moments.T @ ((relax_rates / row_norms)[:, None] * moments)


def build_crossing():
    velocity_set = velocity_list()
    crossing_list = []
    for face_dir in range(6):
        axis_pos = face_dir // 2
        sign_val = 1 if face_dir % 2 == 0 else -1
        members = [lattice_dir for lattice_dir in range(19) if velocity_set[lattice_dir][axis_pos] == -sign_val]
        crossing_list.append(members)
    return crossing_list


def build_layers():
    layer_list = []
    for face_dir in range(6):
        axis_pos = face_dir // 2
        level = 7 if face_dir % 2 == 0 else 0
        others = [other_axis for other_axis in range(3) if other_axis != axis_pos]
        cell_list = []
        for first_coord in range(8):
            for second_coord in range(8):
                coords = [0, 0, 0]
                coords[axis_pos] = level
                coords[others[0]] = first_coord
                coords[others[1]] = second_coord
                cell_list.append(64 * coords[0] + 8 * coords[1] + coords[2])
        layer_list.append(np.array(cell_list, dtype=np.int32))
    return layer_list


def build_sources():
    velocity_set = velocity_list()
    side_table = np.full((19, 512), -1, dtype=np.int32)
    ghost_table = np.zeros((19, 512), dtype=np.int32)
    for lattice_dir in range(19):
        for cell in range(512):
            coords = [cell // 64, (cell // 8) % 8, cell % 8]
            source = [coords[axis_pos] - velocity_set[lattice_dir][axis_pos] for axis_pos in range(3)]
            outside = [axis_pos for axis_pos in range(3) if source[axis_pos] < 0 or source[axis_pos] > 7]
            if len(outside) == 1:
                axis_pos = outside[0]
                side_table[lattice_dir, cell] = 2 * axis_pos + (0 if source[axis_pos] > 7 else 1)
                others = [other_axis for other_axis in range(3) if other_axis != axis_pos]
                ghost_table[lattice_dir, cell] = 8 * source[others[0]] + source[others[1]]
            elif len(outside) > 1:
                side_table[lattice_dir, cell] = 6
    return side_table, ghost_table


def build_quadrants():
    quad_cells = np.zeros((4, 64), dtype=np.int32)
    for quad in range(4):
        for fine_i in range(8):
            for fine_k in range(8):
                quad_cells[quad, 8 * fine_i + fine_k] = 8 * (4 * (quad // 2) + fine_i // 2) + 4 * (quad % 2) + fine_k // 2
    return quad_cells


def build_offsets():
    velocity_set = velocity_list()
    return [int(64 * velocity_set[lattice_dir][0] + 8 * velocity_set[lattice_dir][1] + velocity_set[lattice_dir][2]) for lattice_dir in range(19)]


def equilibrium(states):
    velocity_f32 = jnp.asarray(np.array(velocity_list()), dtype=jnp.float32)
    weight_f32 = jnp.asarray(np.array([1.0 / 3.0] + [1.0 / 18.0] * 6 + [1.0 / 36.0] * 12), dtype=jnp.float32)
    density = jnp.sum(states, axis=1)
    momentum = jnp.einsum("qa,mqn->man", velocity_f32, states, precision=lax.Precision.HIGHEST)
    velocity = momentum / density[:, None, :]
    project = jnp.einsum("qa,man->mqn", velocity_f32, velocity, precision=lax.Precision.HIGHEST)
    square = jnp.sum(velocity * velocity, axis=1)
    return weight_f32[None, :, None] * density[:, None, :] * (1.0 + 3.0 * project + 4.5 * project * project - 1.5 * square[:, None, :])


def collide(states):
    relax_matrix = jnp.asarray(build_relax(), dtype=jnp.float32)
    balance = equilibrium(states)
    return states - jnp.einsum("pq,mqn->mpn", relax_matrix, states - balance, precision=lax.Precision.HIGHEST)


def layer_of(relaxed, face_dir):
    crossing_sets = build_crossing()
    layer_cells = build_layers()
    picked = jnp.take(relaxed, jnp.asarray(crossing_sets[face_dir], dtype=jnp.int32), axis=1)
    picked = jnp.take(picked, jnp.asarray(layer_cells[face_dir ^ 1], dtype=jnp.int32), axis=2)
    return picked.reshape(relaxed.shape[0], 320)


def interface_values(coarse_tiles):
    crossing_sets = build_crossing()
    coarse_ratio = 0.6 / 1.1
    total = coarse_tiles.shape[0]
    outputs = []
    for time_frac in (0.0, 0.5):
        blended = (1.0 - time_frac) * coarse_tiles[:, 0] + time_frac * coarse_tiles[:, 1]
        balance = equilibrium(blended)
        ghost_vals = balance + coarse_ratio * (blended - balance)
        chosen = jnp.take(ghost_vals, jnp.asarray(crossing_sets[2], dtype=jnp.int32), axis=1)
        outputs.append(chosen.reshape(total, 320))
    return jnp.stack(outputs, axis=1)


def spread_quadrant(picked, quadrant):
    quad_table = jnp.asarray(build_quadrants(), dtype=jnp.int32)
    total = picked.shape[0]
    ghost_view = picked.reshape(total, 2, 5, 64)
    cell_index = jnp.take(quad_table, quadrant, axis=0)
    cell_index = jnp.broadcast_to(cell_index[:, None, None, :], (total, 2, 5, 64))
    return jnp.take_along_axis(ghost_view, cell_index, axis=3).reshape(total, 2, 320)


def stream(relaxed, initial, ghosts, present, solid):
    crossing_sets = build_crossing()
    source_side, ghost_cell = build_sources()
    shift_offsets = build_offsets()
    opposite_dir = opposite_list()
    total = relaxed.shape[0]
    fluid = solid == 0
    ghost_view = ghosts.reshape(total, 6, 5, 64)
    pulled = []
    for lattice_dir in range(19):
        moved = jnp.roll(relaxed[:, lattice_dir], shift_offsets[lattice_dir], axis=1)
        usable = jnp.roll(fluid, shift_offsets[lattice_dir], axis=1)
        for face_dir in range(6):
            if lattice_dir in crossing_sets[face_dir]:
                slot_pos = crossing_sets[face_dir].index(lattice_dir)
                through = jnp.asarray(source_side[lattice_dir] == face_dir)[None, :]
                fetched = jnp.take(ghost_view[:, face_dir, slot_pos], jnp.asarray(ghost_cell[lattice_dir]), axis=1)
                moved = jnp.where(through, fetched, moved)
                usable = jnp.where(through, present[:, face_dir:face_dir + 1], usable)
        edge_mask = jnp.asarray(source_side[lattice_dir] == 6)[None, :]
        usable = jnp.where(edge_mask, False, usable)
        pulled.append(jnp.where(usable, moved, relaxed[:, opposite_dir[lattice_dir]]))
    read = jnp.stack(pulled, axis=1)
    return jnp.where(fluid[:, None, :], read, initial)


def reference(populations, coarse_faces, neighbors, interface, solid):
    face_ids = jnp.arange(6, dtype=jnp.int32)
    has_coarse = interface[:, 0] >= 0
    present = (neighbors >= 0) | ((face_ids[None, :] == 2) & has_coarse[:, None])
    coarse_vals = interface_values(coarse_faces)
    picked = jnp.take(coarse_vals, jnp.clip(interface[:, 0], 0, CBLOCKS - 1), axis=0)
    fine_ghost = spread_quadrant(picked, interface[:, 1])
    current = populations
    for substep in range(2):
        grouped = current.reshape(N_BLK, BLK_DEV, Q, CELLS)
        relaxed = lax.map(collide, grouped).reshape(BLOCKS, Q, CELLS)
        ghosts = []
        for face_dir in range(6):
            layer = layer_of(relaxed, face_dir)
            fetched = jnp.take(layer, jnp.clip(neighbors[:, face_dir], 0, BLOCKS - 1), axis=0)
            if face_dir == 2:
                fetched = jnp.where(has_coarse[:, None], fine_ghost[:, substep], fetched)
            ghosts.append(fetched)
        current = stream(relaxed, populations, jnp.stack(ghosts, axis=1), present, solid)
    return current
```

```python
import jax
import jax.numpy as jnp
import numpy as np
from jax import lax
from jax.experimental import pallas as pl
from jax.experimental.pallas import tpu as pltpu
from jax.sharding import PartitionSpec as P

F32, BF16, I32 = jnp.float32, jnp.bfloat16, jnp.int32
LANES = 128
VEL = [
    (0, 0, 0),
    (1, 0, 0), (-1, 0, 0), (0, 1, 0), (0, -1, 0), (0, 0, 1), (0, 0, -1),
    (1, 1, 0), (-1, -1, 0), (1, -1, 0), (-1, 1, 0),
    (1, 0, 1), (-1, 0, -1), (1, 0, -1), (-1, 0, 1),
    (0, 1, 1), (0, -1, -1), (0, 1, -1), (0, -1, 1),
]
Q = len(VEL)
OPP = [VEL.index((-x, -y, -z)) for x, y, z in VEL]
CROSSING = [
    [q for q in range(Q) if VEL[q][d // 2] == (-1 if d % 2 == 0 else 1)] for d in range(6)
]


def rates():
    v = np.array(VEL) * 1.0
    x, y, z = v[:, 0], v[:, 1], v[:, 2]
    s = x * x + y * y + z * z
    rows = [
        np.ones(19), 19 * s - 30, (21 * s * s - 53 * s + 24) / 2,
        x, (5 * s - 9) * x, y, (5 * s - 9) * y, z, (5 * s - 9) * z,
        3 * x * x - s, (3 * s - 5) * (3 * x * x - s),
        y * y - z * z, (3 * s - 5) * (y * y - z * z),
        x * y, y * z, x * z,
        (y * y - z * z) * x, (z * z - x * x) * y, (x * x - y * y) * z,
    ]
    norms = (np.stack(rows) ** 2).sum(1)
    w = 1.0 / 0.6
    relax = np.array([0, 1.19, 1.4, 0, 1.2, 0, 1.2, 0, 1.2, w, 1.4, w, 1.4, w, w, w, 1.98, 1.98, 1.98])
    return [float(c) for c in relax / norms]


def collide(f):
    c = rates()
    s = {q: f[q] + f[q + 1] for q in range(1, 19, 2)}
    d = {q: f[q] - f[q + 1] for q in range(1, 19, 2)}
    a, b, g = s[7] + s[9], s[11] + s[13], s[15] + s[17]
    s1, s2 = s[1] + (s[3] + s[5]), a + b + g
    rho = f[0] + s1 + s2
    ax1, ax2 = d[7] + d[9], d[11] + d[13]
    ay1, ay2 = d[7] - d[9], d[15] + d[17]
    az1, az2 = d[11] - d[13], d[15] - d[17]
    ax, ay, az = ax1 + ax2, ay1 + ay2, az1 + az2
    jx, jy, jz = d[1] + ax, d[3] + ay, d[5] + az
    inv = 1.0 / rho
    ux, uy, uz = jx * inv, jy * inv, jz * inv
    xx, yy, zz = jx * ux, jy * uy, jz * uz
    jj = xx + yy + zz
    r1 = (19 * c[1]) * (s2 - f[0] - jj)
    r2 = c[2] * (9 * f[0] - 7 * s1 - 2 * s2 + 5.5 * jj)
    t1, t2, pe = 2 * s[1] - (s[3] + s[5]), a + b - 2 * g, 3 * xx - jj
    v1, v2, we = s[3] - s[5], a - b, yy - zz
    r9, r10 = c[9] * (t1 + t2 - pe), c[10] * (t2 - 2 * t1 + 0.5 * pe)
    r11, r12 = c[11] * (v1 + v2 - we), c[12] * (v2 - 2 * v1 + 0.5 * we)
    r13 = c[13] * (s[7] - s[9] - jx * uy)
    r14 = c[14] * (s[15] - s[17] - jy * uz)
    r15 = c[15] * (s[11] - s[13] - jx * uz)
    r4 = (c[4] * 5 / 3) * (ax - 2 * d[1])
    r6 = (c[6] * 5 / 3) * (ay - 2 * d[3])
    r8 = (c[8] * 5 / 3) * (az - 2 * d[5])
    r16, r17, r18 = c[16] * (ax1 - ax2), c[17] * (ay2 - ay1), c[18] * (az1 - az2)
    ea, eb = -11 * r1 - 4 * r2, 8 * r1 + r2
    a9, a11 = r9 - 2 * r10, r11 - 2 * r12
    b9, b11 = r9 + r10, r11 + r12
    exy, exz, eyz = eb + b9 + b11, eb + b9 - b11, eb - 2 * b9
    even = {
        1: ea + 2 * a9, 3: ea - a9 + a11, 5: ea - a9 - a11,
        7: exy + r13, 9: exy - r13, 11: exz + r15, 13: exz - r15, 15: eyz + r14, 17: eyz - r14,
    }
    odd = {
        1: -4 * r4, 3: -4 * r6, 5: -4 * r8,
        7: (r4 + r6) + (r16 - r17), 9: (r4 - r6) + (r16 + r17),
        11: (r4 + r8) - (r16 - r18), 13: (r4 - r8) - (r16 + r18),
        15: (r6 + r8) + (r17 - r18), 17: (r6 - r8) + (r17 + r18),
    }
    out = [f[0] + 30 * r1 - 12 * r2]
    for q in range(1, 19, 2):
        out += [f[q] - even[q] - odd[q], f[q + 1] - even[q] + odd[q]]
    return out


def feq(h):
    rho = h[0]
    for q in range(1, Q):
        rho = rho + h[q]
    safe = jnp.where(rho > 0, rho, 1.0)
    u = []
    for axis in range(3):
        m = None
        for q in range(Q):
            if VEL[q][axis]:
                t = h[q] if VEL[q][axis] > 0 else -h[q]
                m = t if m is None else m + t
        u.append(m / safe)
    sq = u[0] * u[0] + u[1] * u[1] + u[2] * u[2]
    out = {}
    for q in CROSSING[2]:
        p = None
        for axis in range(3):
            if VEL[q][axis]:
                t = u[axis] if VEL[q][axis] > 0 else -u[axis]
                p = t if p is None else p + t
        n = sum(abs(e) for e in VEL[q])
        w = 1.0 / 18.0 if n == 1 else 1.0 / 36.0
        out[q] = w * rho * (1.0 + 3.0 * p + 4.5 * p * p - 1.5 * sq)
    return out


def lanes(rows):
    l = lax.broadcasted_iota(I32, (rows, LANES), 1)
    return l >= 64, (l >> 3) & 7, l & 7


def split(x):
    hi = x.astype(BF16)
    lo = (x - hi.astype(F32)).astype(BF16)
    return jnp.concatenate([hi, lo], axis=0)


def dot(a, b):
    return jnp.dot(a, b, preferred_element_type=F32)


def select_rows(row, offset, count):
    r = lax.broadcasted_iota(I32, (count, row.shape[1]), 0)
    hot = jnp.where(r == row - offset, 1.0, 0.0).astype(BF16)
    return jnp.concatenate([hot, hot], axis=1)


def spread_rows(flags):
    n = flags.shape[1]
    eye = lax.broadcasted_iota(I32, (n, n), 0) == lax.broadcasted_iota(I32, (n, n), 1)
    diag = jnp.where(eye, flags.astype(F32), 0.0).astype(BF16)
    return dot(diag, jnp.ones((n, LANES), BF16))


def sources(q, t, tiles, outer, half):
    ex = VEL[q][0]
    if ex == 0:
        return tiles[t]
    n = t - ex
    other = tiles[n] if 0 <= n < len(tiles) else outer
    return jnp.where(half, other, tiles[t]) if ex > 0 else jnp.where(half, tiles[t], other)


def roll(x, by):
    by %= LANES
    return pltpu.roll(x, by, 1) if by else x


def edges(q, t, count, half, j, k):
    ex, ey, ez = VEL[q]
    cx = None
    if ex > 0 and t == 0:
        cx = jnp.logical_not(half)
    if ex < 0 and t == count - 1:
        cx = half
    cy = None if ey == 0 else (j == (0 if ey > 0 else 7))
    cz = None if ez == 0 else (k == (0 if ez > 0 else 7))
    return cx, cy, cz


def face_of(axis, e):
    return 2 * axis + (1 if e > 0 else 0)


def write_bits(bits_ref, solid_ref, absent, tiles):
    rows = solid_ref.shape[0]
    half, j, k = lanes(rows)
    solid = [solid_ref[:, LANES * t : LANES * (t + 1)] for t in range(tiles)]
    for t in range(tiles):
        acc = jnp.where(solid[t] != 0, 1, 0)
        for q in range(1, Q):
            ex, ey, ez = VEL[q]
            v = roll(sources(q, t, solid, solid[t], half), 64 * abs(ex) + 8 * ey + ez)
            crossed = [c for c in zip(edges(q, t, tiles, half, j, k), (ex, ey, ez), range(3)) if c[0] is not None]
            for c, e, axis in crossed:
                v = jnp.where(c, absent[face_of(axis, e)], v)
            for i in range(len(crossed)):
                for m in range(i):
                    v = jnp.where(crossed[i][0] & crossed[m][0], 1, v)
            acc = acc | (jnp.where(v != 0, 1, 0) << q)
        bits_ref[:, LANES * t : LANES * (t + 1)] = acc


def collide_all(src_ref, dst_ref):
    rows, cells = src_ref.shape[1], src_ref.shape[2]
    tiles = cells // LANES

    def step(i, carry):
        r = pl.ds(pl.multiple_of(8 * (i // tiles), 8), 8)
        l = pl.ds(pl.multiple_of(LANES * (i % tiles), LANES), LANES)
        out = collide([src_ref[q, r, l] for q in range(Q)])
        for q in range(Q):
            dst_ref[q, r, l] = out[q]
        return carry

    lax.fori_loop(0, rows // 8 * tiles, step, 0)


def absences(nbr_ref, ifc_ref):
    out = []
    for d in range(6):
        there = nbr_ref[d : d + 1, :] >= 0
        if d == 2:
            there = there | (ifc_ref[0:1, :] >= 0)
        out.append((1.0 - spread_rows(jnp.where(there, 1.0, 0.0))).astype(I32))
    return out


def fine_ghost(out_ref, co_ref, ifc_ref, theta, position):
    count = co_ref.shape[0]
    blocks = ifc_ref.shape[1]
    tiles = out_ref.shape[2] // LANES
    half = lanes(blocks)[0]
    owner = ifc_ref[0:1, :] - (position + 1) * count
    quad = ifc_ref[1:2, :]
    masks = [
        [spread_rows(jnp.where((owner == c) & (quad == w), 1.0, 0.0)) for w in range(4)]
        for c in range(count)
    ]
    vals = []
    for c in range(count):
        h = []
        for q in range(Q):
            h0 = co_ref[c, q, 0:1, :]
            h.append(h0 if theta == 0 else (1.0 - theta) * h0 + theta * co_ref[c, q, 1:2, :])
        e = feq(h)
        row = {q: e[q] + (0.6 / 1.1) * (h[q] - e[q]) for q in CROSSING[2]}
        vals.append({q: jnp.concatenate([row[q], row[q]], axis=1) for q in CROSSING[2]})
    hi, lo = [], []
    for q in CROSSING[2]:
        parts = []
        for pair in (0, 2):
            acc = None
            for c in range(count):
                m = jnp.where(half, masks[c][pair + 1], masks[c][pair])
                v = m * vals[c][q]
                acc = v if acc is None else acc + v
            parts.append(acc)
        x = jnp.concatenate(parts, axis=1)
        h = x.astype(BF16)
        hi.append(h)
        lo.append((x - h.astype(F32)).astype(BF16))
    left = jnp.concatenate(hi + lo, axis=0)
    rows_k = 256
    kk = lax.broadcasted_iota(I32, (rows_k, LANES), 0)
    ll = lax.broadcasted_iota(I32, (rows_k, LANES), 1)
    w, m = kk >> 6, kk & 63
    n = 5 * blocks
    for t in range(tiles):
        i, k = 2 * t + (ll >> 6), ll & 7
        want = 8 * (4 * (w >> 1) + (i >> 1)) + 4 * (w & 1) + (k >> 1)
        e = jnp.where(m == want, 1.0, 0.0).astype(BF16)
        g = dot(left, e)
        g = g[:n] + g[n:]
        for s in range(5):
            out_ref[s, :, LANES * t : LANES * (t + 1)] = g[blocks * s : blocks * (s + 1)]


def send_faces(post_ref, nbr_ref, first, position, sa_ref, sb_ref):
    blocks = post_ref.shape[1]
    last = post_ref.shape[2] - LANES
    half = lanes(blocks)[0]
    even = position % 2 == 0
    packs = []
    for d, lane, by, native in ((0, last, first + blocks, 1), (1, 0, first - blocks, 0)):
        hot = select_rows(nbr_ref[d : d + 1, :], by, blocks)
        got = [dot(hot, split(post_ref[q, :, lane : lane + LANES])) for q in CROSSING[d ^ 1]]
        pack = []
        for s in range(0, 5, 2):
            a = got[s] if native == 0 else roll(got[s], 64)
            if s + 1 < 5:
                b = got[s + 1] if native == 1 else roll(got[s + 1], 64)
                a = jnp.where(half, b, a)
            pack.append(a)
        packs.append(pack)
    for s in range(3):
        sa_ref[s] = jnp.where(even, packs[0][s], packs[1][s])
        sb_ref[s] = jnp.where(even, packs[1][s], packs[0][s])


def received(ra_ref, rb_ref, position):
    even = position % 2 == 0
    half = lanes(ra_ref.shape[1])[0]
    out = {}
    for s in range(3):
        a, b = ra_ref[s], rb_ref[s]
        up, low = jnp.where(even, a, b), jnp.where(even, b, a)
        for i in (2 * s, 2 * s + 1):
            if i < 5:
                out[CROSSING[0][i]] = up if i % 2 == 0 else roll(up, 64)
                out[CROSSING[1][i]] = low if i % 2 == 1 else roll(low, 64)
    return out


def stream(post_ref, dst_ref, init_ref, bits_ref, nbr_ref, fine_ref, remote, first):
    blocks, cells = post_ref.shape[1], post_ref.shape[2]
    tiles = cells // LANES
    half, j, k = lanes(blocks)
    hot = [select_rows(nbr_ref[(d ^ 1) : (d ^ 1) + 1, :], first, blocks) for d in range(6)]
    span = [slice(LANES * t, LANES * (t + 1)) for t in range(tiles)]
    for q in range(Q):
        ex, ey, ez = VEL[q]
        x = [post_ref[q, :, span[t]] for t in range(tiles)]
        if q:
            parts = [split(v) for v in x]
        gx, gy, gz = None, None, None
        if ex:
            t = 0 if ex < 0 else tiles - 1
            gx = dot(hot[face_of(0, ex)], parts[t]) + remote[q]
        if ey:
            gy = [dot(hot[face_of(1, ey)], p) for p in parts]
            if ey < 0:
                s = CROSSING[2].index(q)
                gy = [g + fine_ref[s, :, span[t]] for t, g in enumerate(gy)]
        if ez:
            gz = [dot(hot[face_of(2, ez)], p) for p in parts]
        for t in range(tiles):
            bits = bits_ref[:, span[t]]
            if q == 0:
                out = x[t]
            else:
                out = roll(sources(q, t, x, gx, half), 64 * abs(ex) + 8 * ey + ez)
                _, cy, cz = edges(q, t, tiles, half, j, k)
                if ey:
                    g = roll(sources(q, t, gy, gy[t], half), 64 * abs(ex) - 56 * ey + ez)
                    out = jnp.where(cy, g, out)
                if ez:
                    g = roll(sources(q, t, gz, gz[t], half), 64 * abs(ex) + 8 * ey - 7 * ez)
                    out = jnp.where(cz, g, out)
                out = jnp.where((bits & (1 << q)) != 0, post_ref[OPP[q], :, span[t]], out)
            out = jnp.where((bits & 1) != 0, init_ref[q, :, span[t]], out)
            dst_ref[q, :, span[t]] = out


def first_kernel(pop_ref, nbr_ref, ifc_ref, solid_ref, post_ref, bits_ref, sa_ref, sb_ref):
    position = lax.axis_index("blk")
    first = position * pop_ref.shape[1]
    collide_all(pop_ref, post_ref)
    send_faces(post_ref, nbr_ref, first, position, sa_ref, sb_ref)
    write_bits(bits_ref, solid_ref, absences(nbr_ref, ifc_ref), pop_ref.shape[2] // LANES)


def middle_kernel(post_ref, pop_ref, bits_ref, ra_ref, rb_ref, co_ref, nbr_ref, ifc_ref, out_ref, sa_ref, sb_ref, fine_ref):
    position = lax.axis_index("blk")
    first = position * pop_ref.shape[1]
    fine_ghost(fine_ref, co_ref, ifc_ref, 0.0, position)
    stream(post_ref, out_ref, pop_ref, bits_ref, nbr_ref, fine_ref, received(ra_ref, rb_ref, position), first)
    collide_all(out_ref, out_ref)
    send_faces(out_ref, nbr_ref, first, position, sa_ref, sb_ref)


def last_kernel(post_ref, pop_ref, bits_ref, ra_ref, rb_ref, co_ref, nbr_ref, ifc_ref, out_ref, fine_ref):
    position = lax.axis_index("blk")
    first = position * pop_ref.shape[1]
    fine_ghost(fine_ref, co_ref, ifc_ref, 0.5, position)
    stream(post_ref, out_ref, pop_ref, bits_ref, nbr_ref, fine_ref, received(ra_ref, rb_ref, position), first)


def shifted(x, by):
    n = lax.axis_size("blk")
    return lax.ppermute(x, "blk", [(i, i + by) for i in range(n) if 0 <= i + by < n])


def swapped(x, off):
    n = lax.axis_size("blk")
    low = [(i, i + 1) for i in range(off, n - 1, 2)]
    return lax.ppermute(x, "blk", low + [(b, a) for a, b in low])


def body(populations, coarse_faces, neighbors, interface, solid):
    pop = populations.transpose(1, 0, 2)
    co = coarse_faces.transpose(0, 2, 1, 3)
    nbr, ifc = neighbors.T, interface.T
    blocks = pop.shape[1]
    state = jax.ShapeDtypeStruct(pop.shape, F32)
    faces = jax.ShapeDtypeStruct((3, blocks, LANES), F32)
    fine = pltpu.VMEM((5,) + pop.shape[1:], F32)
    co = shifted(co, -1)
    post, bits, sa, sb = pl.pallas_call(
        first_kernel, out_shape=(state, jax.ShapeDtypeStruct(solid.shape, I32), faces, faces), name="first"
    )(pop, nbr, ifc, solid)
    ra, rb = swapped(sa, 0), swapped(sb, 1)
    post, sa, sb = pl.pallas_call(
        middle_kernel, out_shape=(state, faces, faces), scratch_shapes=[fine], name="middle"
    )(post, pop, bits, ra, rb, co, nbr, ifc)
    ra, rb = swapped(sa, 0), swapped(sb, 1)
    out = pl.pallas_call(last_kernel, out_shape=state, scratch_shapes=[fine], name="last")(
        post, pop, bits, ra, rb, co, nbr, ifc
    )
    return out.transpose(1, 0, 2)


def solution(mesh):
    placed = (P("blk", None, None), P("blk", None, None, None), P("blk", None), P("blk", None), P("blk", None))
    return jax.shard_map(body, mesh=mesh, in_specs=placed, out_specs=P("blk", None, None), check_vma=False)
```

```python
import functools

import jax
import jax.numpy as jnp
import numpy as np
from jax import lax
from jax.experimental import pallas as pl
from jax.experimental.pallas import tpu as pltpu
from jax.sharding import PartitionSpec as P

F32, BF16, I32 = jnp.float32, jnp.bfloat16, jnp.int32
LANES = 128
VEL = [
    (0, 0, 0),
    (1, 0, 0), (-1, 0, 0), (0, 1, 0), (0, -1, 0), (0, 0, 1), (0, 0, -1),
    (1, 1, 0), (-1, -1, 0), (1, -1, 0), (-1, 1, 0),
    (1, 0, 1), (-1, 0, -1), (1, 0, -1), (-1, 0, 1),
    (0, 1, 1), (0, -1, -1), (0, 1, -1), (0, -1, 1),
]
Q = len(VEL)
OPP = [VEL.index((-x, -y, -z)) for x, y, z in VEL]
CROSSING = [
    [q for q in range(Q) if VEL[q][d // 2] == (-1 if d % 2 == 0 else 1)] for d in range(6)
]


def rates():
    v = np.array(VEL) * 1.0
    x, y, z = v[:, 0], v[:, 1], v[:, 2]
    s = x * x + y * y + z * z
    rows = [
        np.ones(19), 19 * s - 30, (21 * s * s - 53 * s + 24) / 2,
        x, (5 * s - 9) * x, y, (5 * s - 9) * y, z, (5 * s - 9) * z,
        3 * x * x - s, (3 * s - 5) * (3 * x * x - s),
        y * y - z * z, (3 * s - 5) * (y * y - z * z),
        x * y, y * z, x * z,
        (y * y - z * z) * x, (z * z - x * x) * y, (x * x - y * y) * z,
    ]
    norms = (np.stack(rows) ** 2).sum(1)
    w = 1.0 / 0.6
    relax = np.array([0, 1.19, 1.4, 0, 1.2, 0, 1.2, 0, 1.2, w, 1.4, w, 1.4, w, w, w, 1.98, 1.98, 1.98])
    return [float(c) for c in relax / norms]


def collide(f):
    c = rates()
    s = {q: f[q] + f[q + 1] for q in range(1, 19, 2)}
    d = {q: f[q] - f[q + 1] for q in range(1, 19, 2)}
    a, b, g = s[7] + s[9], s[11] + s[13], s[15] + s[17]
    s1, s2 = s[1] + (s[3] + s[5]), a + b + g
    rho = f[0] + s1 + s2
    ax1, ax2 = d[7] + d[9], d[11] + d[13]
    ay1, ay2 = d[7] - d[9], d[15] + d[17]
    az1, az2 = d[11] - d[13], d[15] - d[17]
    ax, ay, az = ax1 + ax2, ay1 + ay2, az1 + az2
    jx, jy, jz = d[1] + ax, d[3] + ay, d[5] + az
    inv = 1.0 / rho
    ux, uy, uz = jx * inv, jy * inv, jz * inv
    xx, yy, zz = jx * ux, jy * uy, jz * uz
    jj = xx + yy + zz
    r1 = (19 * c[1]) * (s2 - f[0] - jj)
    r2 = c[2] * (9 * f[0] - 7 * s1 - 2 * s2 + 5.5 * jj)
    t1, t2, pe = 2 * s[1] - (s[3] + s[5]), a + b - 2 * g, 3 * xx - jj
    v1, v2, we = s[3] - s[5], a - b, yy - zz
    r9, r10 = c[9] * (t1 + t2 - pe), c[10] * (t2 - 2 * t1 + 0.5 * pe)
    r11, r12 = c[11] * (v1 + v2 - we), c[12] * (v2 - 2 * v1 + 0.5 * we)
    r13 = c[13] * (s[7] - s[9] - jx * uy)
    r14 = c[14] * (s[15] - s[17] - jy * uz)
    r15 = c[15] * (s[11] - s[13] - jx * uz)
    r4 = (c[4] * 5 / 3) * (ax - 2 * d[1])
    r6 = (c[6] * 5 / 3) * (ay - 2 * d[3])
    r8 = (c[8] * 5 / 3) * (az - 2 * d[5])
    r16, r17, r18 = c[16] * (ax1 - ax2), c[17] * (ay2 - ay1), c[18] * (az1 - az2)
    ea, eb = -11 * r1 - 4 * r2, 8 * r1 + r2
    a9, a11 = r9 - 2 * r10, r11 - 2 * r12
    b9, b11 = r9 + r10, r11 + r12
    exy, exz, eyz = eb + b9 + b11, eb + b9 - b11, eb - 2 * b9
    even = {
        1: ea + 2 * a9, 3: ea - a9 + a11, 5: ea - a9 - a11,
        7: exy + r13, 9: exy - r13, 11: exz + r15, 13: exz - r15, 15: eyz + r14, 17: eyz - r14,
    }
    odd = {
        1: -4 * r4, 3: -4 * r6, 5: -4 * r8,
        7: (r4 + r6) + (r16 - r17), 9: (r4 - r6) + (r16 + r17),
        11: (r4 + r8) - (r16 - r18), 13: (r4 - r8) - (r16 + r18),
        15: (r6 + r8) + (r17 - r18), 17: (r6 - r8) + (r17 + r18),
    }
    out = [f[0] + 30 * r1 - 12 * r2]
    for q in range(1, 19, 2):
        out += [f[q] - even[q] - odd[q], f[q + 1] - even[q] + odd[q]]
    return out


def feq(h):
    rho = h[0]
    for q in range(1, Q):
        rho = rho + h[q]
    safe = jnp.where(rho > 0, rho, 1.0)
    u = []
    for axis in range(3):
        m = None
        for q in range(Q):
            if VEL[q][axis]:
                t = h[q] if VEL[q][axis] > 0 else -h[q]
                m = t if m is None else m + t
        u.append(m / safe)
    sq = u[0] * u[0] + u[1] * u[1] + u[2] * u[2]
    out = {}
    for q in CROSSING[2]:
        p = None
        for axis in range(3):
            if VEL[q][axis]:
                t = u[axis] if VEL[q][axis] > 0 else -u[axis]
                p = t if p is None else p + t
        n = sum(abs(e) for e in VEL[q])
        w = 1.0 / 18.0 if n == 1 else 1.0 / 36.0
        out[q] = w * rho * (1.0 + 3.0 * p + 4.5 * p * p - 1.5 * sq)
    return out


def lanes(rows):
    l = lax.broadcasted_iota(I32, (rows, LANES), 1)
    return l >= 64, (l >> 3) & 7, l & 7


def split(x):
    hi = x.astype(BF16)
    lo = (x - hi.astype(F32)).astype(BF16)
    return jnp.concatenate([hi, lo], axis=0)


def dot(a, b):
    return jnp.dot(a, b, preferred_element_type=F32)


def select_rows(row, offset, count):
    r = lax.broadcasted_iota(I32, (count, row.shape[1]), 0)
    hot = jnp.where(r == row - offset, 1.0, 0.0).astype(BF16)
    return jnp.concatenate([hot, hot], axis=1)


def spread_rows(flags):
    n = flags.shape[1]
    eye = lax.broadcasted_iota(I32, (n, n), 0) == lax.broadcasted_iota(I32, (n, n), 1)
    diag = jnp.where(eye, flags.astype(F32), 0.0).astype(BF16)
    return dot(diag, jnp.ones((n, LANES), BF16))


def sources(q, t, tiles, outer, half):
    ex = VEL[q][0]
    if ex == 0:
        return tiles[t]
    n = t - ex
    other = tiles[n] if 0 <= n < len(tiles) else outer
    return jnp.where(half, other, tiles[t]) if ex > 0 else jnp.where(half, tiles[t], other)


def roll(x, by):
    by %= LANES
    return pltpu.roll(x, by, 1) if by else x


def edges(q, t, count, half, j, k):
    ex, ey, ez = VEL[q]
    cx = None
    if ex > 0 and t == 0:
        cx = jnp.logical_not(half)
    if ex < 0 and t == count - 1:
        cx = half
    cy = None if ey == 0 else (j == (0 if ey > 0 else 7))
    cz = None if ez == 0 else (k == (0 if ez > 0 else 7))
    return cx, cy, cz


def face_of(axis, e):
    return 2 * axis + (1 if e > 0 else 0)


def bounce_bits(t, solid, absent):
    half, j, k = lanes(solid[0].shape[0])
    acc = jnp.where(solid[t] != 0, 1, 0)
    for q in range(1, Q):
        ex, ey, ez = VEL[q]
        v = roll(sources(q, t, solid, solid[t], half), 64 * abs(ex) + 8 * ey + ez)
        sides = zip(edges(q, t, len(solid), half, j, k), (ex, ey, ez), range(3))
        crossed = [c for c in sides if c[0] is not None]
        for c, e, axis in crossed:
            v = jnp.where(c, absent[face_of(axis, e)], v)
        for i in range(len(crossed)):
            for m in range(i):
                v = jnp.where(crossed[i][0] & crossed[m][0], 1, v)
        acc = acc | (jnp.where(v != 0, 1, 0) << q)
    return acc


def absences(nbr_ref, ifc_ref):
    out = []
    for d in range(6):
        there = nbr_ref[d : d + 1, :] >= 0
        if d == 2:
            there = there | (ifc_ref[0:1, :] >= 0)
        out.append((1.0 - spread_rows(jnp.where(there, 1.0, 0.0))).astype(I32))
    return out


def local_hots(nbr_ref, first):
    n = nbr_ref.shape[1]
    return [select_rows(nbr_ref[(d ^ 1) : (d ^ 1) + 1, :], first, n) for d in range(6)]


def send_rows(row, first, count, cap):
    rel = row - first
    gone = (rel >= 0) & (rel < count)
    rel = jnp.where(gone, rel, 255)
    ahead = spread_rows(rel)[:, :count] < rel.astype(F32)
    rank = jnp.sum(jnp.where(ahead, 1.0, 0.0), axis=0, keepdims=True)
    r = lax.broadcasted_iota(I32, (cap, count), 0).astype(F32)
    hot = jnp.where((r == rank) & gone, 1.0, 0.0).astype(BF16)
    return jnp.concatenate([hot, hot], axis=1)


def take_rows(row, first, count, cap):
    rel = row - first
    gone = jnp.where((rel >= 0) & (rel < count), 1.0, 0.0)
    b = lax.broadcasted_iota(I32, (count, count), 0)
    a = lax.broadcasted_iota(I32, (count, count), 1)
    rank = dot(jnp.where(a < b, gone, 0.0).astype(BF16), jnp.ones((count, LANES), BF16))[:, :cap]
    there = spread_rows(gone)[:, :cap] > 0.5
    r = lax.broadcasted_iota(I32, (count, cap), 1).astype(F32)
    hot = jnp.where((r == rank) & there, 1.0, 0.0).astype(BF16)
    return jnp.concatenate([hot, hot], axis=1)


def coarse_code(ifc_ref, position, count):
    c = ifc_ref[0:1, :]
    code = jnp.where(c >= 0, 2 + 4 * (c - (position + 1) * count) + ifc_ref[1:2, :], 1)
    return spread_rows(code)


def coarse_values(co_ref, cg_ref):
    count = co_ref.shape[0]
    h = []
    for q in range(Q):
        h0 = co_ref[:, q, 0, :]
        h1 = (1.0 - 0.5) * h0 + 0.5 * co_ref[:, q, 1, :]
        h.append(jnp.concatenate([h0, h1], axis=1))
    e = feq(h)
    cg_ref[...] = jnp.zeros_like(cg_ref)
    for s, q in enumerate(CROSSING[2]):
        v = e[q] + (0.6 / 1.1) * (h[q] - e[q])
        for c in range(count):
            cg_ref[5 * c + s : 5 * c + s + 1, :] = v[c : c + 1]


def both_halves(x, upper):
    half = lanes(x.shape[0])[0]
    return jnp.where(half, x, roll(x, 64)) if upper else jnp.where(half, roll(x, 64), x)


def spread_matrix(tiles):
    kk = lax.broadcasted_iota(I32, (256, LANES), 0)
    ll = lax.broadcasted_iota(I32, (256, LANES), 1)
    w, m, k = kk >> 6, kk & 63, ll & 7
    out = []
    for t in range(tiles + 1):
        i = (ll >> 6) * 7 if t == tiles else 2 * t + (ll >> 6)
        want = 8 * (4 * (w >> 1) + (i >> 1)) + 4 * (w & 1) + (k >> 1)
        out.append(jnp.where(m == want, 1.0, 0.0).astype(BF16))
    return out


def coarse_rows(code, cg, count):
    half = lanes(code.shape[0])[0]
    hi, lo = [], []
    for s in range(5):
        parts = []
        for pair in (0, 2):
            acc = jnp.zeros_like(code)
            for c in range(count):
                want = jnp.where(half, 3.0 + 4 * c + pair, 2.0 + 4 * c + pair)
                acc = jnp.where(code == want, cg[5 * c + s : 5 * c + s + 1, :], acc)
            parts.append(acc)
        x = jnp.concatenate(parts, axis=1)
        h = x.astype(BF16)
        hi.append(h)
        lo.append((x - h.astype(F32)).astype(BF16))
    return jnp.concatenate(hi + lo, axis=0)


def coarse_tile(rows, matrix):
    g = dot(rows, matrix)
    n = g.shape[0] // 2
    g = g[:n] + g[n:]
    b = n // 5
    return [g[b * s : b * (s + 1)] for s in range(5)]


def pull(q, t, x, parts, gx, hot, fine, bits, bounced, init):
    if q == 0:
        return jnp.where((bits & 1) != 0, init, x[t])
    half, j, k = lanes(bits.shape[0])
    ex, ey, ez = VEL[q]
    turn = 64 * abs(ex)
    out = roll(sources(q, t, x, gx, half), turn + 8 * ey + ez)
    _, cy, cz = edges(q, t, len(x), half, j, k)
    if ey:
        g = parts[1]
        out = jnp.where(cy, roll(sources(q, t, g, g[t], half), turn - 56 * ey + ez), out)
    if ez:
        g = parts[2]
        out = jnp.where(cz, roll(sources(q, t, g, g[t], half), turn + 8 * ey - 7 * ez), out)
    out = jnp.where((bits & (1 << q)) != 0, bounced, out)
    return jnp.where((bits & 1) != 0, init, out)


def gathers(q, x, hot, fine, remote):
    ex, ey, ez = VEL[q]
    gx, gy, gz = None, None, None
    if q:
        parts = [split(v) for v in x]
    if ex:
        gx = dot(hot[face_of(0, ex)], parts[0 if ex < 0 else len(x) - 1])
        if remote is not None:
            gx = gx + remote[q]
    if ey:
        gy = [dot(hot[face_of(1, ey)], p) for p in parts]
        if ey < 0 and fine is not None:
            s = CROSSING[2].index(q)
            gy = [g + fine(s, t) for t, g in enumerate(gy)]
    if ez:
        gz = [dot(hot[face_of(2, ez)], p) for p in parts]
    return gx, gy, gz


def side_slots(d):
    e = 1 if d == 0 else -1
    return [q for q in range(Q) if VEL[q][0] == e], [q for q in range(Q) if VEL[q][0] != -e]


def outer_kernel(pop_ref, nbr_ref, ifc_ref, solid_ref, co_ref, post_ref, bits_ref, cg_ref, sa_ref, sb_ref, buf_ref, pack_ref, sem):
    position = lax.axis_index("blk")
    blocks = solid_ref.shape[0]
    tiles = solid_ref.shape[1] // LANES
    first = position * blocks
    even = position % 2 == 0
    count = co_ref.shape[0]
    copies = []
    for side, t in ((0, tiles - 1), (1, 0)):
        copy = pltpu.make_async_copy(
            pop_ref.at[:, :, pl.ds(LANES * t, LANES)], buf_ref.at[side], sem.at[side]
        )
        copy.start()
        copies.append(copy)
    half, j, k = lanes(blocks)
    coarse_values(co_ref, cg_ref)
    code = coarse_code(ifc_ref, position, count)
    absent = absences(nbr_ref, ifc_ref)
    hot = local_hots(nbr_ref, first)
    solid = [solid_ref[:, LANES * t : LANES * (t + 1)] for t in range(tiles)]
    bits_ref[0] = bounce_bits(tiles - 1, solid, absent)
    bits_ref[1] = bounce_bits(0, solid, absent)
    for side, t in ((0, tiles - 1), (1, 0)):
        copies[side].wait()

        def step(g, carry, side=side):
            r = pl.ds(pl.multiple_of(8 * g, 8), 8)
            out = collide([buf_ref[side, q, r, :] for q in range(Q)])
            for q in range(Q):
                post_ref[side, q, r, :] = out[q]
            return carry

        lax.fori_loop(0, blocks // 8, step, 0)
        bits = bits_ref[side]
        to = send_rows(nbr_ref[side : side + 1, :], first + (blocks if side == 0 else -blocks), blocks, pack_ref.shape[2])
        face, layer = side_slots(side)
        slots = [post_ref[side, q] for q in face]
        for q in layer:
            ex, ey, ez = VEL[q]
            x = post_ref[side, q]
            turn = 64 * abs(ex)
            out = roll(x, turn + 8 * ey + ez)
            _, cy, cz = edges(q, t, tiles, half, j, k)
            if ey or ez:
                parts = split(x)
            if ey:
                out = jnp.where(cy, roll(dot(hot[face_of(1, ey)], parts), turn - 56 * ey + ez), out)
            if ez:
                out = jnp.where(cz, roll(dot(hot[face_of(2, ez)], parts), turn + 8 * ey - 7 * ez), out)
            if q:
                out = jnp.where((bits & (1 << q)) != 0, post_ref[side, OPP[q]], out)
            slots.append(out)
        slots.append(code)
        for s in range(0, len(slots), 2):
            a, b = slots[s], slots[s + 1]
            packed = jnp.where(half, b, roll(a, 64)) if side == 0 else jnp.where(half, roll(b, 64), a)
            pack_ref[side, s // 2] = dot(to, split(packed))
    n = pack_ref.shape[1]
    for s in range(n):
        sa_ref[s] = jnp.where(even, pack_ref[0, s], pack_ref[1, s])
        sb_ref[s] = jnp.where(even, pack_ref[1, s], pack_ref[0, s])
    sa_ref[n] = cg_ref[...]
    sb_ref[n] = cg_ref[...]


def inner_kernel(pop_ref, nbr_ref, ifc_ref, solid_ref, outer_ref, obits_ref, cur_ref, bits_ref, code_ref, spread_ref, take_ref, mid_ref, *, count):
    position = lax.axis_index("blk")
    blocks = solid_ref.shape[0]
    tiles = solid_ref.shape[1] // LANES
    first = position * blocks
    groups = blocks // 8

    def step(i, carry):
        n, g = i // groups, i % groups
        r = pl.ds(pl.multiple_of(8 * g, 8), 8)
        l = pl.ds(pl.multiple_of(LANES * (n + 1), LANES), LANES)
        out = collide([pop_ref[q, r, l] for q in range(Q)])
        for q in range(Q):
            mid_ref[n, q, r, :] = out[q]
        return carry

    lax.fori_loop(0, groups * (tiles - 2), step, 0)
    code_ref[...] = coarse_code(ifc_ref, position, count)
    for t, m in enumerate(spread_matrix(tiles)):
        spread_ref[t] = m
    cap = take_ref.shape[2] // 2
    take_ref[0] = take_rows(nbr_ref[0:1, :], first + blocks, blocks, cap)
    take_ref[1] = take_rows(nbr_ref[1:2, :], first - blocks, blocks, cap)
    absent = absences(nbr_ref, ifc_ref)
    hot = local_hots(nbr_ref, first)
    span = [slice(LANES * t, LANES * (t + 1)) for t in range(tiles)]
    solid = [solid_ref[:, span[t]] for t in range(tiles)]
    bits_ref[:, span[0]] = obits_ref[1]
    bits_ref[:, span[-1]] = obits_ref[0]
    for t in range(1, tiles - 1):
        bits_ref[:, span[t]] = bounce_bits(t, solid, absent)

    def post(q, t):
        if t == 0:
            return outer_ref[1, q]
        return outer_ref[0, q] if t == tiles - 1 else mid_ref[t - 1, q]

    for q in range(Q):
        x = [post(q, t) for t in range(tiles)]
        ghosts = gathers(q, x, hot, None, None)
        for t in range(tiles):
            cur_ref[q, :, span[t]] = pull(
                q, t, x, ghosts, ghosts[0], hot, None, bits_ref[:, span[t]], post(OPP[q], t), pop_ref[q, :, span[t]]
            )


def final_kernel(cur_ref, outer_ref, bits_ref, code_ref, spread_ref, take_ref, cg_ref, far_ref, ra_ref, rb_ref, nbr_ref, out_ref, now_ref, post_ref, fine_ref, buf_ref, ghost_ref, got_ref, sem, *, count):
    position = lax.axis_index("blk")
    blocks, cells = bits_ref.shape
    tiles = cells // LANES
    first = position * blocks
    even = position % 2 == 0
    half, j, k = lanes(blocks)
    span = [slice(LANES * t, LANES * (t + 1)) for t in range(tiles)]
    n = ra_ref.shape[0] - 1

    for s in range(n):
        got_ref[0, s] = dot(take_ref[0], split(jnp.where(even, ra_ref[s], rb_ref[s])))
        got_ref[1, s] = dot(take_ref[1], split(jnp.where(even, rb_ref[s], ra_ref[s])))

    def from_next(s):
        return got_ref[0, s // 2] if s % 2 == 0 else roll(got_ref[0, s // 2], 64)

    def from_prev(s):
        return got_ref[1, s // 2] if s % 2 == 1 else roll(got_ref[1, s // 2], 64)

    up_face, up_layer = side_slots(1)
    low_face, low_layer = side_slots(0)
    up = {q: from_next(s) for s, q in enumerate(up_face)}
    low = {q: from_prev(s) for s, q in enumerate(low_face)}
    code = code_ref[...]
    up_code = both_halves(from_next(2 * n - 1), False)
    low_code = both_halves(from_prev(2 * n - 1), True)
    near = jnp.where(even, ra_ref[n], rb_ref[n])

    rows = coarse_rows(code, both_halves(near, False), count)
    for t in range(tiles):
        for s, v in enumerate(coarse_tile(rows, spread_ref[t])):
            fine_ref[s, :, span[t]] = v
    patched = [q for q in range(Q) if VEL[q][0] or VEL[q][1] < 0]
    for q in patched:
        ex, ey, ez = VEL[q]
        for t in range(tiles):
            v = cur_ref[q, :, span[t]]
            cx, cy, cz = edges(q, t, tiles, half, j, k)
            if ey < 0:
                f = [fine_ref[CROSSING[2].index(q), :, span[m]] for m in range(tiles)]
                g = roll(sources(q, t, f, f[t], half), 64 * abs(ex) - 56 * ey + ez)
                ok = cy
                if cx is not None:
                    ok = ok & jnp.logical_not(cx)
                if cz is not None:
                    ok = ok & jnp.logical_not(cz)
                v = v + jnp.where(ok, g, 0.0)
            if cx is not None:
                ok = cx
                for c in (cy, cz):
                    if c is not None:
                        ok = ok & jnp.logical_not(c)
                v = v + jnp.where(ok, roll(up[q] if ex < 0 else low[q], 64 + 8 * ey + ez), 0.0)
            now_ref[q, :, span[t]] = v

    up_rows = coarse_rows(up_code, both_halves(far_ref[...], False), count)
    low_rows = coarse_rows(low_code, both_halves(cg_ref[...], False), count)
    up_fine = coarse_tile(up_rows, spread_ref[tiles])
    low_fine = coarse_tile(low_rows, spread_ref[tiles])
    for q in range(Q):
        ex, ey, ez = VEL[q]
        _, cy, cz = edges(q, 0, tiles, half, j, k)
        corner = cy if cz is None else (cz if cy is None else cy | cz)
        sides = []
        for e, layer, face, take, mine in (
            (-1, up_layer, up, from_next, outer_ref.at[0]),
            (1, low_layer, low, from_prev, outer_ref.at[1]),
        ):
            if ex == -e:
                v = roll(mine[q], 64 + 8 * ey + ez)
                if corner is not None:
                    v = jnp.where(corner, face[OPP[q]], v)
            else:
                v = take(5 + layer.index(q))
                if ey < 0:
                    f = (up_fine if e < 0 else low_fine)[CROSSING[2].index(q)]
                    ok = cy if cz is None else cy & jnp.logical_not(cz)
                    v = v + jnp.where(ok, roll(f, ez), 0.0)
            sides.append(v)
        ghost_ref[q] = jnp.where(half, sides[1], sides[0])

    def layer_step(g, carry):
        r = pl.ds(pl.multiple_of(8 * g, 8), 8)
        out = collide([ghost_ref[q, r, :] for q in range(Q)])
        for q in range(Q):
            if VEL[q][0]:
                ghost_ref[q, r, :] = out[q]
        return carry

    lax.fori_loop(0, blocks // 8, layer_step, 0)

    def now(q):
        return now_ref if q in patched else cur_ref

    def step(i, carry):
        r = pl.ds(pl.multiple_of(8 * (i // tiles), 8), 8)
        l = pl.ds(pl.multiple_of(LANES * (i % tiles), LANES), LANES)
        out = collide([now(q)[q, r, l] for q in range(Q)])
        for q in range(Q):
            post_ref[q, r, l] = out[q]
        return carry

    lax.fori_loop(0, blocks // 8 * tiles, step, 0)

    rows = coarse_rows(code, both_halves(near, True), count)
    for t in range(tiles):
        for s, v in enumerate(coarse_tile(rows, spread_ref[t])):
            fine_ref[s, :, span[t]] = v
    hot = local_hots(nbr_ref, first)
    remote = {}
    for q in range(Q):
        if VEL[q][0]:
            there = (up_code if VEL[q][0] < 0 else low_code) > 0.5
            remote[q] = jnp.where(there, ghost_ref[q], 0.0)
    copies = []
    for q in range(Q):
        x = [post_ref[q, :, span[t]] for t in range(tiles)]
        ghosts = gathers(q, x, hot, lambda s, t: fine_ref[s, :, span[t]], remote)
        for t in range(tiles):
            buf_ref[q, :, span[t]] = pull(
                q, t, x, ghosts, ghosts[0], hot, None, bits_ref[:, span[t]], post_ref[OPP[q], :, span[t]], now(q)[q, :, span[t]]
            )
        copy = pltpu.make_async_copy(buf_ref.at[q], out_ref.at[q], sem.at[q])
        copy.start()
        copies.append(copy)
    for copy in copies:
        copy.wait()


def shifted(x, by):
    n = lax.axis_size("blk")
    return lax.ppermute(x, "blk", [(i, i + by) for i in range(n) if 0 <= i + by < n])


def swapped(x, off):
    n = lax.axis_size("blk")
    low = [(i, i + 1) for i in range(off, n - 1, 2)]
    return lax.ppermute(x, "blk", low + [(b, a) for a, b in low])


def held(x):
    return pltpu.with_memory_space_constraint(x, pltpu.VMEM)


def body(populations, coarse_faces, neighbors, interface, solid):
    pop = populations.transpose(1, 0, 2)
    co = coarse_faces.transpose(0, 2, 1, 3)
    nbr, ifc = neighbors.T, interface.T
    blocks, cells = pop.shape[1:]
    count = co.shape[0]
    tiles = cells // LANES
    dense = pl.BlockSpec(memory_space=pltpu.VMEM)
    away = pl.BlockSpec(memory_space=pl.ANY)
    cap = blocks // 2
    payload = pltpu.VMEM((11, cap, LANES), F32)
    room = pltpu.CompilerParams(vmem_limit_bytes=20 << 20)
    outer, obits, cg, sa, sb = pl.pallas_call(
        outer_kernel,
        in_specs=[away] + [dense] * 4,
        out_shape=(
            pltpu.VMEM((2, Q, blocks, LANES), F32),
            pltpu.VMEM((2, blocks, LANES), I32),
            pltpu.VMEM((cap, LANES), F32),
            payload,
            payload,
        ),
        scratch_shapes=[
            pltpu.VMEM((2, Q, blocks, LANES), F32),
            pltpu.VMEM((2, 10, cap, LANES), F32),
            pltpu.SemaphoreType.DMA((2,)),
        ],
        name="outer",
    )(pop, nbr, ifc, solid, co)
    ra, rb, far = swapped(sa, 0), swapped(sb, 1), shifted(cg, -2)
    outer, obits = held(outer), held(obits)
    cur, bits, code, spread, take = pl.pallas_call(
        functools.partial(inner_kernel, count=count),
        in_specs=[dense] * 6,
        out_shape=(
            pltpu.VMEM((Q, blocks, cells), F32),
            pltpu.VMEM((blocks, cells), I32),
            pltpu.VMEM((blocks, LANES), F32),
            pltpu.VMEM((tiles + 1, 256, LANES), BF16),
            pltpu.VMEM((2, blocks, 2 * cap), BF16),
        ),
        compiler_params=room,
        scratch_shapes=[pltpu.VMEM((tiles - 2, Q, blocks, LANES), F32)],
        cost_estimate=pl.CostEstimate(flops=100_000_000, bytes_accessed=4_000_000, transcendentals=0),
        name="inner",
    )(pop, nbr, ifc, solid, outer, obits)
    out = pl.pallas_call(
        functools.partial(final_kernel, count=count),
        in_specs=[dense] * 11,
        out_specs=away,
        out_shape=jax.ShapeDtypeStruct(pop.shape, F32),
        scratch_shapes=[
            pltpu.VMEM((Q, blocks, cells), F32),
            pltpu.VMEM((Q, blocks, cells), F32),
            pltpu.VMEM((5, blocks, cells), F32),
            pltpu.VMEM((Q, blocks, cells), F32),
            pltpu.VMEM((Q, blocks, LANES), F32),
            pltpu.VMEM((2, 10, blocks, LANES), F32),
            pltpu.SemaphoreType.DMA((Q,)),
        ],
        compiler_params=room,
        name="final",
    )(*(held(x) for x in (cur, outer, bits, code, spread, take, cg, far, ra, rb)), nbr)
    return out.transpose(1, 0, 2)


def solution(mesh):
    placed = (P("blk", None, None), P("blk", None, None, None), P("blk", None), P("blk", None), P("blk", None))
    return jax.shard_map(body, mesh=mesh, in_specs=placed, out_specs=P("blk", None, None), check_vma=False)
```

```python
import functools

import jax
import jax.numpy as jnp
import numpy as np
from jax import lax
from jax.experimental import pallas as pl
from jax.experimental.pallas import tpu as pltpu
from jax.sharding import PartitionSpec as P

F32, BF16, I32 = jnp.float32, jnp.bfloat16, jnp.int32
LANES = 128
VEL = [
    (0, 0, 0),
    (1, 0, 0), (-1, 0, 0), (0, 1, 0), (0, -1, 0), (0, 0, 1), (0, 0, -1),
    (1, 1, 0), (-1, -1, 0), (1, -1, 0), (-1, 1, 0),
    (1, 0, 1), (-1, 0, -1), (1, 0, -1), (-1, 0, 1),
    (0, 1, 1), (0, -1, -1), (0, 1, -1), (0, -1, 1),
]
Q = len(VEL)
OPP = [VEL.index((-x, -y, -z)) for x, y, z in VEL]
CROSSING = [
    [q for q in range(Q) if VEL[q][d // 2] == (-1 if d % 2 == 0 else 1)] for d in range(6)
]


def rates():
    v = np.array(VEL) * 1.0
    x, y, z = v[:, 0], v[:, 1], v[:, 2]
    s = x * x + y * y + z * z
    rows = [
        np.ones(19), 19 * s - 30, (21 * s * s - 53 * s + 24) / 2,
        x, (5 * s - 9) * x, y, (5 * s - 9) * y, z, (5 * s - 9) * z,
        3 * x * x - s, (3 * s - 5) * (3 * x * x - s),
        y * y - z * z, (3 * s - 5) * (y * y - z * z),
        x * y, y * z, x * z,
        (y * y - z * z) * x, (z * z - x * x) * y, (x * x - y * y) * z,
    ]
    norms = (np.stack(rows) ** 2).sum(1)
    w = 1.0 / 0.6
    relax = np.array([0, 1.19, 1.4, 0, 1.2, 0, 1.2, 0, 1.2, w, 1.4, w, 1.4, w, w, w, 1.98, 1.98, 1.98])
    return [float(c) for c in relax / norms]


def collide(f):
    c = rates()
    s = {q: f[q] + f[q + 1] for q in range(1, 19, 2)}
    d = {q: f[q] - f[q + 1] for q in range(1, 19, 2)}
    a, b, g = s[7] + s[9], s[11] + s[13], s[15] + s[17]
    s1, s2 = s[1] + (s[3] + s[5]), a + b + g
    rho = f[0] + s1 + s2
    ax1, ax2 = d[7] + d[9], d[11] + d[13]
    ay1, ay2 = d[7] - d[9], d[15] + d[17]
    az1, az2 = d[11] - d[13], d[15] - d[17]
    ax, ay, az = ax1 + ax2, ay1 + ay2, az1 + az2
    jx, jy, jz = d[1] + ax, d[3] + ay, d[5] + az
    inv = 1.0 / rho
    ux, uy, uz = jx * inv, jy * inv, jz * inv
    xx, yy, zz = jx * ux, jy * uy, jz * uz
    jj = xx + yy + zz
    r1 = (19 * c[1]) * (s2 - f[0] - jj)
    r2 = c[2] * (9 * f[0] - 7 * s1 - 2 * s2 + 5.5 * jj)
    t1, t2, pe = 2 * s[1] - (s[3] + s[5]), a + b - 2 * g, 3 * xx - jj
    v1, v2, we = s[3] - s[5], a - b, yy - zz
    r9, r10 = c[9] * (t1 + t2 - pe), c[10] * (t2 - 2 * t1 + 0.5 * pe)
    r11, r12 = c[11] * (v1 + v2 - we), c[12] * (v2 - 2 * v1 + 0.5 * we)
    r13 = c[13] * (s[7] - s[9] - jx * uy)
    r14 = c[14] * (s[15] - s[17] - jy * uz)
    r15 = c[15] * (s[11] - s[13] - jx * uz)
    r4 = (c[4] * 5 / 3) * (ax - 2 * d[1])
    r6 = (c[6] * 5 / 3) * (ay - 2 * d[3])
    r8 = (c[8] * 5 / 3) * (az - 2 * d[5])
    r16, r17, r18 = c[16] * (ax1 - ax2), c[17] * (ay2 - ay1), c[18] * (az1 - az2)
    ea, eb = -11 * r1 - 4 * r2, 8 * r1 + r2
    a9, a11 = r9 - 2 * r10, r11 - 2 * r12
    b9, b11 = r9 + r10, r11 + r12
    exy, exz, eyz = eb + b9 + b11, eb + b9 - b11, eb - 2 * b9
    even = {
        1: ea + 2 * a9, 3: ea - a9 + a11, 5: ea - a9 - a11,
        7: exy + r13, 9: exy - r13, 11: exz + r15, 13: exz - r15, 15: eyz + r14, 17: eyz - r14,
    }
    odd = {
        1: -4 * r4, 3: -4 * r6, 5: -4 * r8,
        7: (r4 + r6) + (r16 - r17), 9: (r4 - r6) + (r16 + r17),
        11: (r4 + r8) - (r16 - r18), 13: (r4 - r8) - (r16 + r18),
        15: (r6 + r8) + (r17 - r18), 17: (r6 - r8) + (r17 + r18),
    }
    out = [f[0] + 30 * r1 - 12 * r2]
    for q in range(1, 19, 2):
        out += [f[q] - even[q] - odd[q], f[q + 1] - even[q] + odd[q]]
    return out


def feq(h):
    rho = h[0]
    for q in range(1, Q):
        rho = rho + h[q]
    safe = jnp.where(rho > 0, rho, 1.0)
    u = []
    for axis in range(3):
        m = None
        for q in range(Q):
            if VEL[q][axis]:
                t = h[q] if VEL[q][axis] > 0 else -h[q]
                m = t if m is None else m + t
        u.append(m / safe)
    sq = u[0] * u[0] + u[1] * u[1] + u[2] * u[2]
    out = {}
    for q in CROSSING[2]:
        p = None
        for axis in range(3):
            if VEL[q][axis]:
                t = u[axis] if VEL[q][axis] > 0 else -u[axis]
                p = t if p is None else p + t
        n = sum(abs(e) for e in VEL[q])
        w = 1.0 / 18.0 if n == 1 else 1.0 / 36.0
        out[q] = w * rho * (1.0 + 3.0 * p + 4.5 * p * p - 1.5 * sq)
    return out


def lanes(rows):
    l = lax.broadcasted_iota(I32, (rows, LANES), 1)
    return l >= 64, (l >> 3) & 7, l & 7


def split(x):
    hi = x.astype(BF16)
    lo = (x - hi.astype(F32)).astype(BF16)
    return jnp.concatenate([hi, lo], axis=0)


def dot(a, b):
    return jnp.dot(a, b, preferred_element_type=F32)


def select_rows(row, offset, count):
    r = lax.broadcasted_iota(I32, (count, row.shape[1]), 0)
    hot = jnp.where(r == row - offset, 1.0, 0.0).astype(BF16)
    return jnp.concatenate([hot, hot], axis=1)


def spread_rows(flags):
    n = flags.shape[1]
    eye = lax.broadcasted_iota(I32, (n, n), 0) == lax.broadcasted_iota(I32, (n, n), 1)
    diag = jnp.where(eye, flags.astype(F32), 0.0).astype(BF16)
    return dot(diag, jnp.ones((n, LANES), BF16))


def sources(q, t, tiles, outer, half):
    ex = VEL[q][0]
    if ex == 0:
        return tiles[t]
    n = t - ex
    other = tiles[n] if 0 <= n < len(tiles) else outer
    return jnp.where(half, other, tiles[t]) if ex > 0 else jnp.where(half, tiles[t], other)


def roll(x, by):
    by %= LANES
    return pltpu.roll(x, by, 1) if by else x


def edges(q, t, count, half, j, k):
    ex, ey, ez = VEL[q]
    cx = None
    if ex > 0 and t == 0:
        cx = jnp.logical_not(half)
    if ex < 0 and t == count - 1:
        cx = half
    cy = None if ey == 0 else (j == (0 if ey > 0 else 7))
    cz = None if ez == 0 else (k == (0 if ez > 0 else 7))
    return cx, cy, cz


def face_of(axis, e):
    return 2 * axis + (1 if e > 0 else 0)


def bounce_bits(t, solid, absent):
    half, j, k = lanes(solid[0].shape[0])
    acc = jnp.where(solid[t] != 0, 1, 0)
    for q in range(1, Q):
        ex, ey, ez = VEL[q]
        v = roll(sources(q, t, solid, solid[t], half), 64 * abs(ex) + 8 * ey + ez)
        sides = zip(edges(q, t, len(solid), half, j, k), (ex, ey, ez), range(3))
        crossed = [c for c in sides if c[0] is not None]
        for c, e, axis in crossed:
            v = jnp.where(c, absent[face_of(axis, e)], v)
        for i in range(len(crossed)):
            for m in range(i):
                v = jnp.where(crossed[i][0] & crossed[m][0], 1, v)
        acc = acc | (jnp.where(v != 0, 1, 0) << q)
    return acc


def absences(nbr_ref, ifc_ref):
    out = []
    for d in range(6):
        there = nbr_ref[d : d + 1, :] >= 0
        if d == 2:
            there = there | (ifc_ref[0:1, :] >= 0)
        out.append((1.0 - spread_rows(jnp.where(there, 1.0, 0.0))).astype(I32))
    return out


def local_hots(nbr_ref, first):
    n = nbr_ref.shape[1]
    return [select_rows(nbr_ref[(d ^ 1) : (d ^ 1) + 1, :], first, n) for d in range(6)]


def send_rows(row, first, count, cap):
    rel = row - first
    gone = (rel >= 0) & (rel < count)
    rel = jnp.where(gone, rel, 255)
    ahead = spread_rows(rel)[:, :count] < rel.astype(F32)
    rank = jnp.sum(jnp.where(ahead, 1.0, 0.0), axis=0, keepdims=True)
    r = lax.broadcasted_iota(I32, (cap, count), 0).astype(F32)
    hot = jnp.where((r == rank) & gone, 1.0, 0.0).astype(BF16)
    return jnp.concatenate([hot, hot], axis=1)


def take_rows(row, first, count, cap):
    rel = row - first
    gone = jnp.where((rel >= 0) & (rel < count), 1.0, 0.0)
    b = lax.broadcasted_iota(I32, (count, count), 0)
    a = lax.broadcasted_iota(I32, (count, count), 1)
    rank = dot(jnp.where(a < b, gone, 0.0).astype(BF16), jnp.ones((count, LANES), BF16))[:, :cap]
    there = spread_rows(gone)[:, :cap] > 0.5
    r = lax.broadcasted_iota(I32, (count, cap), 1).astype(F32)
    hot = jnp.where((r == rank) & there, 1.0, 0.0).astype(BF16)
    return jnp.concatenate([hot, hot], axis=1)


def coarse_code(ifc_ref, position, count):
    c = ifc_ref[0:1, :]
    code = jnp.where(c >= 0, 2 + 4 * (c - (position + 1) * count) + ifc_ref[1:2, :], 1)
    return spread_rows(code)


def coarse_values(co_ref, cg_ref):
    count = co_ref.shape[0]
    h = []
    for q in range(Q):
        h0 = co_ref[:, q, 0, :]
        h1 = (1.0 - 0.5) * h0 + 0.5 * co_ref[:, q, 1, :]
        h.append(jnp.concatenate([h0, h1], axis=1))
    e = feq(h)
    cg_ref[...] = jnp.zeros_like(cg_ref)
    for s, q in enumerate(CROSSING[2]):
        v = e[q] + (0.6 / 1.1) * (h[q] - e[q])
        for c in range(count):
            cg_ref[5 * c + s : 5 * c + s + 1, :] = v[c : c + 1]


def both_halves(x, upper):
    half = lanes(x.shape[0])[0]
    return jnp.where(half, x, roll(x, 64)) if upper else jnp.where(half, roll(x, 64), x)


def spread_matrix(tiles):
    kk = lax.broadcasted_iota(I32, (256, LANES), 0)
    ll = lax.broadcasted_iota(I32, (256, LANES), 1)
    w, m, k = kk >> 6, kk & 63, ll & 7
    out = []
    for t in range(tiles + 1):
        i = (ll >> 6) * 7 if t == tiles else 2 * t + (ll >> 6)
        want = 8 * (4 * (w >> 1) + (i >> 1)) + 4 * (w & 1) + (k >> 1)
        out.append(jnp.where(m == want, 1.0, 0.0).astype(BF16))
    return out


def coarse_rows(code, cg, count):
    half = lanes(code.shape[0])[0]
    hi, lo = [], []
    for s in range(5):
        parts = []
        for pair in (0, 2):
            acc = jnp.zeros_like(code)
            for c in range(count):
                want = jnp.where(half, 3.0 + 4 * c + pair, 2.0 + 4 * c + pair)
                acc = jnp.where(code == want, cg[5 * c + s : 5 * c + s + 1, :], acc)
            parts.append(acc)
        x = jnp.concatenate(parts, axis=1)
        h = x.astype(BF16)
        hi.append(h)
        lo.append((x - h.astype(F32)).astype(BF16))
    return jnp.concatenate(hi + lo, axis=0)


def coarse_tile(rows, matrix):
    g = dot(rows, matrix)
    n = g.shape[0] // 2
    g = g[:n] + g[n:]
    b = n // 5
    return [g[b * s : b * (s + 1)] for s in range(5)]


def pull(q, t, x, parts, gx, hot, fine, bits, bounced, init):
    if q == 0:
        return jnp.where((bits & 1) != 0, init, x[t])
    half, j, k = lanes(bits.shape[0])
    ex, ey, ez = VEL[q]
    turn = 64 * abs(ex)
    out = roll(sources(q, t, x, gx, half), turn + 8 * ey + ez)
    _, cy, cz = edges(q, t, len(x), half, j, k)
    if ey:
        g = parts[1]
        out = jnp.where(cy, roll(sources(q, t, g, g[t], half), turn - 56 * ey + ez), out)
    if ez:
        g = parts[2]
        out = jnp.where(cz, roll(sources(q, t, g, g[t], half), turn + 8 * ey - 7 * ez), out)
    out = jnp.where((bits & (1 << q)) != 0, bounced, out)
    return jnp.where((bits & 1) != 0, init, out)


def gathers(q, x, hot, fine, remote):
    ex, ey, ez = VEL[q]
    gx, gy, gz = None, None, None
    if q:
        parts = [split(v) for v in x]
    if ex:
        gx = dot(hot[face_of(0, ex)], parts[0 if ex < 0 else len(x) - 1])
        if remote is not None:
            gx = gx + remote[q]
    if ey:
        gy = [dot(hot[face_of(1, ey)], p) for p in parts]
        if ey < 0 and fine is not None:
            s = CROSSING[2].index(q)
            gy = [g + fine(s, t) for t, g in enumerate(gy)]
    if ez:
        gz = [dot(hot[face_of(2, ez)], p) for p in parts]
    return gx, gy, gz


def side_slots(d):
    e = 1 if d == 0 else -1
    return [q for q in range(Q) if VEL[q][0] == e], [q for q in range(Q) if VEL[q][0] != -e]


def outer_kernel(pop_ref, *refs):
    given, (post_ref, bits_ref, cg_ref, sa_ref, sb_ref), (buf_ref, pack_ref, *held_refs, sem) = refs[:4], refs[4:9], refs[9:]
    small = [pltpu.make_async_copy(a, b, sem.at[2 + i]) for i, (a, b) in enumerate(zip(given, held_refs))]
    for copy in small:
        copy.start()
    nbr_ref, ifc_ref, solid_ref, co_ref = held_refs
    position = lax.axis_index("blk")
    blocks = solid_ref.shape[0]
    tiles = solid_ref.shape[1] // LANES
    first = position * blocks
    even = position % 2 == 0
    count = co_ref.shape[0]
    copies = []
    for side, t in ((0, tiles - 1), (1, 0)):
        copy = pltpu.make_async_copy(
            pop_ref.at[:, :, pl.ds(LANES * t, LANES)], buf_ref.at[side], sem.at[side]
        )
        copy.start()
        copies.append(copy)
    half, j, k = lanes(blocks)
    for copy in small:
        copy.wait()
    coarse_values(co_ref, cg_ref)
    code = coarse_code(ifc_ref, position, count)
    absent = absences(nbr_ref, ifc_ref)
    hot = local_hots(nbr_ref, first)
    solid = [solid_ref[:, LANES * t : LANES * (t + 1)] for t in range(tiles)]
    bits_ref[0] = bounce_bits(tiles - 1, solid, absent)
    bits_ref[1] = bounce_bits(0, solid, absent)
    for side, t in ((0, tiles - 1), (1, 0)):
        copies[side].wait()

        def step(g, carry, side=side):
            r = pl.ds(pl.multiple_of(8 * g, 8), 8)
            out = collide([buf_ref[side, q, r, :] for q in range(Q)])
            for q in range(Q):
                post_ref[side, q, r, :] = out[q]
            return carry

        lax.fori_loop(0, blocks // 8, step, 0)
        bits = bits_ref[side]
        to = send_rows(nbr_ref[side : side + 1, :], first + (blocks if side == 0 else -blocks), blocks, pack_ref.shape[2])
        face, layer = side_slots(side)
        slots = [post_ref[side, q] for q in face]
        for q in layer:
            ex, ey, ez = VEL[q]
            x = post_ref[side, q]
            turn = 64 * abs(ex)
            out = roll(x, turn + 8 * ey + ez)
            _, cy, cz = edges(q, t, tiles, half, j, k)
            if ey or ez:
                parts = split(x)
            if ey:
                out = jnp.where(cy, roll(dot(hot[face_of(1, ey)], parts), turn - 56 * ey + ez), out)
            if ez:
                out = jnp.where(cz, roll(dot(hot[face_of(2, ez)], parts), turn + 8 * ey - 7 * ez), out)
            if q:
                out = jnp.where((bits & (1 << q)) != 0, post_ref[side, OPP[q]], out)
            slots.append(out)
        slots.append(code)
        for s in range(0, len(slots), 2):
            a, b = slots[s], slots[s + 1]
            packed = jnp.where(half, b, roll(a, 64)) if side == 0 else jnp.where(half, roll(b, 64), a)
            pack_ref[side, s // 2] = dot(to, split(packed))
    n = pack_ref.shape[1]
    for s in range(n):
        sa_ref[s] = jnp.where(even, pack_ref[0, s], pack_ref[1, s])
        sb_ref[s] = jnp.where(even, pack_ref[1, s], pack_ref[0, s])
    sa_ref[n] = cg_ref[...]
    sb_ref[n] = cg_ref[...]


def inner_kernel(pop_ref, nbr_ref, ifc_ref, solid_ref, outer_ref, obits_ref, cur_ref, bits_ref, code_ref, spread_ref, take_ref, mid_ref, *, count):
    position = lax.axis_index("blk")
    blocks = solid_ref.shape[0]
    tiles = solid_ref.shape[1] // LANES
    first = position * blocks
    groups = blocks // 8

    def step(i, carry):
        n, g = i // groups, i % groups
        r = pl.ds(pl.multiple_of(8 * g, 8), 8)
        l = pl.ds(pl.multiple_of(LANES * (n + 1), LANES), LANES)
        out = collide([pop_ref[q, r, l] for q in range(Q)])
        for q in range(Q):
            mid_ref[n, q, r, :] = out[q]
        return carry

    lax.fori_loop(0, groups * (tiles - 2), step, 0)
    code_ref[...] = coarse_code(ifc_ref, position, count)
    for t, m in enumerate(spread_matrix(tiles)):
        spread_ref[t] = m
    cap = take_ref.shape[2] // 2
    take_ref[0] = take_rows(nbr_ref[0:1, :], first + blocks, blocks, cap)
    take_ref[1] = take_rows(nbr_ref[1:2, :], first - blocks, blocks, cap)
    absent = absences(nbr_ref, ifc_ref)
    hot = local_hots(nbr_ref, first)
    span = [slice(LANES * t, LANES * (t + 1)) for t in range(tiles)]
    solid = [solid_ref[:, span[t]] for t in range(tiles)]
    bits_ref[:, span[0]] = obits_ref[1]
    bits_ref[:, span[-1]] = obits_ref[0]
    for t in range(1, tiles - 1):
        bits_ref[:, span[t]] = bounce_bits(t, solid, absent)

    def post(q, t):
        if t == 0:
            return outer_ref[1, q]
        return outer_ref[0, q] if t == tiles - 1 else mid_ref[t - 1, q]

    for q in range(Q):
        x = [post(q, t) for t in range(tiles)]
        ghosts = gathers(q, x, hot, None, None)
        for t in range(tiles):
            cur_ref[q, :, span[t]] = pull(
                q, t, x, ghosts, ghosts[0], hot, None, bits_ref[:, span[t]], post(OPP[q], t), pop_ref[q, :, span[t]]
            )


def patched(q):
    return VEL[q][0] != 0 or VEL[q][1] < 0


def current_kernel(cur_ref, outer_ref, code_ref, spread_ref, take_ref, cg_ref, ra_ref, rb_ref, now_ref, post_ref, fine_ref, ghost_ref, codes_ref, got_ref, *, count):
    position = lax.axis_index("blk")
    blocks, cells = cur_ref.shape[1:]
    tiles = cells // LANES
    even = position % 2 == 0
    half, j, k = lanes(blocks)
    span = [slice(LANES * t, LANES * (t + 1)) for t in range(tiles)]
    n = ra_ref.shape[0] - 1

    for s in range(n):
        got_ref[0, s] = dot(take_ref[0], split(jnp.where(even, ra_ref[s], rb_ref[s])))
        got_ref[1, s] = dot(take_ref[1], split(jnp.where(even, rb_ref[s], ra_ref[s])))

    def from_next(s):
        return got_ref[0, s // 2] if s % 2 == 0 else roll(got_ref[0, s // 2], 64)

    def from_prev(s):
        return got_ref[1, s // 2] if s % 2 == 1 else roll(got_ref[1, s // 2], 64)

    up_face, up_layer = side_slots(1)
    low_face, low_layer = side_slots(0)
    up = {q: from_next(s) for s, q in enumerate(up_face)}
    low = {q: from_prev(s) for s, q in enumerate(low_face)}
    code = code_ref[...]
    up_code = both_halves(from_next(2 * n - 1), False)
    low_code = both_halves(from_prev(2 * n - 1), True)
    codes_ref[0] = up_code
    codes_ref[1] = low_code
    near = jnp.where(even, ra_ref[n], rb_ref[n])

    rows = coarse_rows(code, both_halves(near, False), count)
    for t in range(tiles):
        for s, v in enumerate(coarse_tile(rows, spread_ref[t])):
            fine_ref[s, :, span[t]] = v
    for q in range(Q):
        ex, ey, ez = VEL[q]
        for t in range(tiles):
            v = cur_ref[q, :, span[t]]
            cx, cy, cz = edges(q, t, tiles, half, j, k)
            if ey < 0:
                f = [fine_ref[CROSSING[2].index(q), :, span[m]] for m in range(tiles)]
                g = roll(sources(q, t, f, f[t], half), 64 * abs(ex) - 56 * ey + ez)
                ok = cy
                if cx is not None:
                    ok = ok & jnp.logical_not(cx)
                if cz is not None:
                    ok = ok & jnp.logical_not(cz)
                v = v + jnp.where(ok, g, 0.0)
            if cx is not None:
                ok = cx
                for c in (cy, cz):
                    if c is not None:
                        ok = ok & jnp.logical_not(c)
                v = v + jnp.where(ok, roll(up[q] if ex < 0 else low[q], 64 + 8 * ey + ez), 0.0)
            now_ref[q, :, span[t]] = v

    low_rows = coarse_rows(low_code, both_halves(cg_ref[...], False), count)
    low_fine = coarse_tile(low_rows, spread_ref[tiles])
    for q in range(Q):
        ex, ey, ez = VEL[q]
        _, cy, cz = edges(q, 0, tiles, half, j, k)
        corner = cy if cz is None else (cz if cy is None else cy | cz)
        sides = []
        for e, layer, face, take, mine in (
            (-1, up_layer, up, from_next, outer_ref.at[0]),
            (1, low_layer, low, from_prev, outer_ref.at[1]),
        ):
            if ex == -e:
                v = roll(mine[q], 64 + 8 * ey + ez)
                if corner is not None:
                    v = jnp.where(corner, face[OPP[q]], v)
            else:
                v = take(5 + layer.index(q))
                if ey < 0 and e > 0:
                    ok = cy if cz is None else cy & jnp.logical_not(cz)
                    v = v + jnp.where(ok, roll(low_fine[CROSSING[2].index(q)], ez), 0.0)
            sides.append(v)
        ghost_ref[q] = jnp.where(half, sides[1], sides[0])

    def step(i, carry):
        r = pl.ds(pl.multiple_of(8 * (i // tiles), 8), 8)
        l = pl.ds(pl.multiple_of(LANES * (i % tiles), LANES), LANES)
        out = collide([now_ref[q, r, l] for q in range(Q)])
        for q in range(Q):
            post_ref[q, r, l] = out[q]
        return carry

    lax.fori_loop(0, blocks // 8 * tiles, step, 0)

    rows = coarse_rows(code, both_halves(near, True), count)
    for t in range(tiles):
        for s, v in enumerate(coarse_tile(rows, spread_ref[t])):
            fine_ref[s, :, span[t]] = v


def final_kernel(now_ref, post_ref, fine_ref, half_ref, codes_ref, bits_ref, spread_ref, far_ref, nbr_ref, out_ref, buf_ref, ghost_ref, sem, *, count):
    position = lax.axis_index("blk")
    blocks, cells = bits_ref.shape
    tiles = cells // LANES
    first = position * blocks
    half, j, k = lanes(blocks)
    span = [slice(LANES * t, LANES * (t + 1)) for t in range(tiles)]
    up_rows = coarse_rows(codes_ref[0], both_halves(far_ref[...], False), count)
    up_fine = coarse_tile(up_rows, spread_ref[tiles])
    for q in range(Q):
        v = half_ref[q]
        if VEL[q][1] < 0 and VEL[q][0] <= 0:
            _, cy, cz = edges(q, 0, tiles, half, j, k)
            ok = cy & jnp.logical_not(half)
            if cz is not None:
                ok = ok & jnp.logical_not(cz)
            v = v + jnp.where(ok, roll(up_fine[CROSSING[2].index(q)], VEL[q][2]), 0.0)
        ghost_ref[q] = v

    def layer_step(g, carry):
        r = pl.ds(pl.multiple_of(8 * g, 8), 8)
        out = collide([ghost_ref[q, r, :] for q in range(Q)])
        for q in range(Q):
            if VEL[q][0]:
                ghost_ref[q, r, :] = out[q]
        return carry

    lax.fori_loop(0, blocks // 8, layer_step, 0)
    hot = local_hots(nbr_ref, first)
    remote = {}
    for q in range(Q):
        if VEL[q][0]:
            there = codes_ref[0 if VEL[q][0] < 0 else 1] > 0.5
            remote[q] = jnp.where(there, ghost_ref[q], 0.0)
    copies = []
    for q in range(Q):
        x = [post_ref[q, :, span[t]] for t in range(tiles)]
        ghosts = gathers(q, x, hot, lambda s, t: fine_ref[s, :, span[t]], remote)
        for t in range(tiles):
            buf_ref[q, :, span[t]] = pull(
                q, t, x, ghosts, ghosts[0], hot, None, bits_ref[:, span[t]], post_ref[OPP[q], :, span[t]], now_ref[q, :, span[t]]
            )
        copy = pltpu.make_async_copy(buf_ref.at[q], out_ref.at[q], sem.at[q])
        copy.start()
        copies.append(copy)
    for copy in copies:
        copy.wait()


def shifted(x, by):
    n = lax.axis_size("blk")
    return lax.ppermute(x, "blk", [(i, i + by) for i in range(n) if 0 <= i + by < n])


def swapped(x, off):
    n = lax.axis_size("blk")
    low = [(i, i + 1) for i in range(off, n - 1, 2)]
    return lax.ppermute(x, "blk", low + [(b, a) for a, b in low])


def held(x):
    return pltpu.with_memory_space_constraint(x, pltpu.VMEM)


def body(populations, coarse_faces, neighbors, interface, solid):
    pop = populations.transpose(1, 0, 2)
    co = coarse_faces.transpose(0, 2, 1, 3)
    nbr, ifc = neighbors.T, interface.T
    blocks, cells = pop.shape[1:]
    count = co.shape[0]
    tiles = cells // LANES
    dense = pl.BlockSpec(memory_space=pltpu.VMEM)
    away = pl.BlockSpec(memory_space=pl.ANY)
    cap = blocks // 2
    payload = pltpu.VMEM((11, cap, LANES), F32)
    room = pltpu.CompilerParams(vmem_limit_bytes=20 << 20)
    outer, obits, cg, sa, sb = pl.pallas_call(
        outer_kernel,
        in_specs=[away] * 5,
        out_shape=(
            pltpu.VMEM((2, Q, blocks, LANES), F32),
            pltpu.VMEM((2, blocks, LANES), I32),
            pltpu.VMEM((cap, LANES), F32),
            payload,
            payload,
        ),
        scratch_shapes=[
            pltpu.VMEM((2, Q, blocks, LANES), F32),
            pltpu.VMEM((2, 10, cap, LANES), F32),
            *(pltpu.VMEM(a.shape, a.dtype) for a in (nbr, ifc, solid, co)),
            pltpu.SemaphoreType.DMA((6,)),
        ],
        name="outer",
    )(pop, nbr, ifc, solid, co)
    rb = swapped(sb, 1)
    far = shifted(cg, -2)
    ra = swapped(sa, 0)
    outer, obits = held(outer), held(obits)
    cur, bits, code, spread, take = pl.pallas_call(
        functools.partial(inner_kernel, count=count),
        in_specs=[dense] * 6,
        out_shape=(
            pltpu.VMEM((Q, blocks, cells), F32),
            pltpu.VMEM((blocks, cells), I32),
            pltpu.VMEM((blocks, LANES), F32),
            pltpu.VMEM((tiles + 1, 256, LANES), BF16),
            pltpu.VMEM((2, blocks, 2 * cap), BF16),
        ),
        compiler_params=room,
        scratch_shapes=[pltpu.VMEM((tiles - 2, Q, blocks, LANES), F32)],
        cost_estimate=pl.CostEstimate(flops=100_000_000, bytes_accessed=4_000_000, transcendentals=0),
        name="inner",
    )(pop, nbr, ifc, solid, outer, obits)
    state = pltpu.VMEM((Q, blocks, cells), F32)
    layer = pltpu.VMEM((Q, blocks, LANES), F32)
    now, post, fine, ghost, codes = pl.pallas_call(
        functools.partial(current_kernel, count=count),
        in_specs=[dense] * 8,
        out_shape=(state, state, pltpu.VMEM((5, blocks, cells), F32), layer, pltpu.VMEM((2, blocks, LANES), F32)),
        scratch_shapes=[pltpu.VMEM((2, 10, blocks, LANES), F32)],
        compiler_params=room,
        cost_estimate=pl.CostEstimate(flops=100_000_000, bytes_accessed=4_000_000, transcendentals=0),
        name="current",
    )(*(held(x) for x in (cur, outer, code, spread, take, cg, ra, rb)))
    out = pl.pallas_call(
        functools.partial(final_kernel, count=count),
        in_specs=[dense] * 9,
        out_specs=away,
        out_shape=jax.ShapeDtypeStruct(pop.shape, F32),
        scratch_shapes=[state, layer, pltpu.SemaphoreType.DMA((Q,))],
        compiler_params=room,
        name="final",
    )(*(held(x) for x in (now, post, fine, ghost, codes, bits, spread, far)), nbr)
    return out.transpose(1, 0, 2)


def solution(mesh):
    placed = (P("blk", None, None), P("blk", None, None, None), P("blk", None), P("blk", None), P("blk", None))
    return jax.shard_map(body, mesh=mesh, in_specs=placed, out_specs=P("blk", None, None), check_vma=False)
```

```python
import functools

import jax
import jax.numpy as jnp
import numpy as np
from jax import lax
from jax.experimental import pallas as pl
from jax.experimental.pallas import tpu as pltpu
from jax.sharding import PartitionSpec as P


F32, BF16, I32 = jnp.float32, jnp.bfloat16, jnp.int32
LANES = 128
VEL = [
    (0, 0, 0),
    (1, 0, 0), (-1, 0, 0), (0, 1, 0), (0, -1, 0), (0, 0, 1), (0, 0, -1),
    (1, 1, 0), (-1, -1, 0), (1, -1, 0), (-1, 1, 0),
    (1, 0, 1), (-1, 0, -1), (1, 0, -1), (-1, 0, 1),
    (0, 1, 1), (0, -1, -1), (0, 1, -1), (0, -1, 1),
]
Q = len(VEL)
OPP = [VEL.index((-x, -y, -z)) for x, y, z in VEL]
CROSSING = [
    [q for q in range(Q) if VEL[q][d // 2] == (-1 if d % 2 == 0 else 1)] for d in range(6)
]


def rates():
    v = np.array(VEL) * 1.0
    x, y, z = v[:, 0], v[:, 1], v[:, 2]
    s = x * x + y * y + z * z
    rows = [
        np.ones(19), 19 * s - 30, (21 * s * s - 53 * s + 24) / 2,
        x, (5 * s - 9) * x, y, (5 * s - 9) * y, z, (5 * s - 9) * z,
        3 * x * x - s, (3 * s - 5) * (3 * x * x - s),
        y * y - z * z, (3 * s - 5) * (y * y - z * z),
        x * y, y * z, x * z,
        (y * y - z * z) * x, (z * z - x * x) * y, (x * x - y * y) * z,
    ]
    norms = (np.stack(rows) ** 2).sum(1)
    w = 1.0 / 0.6
    relax = np.array([0, 1.19, 1.4, 0, 1.2, 0, 1.2, 0, 1.2, w, 1.4, w, 1.4, w, w, w, 1.98, 1.98, 1.98])
    return [float(c) for c in relax / norms]


def collide(f):
    c = rates()
    s = {q: f[q] + f[q + 1] for q in range(1, 19, 2)}
    d = {q: f[q] - f[q + 1] for q in range(1, 19, 2)}
    a, b, g = s[7] + s[9], s[11] + s[13], s[15] + s[17]
    s1, s2 = s[1] + (s[3] + s[5]), a + b + g
    rho = f[0] + s1 + s2
    ax1, ax2 = d[7] + d[9], d[11] + d[13]
    ay1, ay2 = d[7] - d[9], d[15] + d[17]
    az1, az2 = d[11] - d[13], d[15] - d[17]
    ax, ay, az = ax1 + ax2, ay1 + ay2, az1 + az2
    jx, jy, jz = d[1] + ax, d[3] + ay, d[5] + az
    inv = 1.0 / rho
    ux, uy, uz = jx * inv, jy * inv, jz * inv
    xx, yy, zz = jx * ux, jy * uy, jz * uz
    jj = xx + yy + zz
    r1 = (19 * c[1]) * (s2 - f[0] - jj)
    r2 = c[2] * (9 * f[0] - 7 * s1 - 2 * s2 + 5.5 * jj)
    t1, t2, pe = 2 * s[1] - (s[3] + s[5]), a + b - 2 * g, 3 * xx - jj
    v1, v2, we = s[3] - s[5], a - b, yy - zz
    r9, r10 = c[9] * (t1 + t2 - pe), c[10] * (t2 - 2 * t1 + 0.5 * pe)
    r11, r12 = c[11] * (v1 + v2 - we), c[12] * (v2 - 2 * v1 + 0.5 * we)
    r13 = c[13] * (s[7] - s[9] - jx * uy)
    r14 = c[14] * (s[15] - s[17] - jy * uz)
    r15 = c[15] * (s[11] - s[13] - jx * uz)
    r4 = (c[4] * 5 / 3) * (ax - 2 * d[1])
    r6 = (c[6] * 5 / 3) * (ay - 2 * d[3])
    r8 = (c[8] * 5 / 3) * (az - 2 * d[5])
    r16, r17, r18 = c[16] * (ax1 - ax2), c[17] * (ay2 - ay1), c[18] * (az1 - az2)
    ea, eb = -11 * r1 - 4 * r2, 8 * r1 + r2
    a9, a11 = r9 - 2 * r10, r11 - 2 * r12
    b9, b11 = r9 + r10, r11 + r12
    exy, exz, eyz = eb + b9 + b11, eb + b9 - b11, eb - 2 * b9
    even = {
        1: ea + 2 * a9, 3: ea - a9 + a11, 5: ea - a9 - a11,
        7: exy + r13, 9: exy - r13, 11: exz + r15, 13: exz - r15, 15: eyz + r14, 17: eyz - r14,
    }
    odd = {
        1: -4 * r4, 3: -4 * r6, 5: -4 * r8,
        7: (r4 + r6) + (r16 - r17), 9: (r4 - r6) + (r16 + r17),
        11: (r4 + r8) - (r16 - r18), 13: (r4 - r8) - (r16 + r18),
        15: (r6 + r8) + (r17 - r18), 17: (r6 - r8) + (r17 + r18),
    }
    out = [f[0] + 30 * r1 - 12 * r2]
    for q in range(1, 19, 2):
        out += [f[q] - even[q] - odd[q], f[q + 1] - even[q] + odd[q]]
    return out


def feq(h):
    rho = h[0]
    for q in range(1, Q):
        rho = rho + h[q]
    safe = jnp.where(rho > 0, rho, 1.0)
    u = []
    for axis in range(3):
        m = None
        for q in range(Q):
            if VEL[q][axis]:
                t = h[q] if VEL[q][axis] > 0 else -h[q]
                m = t if m is None else m + t
        u.append(m / safe)
    sq = u[0] * u[0] + u[1] * u[1] + u[2] * u[2]
    out = {}
    for q in CROSSING[2]:
        p = None
        for axis in range(3):
            if VEL[q][axis]:
                t = u[axis] if VEL[q][axis] > 0 else -u[axis]
                p = t if p is None else p + t
        n = sum(abs(e) for e in VEL[q])
        w = 1.0 / 18.0 if n == 1 else 1.0 / 36.0
        out[q] = w * rho * (1.0 + 3.0 * p + 4.5 * p * p - 1.5 * sq)
    return out


def lanes(rows):
    l = lax.broadcasted_iota(I32, (rows, LANES), 1)
    return l >= 64, (l >> 3) & 7, l & 7


def split(x):
    hi = x.astype(BF16)
    lo = (x - hi.astype(F32)).astype(BF16)
    return jnp.concatenate([hi, lo], axis=0)


def dot(a, b):
    return jnp.dot(a, b, preferred_element_type=F32)


def select_rows(row, offset, count):
    r = lax.broadcasted_iota(I32, (count, row.shape[1]), 0)
    hot = jnp.where(r == row - offset, 1.0, 0.0).astype(BF16)
    return jnp.concatenate([hot, hot], axis=1)


def spread_rows(flags):
    n = flags.shape[1]
    eye = lax.broadcasted_iota(I32, (n, n), 0) == lax.broadcasted_iota(I32, (n, n), 1)
    diag = jnp.where(eye, flags.astype(F32), 0.0).astype(BF16)
    return dot(diag, jnp.ones((n, LANES), BF16))


def sources(q, t, tiles, outer, half):
    ex = VEL[q][0]
    if ex == 0:
        return tiles[t]
    n = t - ex
    other = tiles[n] if 0 <= n < len(tiles) else outer
    return jnp.where(half, other, tiles[t]) if ex > 0 else jnp.where(half, tiles[t], other)


def roll(x, by):
    by %= LANES
    return pltpu.roll(x, by, 1) if by else x


def edges(q, t, count, half, j, k):
    ex, ey, ez = VEL[q]
    cx = None
    if ex > 0 and t == 0:
        cx = jnp.logical_not(half)
    if ex < 0 and t == count - 1:
        cx = half
    cy = None if ey == 0 else (j == (0 if ey > 0 else 7))
    cz = None if ez == 0 else (k == (0 if ez > 0 else 7))
    return cx, cy, cz


def face_of(axis, e):
    return 2 * axis + (1 if e > 0 else 0)


def bounce_bits(t, solid, absent):
    half, j, k = lanes(solid[0].shape[0])
    acc = jnp.where(solid[t] != 0, 1, 0)
    for q in range(1, Q):
        ex, ey, ez = VEL[q]
        v = roll(sources(q, t, solid, solid[t], half), 64 * abs(ex) + 8 * ey + ez)
        sides = zip(edges(q, t, len(solid), half, j, k), (ex, ey, ez), range(3))
        crossed = [c for c in sides if c[0] is not None]
        for c, e, axis in crossed:
            v = jnp.where(c, absent[face_of(axis, e)], v)
        for i in range(len(crossed)):
            for m in range(i):
                v = jnp.where(crossed[i][0] & crossed[m][0], 1, v)
        acc = acc | (jnp.where(v != 0, 1, 0) << q)
    return acc


def absences(nbr_ref, ifc_ref):
    out = []
    for d in range(6):
        there = nbr_ref[d : d + 1, :] >= 0
        if d == 2:
            there = there | (ifc_ref[0:1, :] >= 0)
        out.append((1.0 - spread_rows(jnp.where(there, 1.0, 0.0))).astype(I32))
    return out


def local_hots(nbr_ref, first):
    n = nbr_ref.shape[1]
    return [select_rows(nbr_ref[(d ^ 1) : (d ^ 1) + 1, :], first, n) for d in range(6)]


def send_rows(row, first, count, cap):
    rel = row - first
    gone = (rel >= 0) & (rel < count)
    rel = jnp.where(gone, rel, 255)
    ahead = spread_rows(rel)[:, :count] < rel.astype(F32)
    rank = jnp.sum(jnp.where(ahead, 1.0, 0.0), axis=0, keepdims=True)
    r = lax.broadcasted_iota(I32, (cap, count), 0).astype(F32)
    hot = jnp.where((r == rank) & gone, 1.0, 0.0).astype(BF16)
    return jnp.concatenate([hot, hot], axis=1)


def take_rows(row, first, count, cap):
    rel = row - first
    gone = jnp.where((rel >= 0) & (rel < count), 1.0, 0.0)
    b = lax.broadcasted_iota(I32, (count, count), 0)
    a = lax.broadcasted_iota(I32, (count, count), 1)
    rank = dot(jnp.where(a < b, gone, 0.0).astype(BF16), jnp.ones((count, LANES), BF16))[:, :cap]
    there = spread_rows(gone)[:, :cap] > 0.5
    r = lax.broadcasted_iota(I32, (count, cap), 1).astype(F32)
    hot = jnp.where((r == rank) & there, 1.0, 0.0).astype(BF16)
    return jnp.concatenate([hot, hot], axis=1)


def coarse_code(ifc_ref, position, count):
    c = ifc_ref[0:1, :]
    code = jnp.where(c >= 0, 2 + 4 * (c - (position + 1) * count) + ifc_ref[1:2, :], 1)
    return spread_rows(code)


def pack_kernel(part_ref, co_ref, far_co_ref, send_ref):
    refs = (co_ref, far_co_ref)
    count = co_ref.shape[0]
    n = part_ref.shape[0]
    send_ref[:n] = part_ref[...]
    h = []
    for q in range(Q):
        h0 = jnp.concatenate([r[:, q, 0, :] for r in refs], axis=0)
        h1 = (1.0 - 0.5) * h0 + 0.5 * jnp.concatenate([r[:, q, 1, :] for r in refs], axis=0)
        h.append(jnp.concatenate([h0, h1], axis=1))
    e = feq(h)
    send_ref[n:] = jnp.zeros_like(send_ref[n:])
    for s, q in enumerate(CROSSING[2]):
        v = e[q] + (0.6 / 1.1) * (h[q] - e[q])
        for o in range(2):
            for c in range(count):
                send_ref[n + o, 5 * c + s : 5 * c + s + 1, :] = v[count * o + c : count * o + c + 1]


def both_halves(x, upper):
    half = lanes(x.shape[0])[0]
    return jnp.where(half, x, roll(x, 64)) if upper else jnp.where(half, roll(x, 64), x)


def spread_matrix(tiles):
    kk = lax.broadcasted_iota(I32, (256, LANES), 0)
    ll = lax.broadcasted_iota(I32, (256, LANES), 1)
    w, m, k = kk >> 6, kk & 63, ll & 7
    out = []
    for t in range(tiles + 1):
        i = (ll >> 6) * 7 if t == tiles else 2 * t + (ll >> 6)
        want = 8 * (4 * (w >> 1) + (i >> 1)) + 4 * (w & 1) + (k >> 1)
        out.append(jnp.where(m == want, 1.0, 0.0).astype(BF16))
    return out


def coarse_rows(code, cg, count):
    half = lanes(code.shape[0])[0]
    hi, lo = [], []
    for s in range(5):
        parts = []
        for pair in (0, 2):
            acc = jnp.zeros_like(code)
            for c in range(count):
                want = jnp.where(half, 3.0 + 4 * c + pair, 2.0 + 4 * c + pair)
                acc = jnp.where(code == want, cg[5 * c + s : 5 * c + s + 1, :], acc)
            parts.append(acc)
        x = jnp.concatenate(parts, axis=1)
        h = x.astype(BF16)
        hi.append(h)
        lo.append((x - h.astype(F32)).astype(BF16))
    return jnp.concatenate(hi + lo, axis=0)


def coarse_tile(rows, matrix):
    g = dot(rows, matrix)
    n = g.shape[0] // 2
    g = g[:n] + g[n:]
    b = n // 5
    return [g[b * s : b * (s + 1)] for s in range(5)]


def pull(q, t, x, parts, gx, bits, bounced, init):
    if q == 0:
        return jnp.where((bits & 1) != 0, init, x[t])
    half, j, k = lanes(bits.shape[0])
    ex, ey, ez = VEL[q]
    turn = 64 * abs(ex)
    out = roll(sources(q, t, x, gx, half), turn + 8 * ey + ez)
    _, cy, cz = edges(q, t, len(x), half, j, k)
    if ey:
        g = parts[1]
        out = jnp.where(cy, roll(sources(q, t, g, g[t], half), turn - 56 * ey + ez), out)
    if ez:
        g = parts[2]
        out = jnp.where(cz, roll(sources(q, t, g, g[t], half), turn + 8 * ey - 7 * ez), out)
    out = jnp.where((bits & (1 << q)) != 0, bounced, out)
    return jnp.where((bits & 1) != 0, init, out)


def gathers(q, x, hot, fine, remote):
    ex, ey, ez = VEL[q]
    gx, gy, gz = None, None, None
    if q:
        parts = [split(v) for v in x]
    if ex:
        gx = dot(hot[face_of(0, ex)], parts[0 if ex < 0 else len(x) - 1])
        if remote is not None:
            gx = gx + remote[q]
    if ey:
        gy = [dot(hot[face_of(1, ey)], p) for p in parts]
        if ey < 0 and fine is not None:
            s = CROSSING[2].index(q)
            gy = [g + fine(s, t) for t, g in enumerate(gy)]
    if ez:
        gz = [dot(hot[face_of(2, ez)], p) for p in parts]
    return gx, gy, gz


def side_slots(d):
    e = 1 if d == 0 else -1
    return [q for q in range(Q) if VEL[q][0] == e], [q for q in range(Q) if VEL[q][0] != -e]


def prepare_side(side, load, nbr_ref, solid, bits_put, post_ref, send_ref, hot, absent, code, first, ready=None):
    tiles = len(solid)
    blocks = solid[0].shape[0]
    t = tiles - 1 if side == 0 else 0
    half, j, k = lanes(blocks)
    bits = bounce_bits(t, solid, absent)
    bits_put(t, bits)
    if ready is not None:
        ready()

    def step(g, carry):
        r = pl.ds(pl.multiple_of(8 * g, 8), 8)
        out = collide([load(q, r, t) for q in range(Q)])
        for q in range(Q):
            post_ref[side, q, r, :] = out[q]
        return carry

    lax.fori_loop(0, blocks // 8, step, 0)
    to = send_rows(nbr_ref[side : side + 1, :], first + (blocks if side == 0 else -blocks), blocks, send_ref.shape[1])
    face, layer = side_slots(side)
    slots = [post_ref[side, q] for q in face]
    for q in layer:
        ex, ey, ez = VEL[q]
        x = post_ref[side, q]
        turn = 64 * abs(ex)
        out = roll(x, turn + 8 * ey + ez)
        _, cy, cz = edges(q, t, tiles, half, j, k)
        if ey or ez:
            parts = split(x)
        if ey:
            out = jnp.where(cy, roll(dot(hot[face_of(1, ey)], parts), turn - 56 * ey + ez), out)
        if ez:
            out = jnp.where(cz, roll(dot(hot[face_of(2, ez)], parts), turn + 8 * ey - 7 * ez), out)
        if q:
            out = jnp.where((bits & (1 << q)) != 0, post_ref[side, OPP[q]], out)
        slots.append(out)
    slots.append(code)
    for s in range(0, len(slots), 2):
        a, b = slots[s], slots[s + 1]
        packed = jnp.where(half, b, roll(a, 64)) if side == 0 else jnp.where(half, roll(b, 64), a)
        send_ref[s // 2] = dot(to, split(packed))


def outer_kernel(pop_hbm, *refs):
    given, (post_ref, bits_ref, co_ref, send_ref), (tile_ref, *small_refs, sem) = refs[:4], refs[4:8], refs[8:]
    nbr_ref, ifc_ref, solid_ref = small_refs
    position = lax.axis_index("blk")
    blocks = solid_ref.shape[0]
    tiles = solid_ref.shape[1] // LANES
    even = position % 2 == 0
    mine = pl.ds(pl.multiple_of(jnp.where(even, 0, LANES * (tiles - 1)), LANES), LANES)
    pairs = [(pop_hbm.at[:, :, mine], tile_ref), *zip(given, (*small_refs, co_ref))]
    copies = [pltpu.make_async_copy(a, b, sem.at[i]) for i, (a, b) in enumerate(pairs)]
    for copy in copies[1:] + copies[:1]:
        copy.start()
    for copy in copies[1:]:
        copy.wait()
    first = position * blocks
    code = coarse_code(ifc_ref, position, co_ref.shape[0])
    absent = absences(nbr_ref, ifc_ref)
    hot = local_hots(nbr_ref, first)
    solid = [solid_ref[:, LANES * t : LANES * (t + 1)] for t in range(tiles)]

    def load(q, r, t):
        return tile_ref[q, r, :]

    def put(t, bits):
        bits_ref[...] = bits

    for side in (0, 1):

        @pl.when(position % 2 == 1 - side)
        def _(side=side):
            prepare_side(side, load, nbr_ref, solid, put, post_ref, send_ref, hot, absent, code, first, copies[0].wait)


def inner_kernel(pop_ref, nbr_ref, ifc_ref, solid_ref, ahead_ref, abits_ref, cur_ref, outer_ref, bits_ref, code_ref, spread_ref, take_ref, send_ref, mid_ref, *, count):
    position = lax.axis_index("blk")
    blocks = solid_ref.shape[0]
    tiles = solid_ref.shape[1] // LANES
    first = position * blocks
    groups = blocks // 8
    span = [slice(LANES * t, LANES * (t + 1)) for t in range(tiles)]
    code = coarse_code(ifc_ref, position, count)
    code_ref[...] = code
    absent = absences(nbr_ref, ifc_ref)
    hot = local_hots(nbr_ref, first)
    solid = [solid_ref[:, span[t]] for t in range(tiles)]

    def load(q, r, t):
        return pop_ref[q, r, span[t]]

    def put(t, bits):
        bits_ref[:, span[t]] = bits

    for side in (0, 1):

        @pl.when(position % 2 == side)
        def _(side=side):
            prepare_side(side, load, nbr_ref, solid, put, outer_ref, send_ref, hot, absent, code, first)
            outer_ref[1 - side] = ahead_ref[1 - side]
            put(0 if side == 0 else tiles - 1, abits_ref[...])

    def step(i, carry):
        n, g = i // groups, i % groups
        r = pl.ds(pl.multiple_of(8 * g, 8), 8)
        l = pl.ds(pl.multiple_of(LANES * (n + 1), LANES), LANES)
        out = collide([pop_ref[q, r, l] for q in range(Q)])
        for q in range(Q):
            mid_ref[n, q, r, :] = out[q]
        return carry

    lax.fori_loop(0, groups * (tiles - 2), step, 0)
    for t, m in enumerate(spread_matrix(tiles)):
        spread_ref[t] = m
    cap = take_ref.shape[2] // 2
    take_ref[0] = take_rows(nbr_ref[0:1, :], first + blocks, blocks, cap)
    take_ref[1] = take_rows(nbr_ref[1:2, :], first - blocks, blocks, cap)
    for t in range(1, tiles - 1):
        put(t, bounce_bits(t, solid, absent))

    def post(q, t):
        if t == 0:
            return outer_ref[1, q]
        return outer_ref[0, q] if t == tiles - 1 else mid_ref[t - 1, q]

    for q in range(Q):
        x = [post(q, t) for t in range(tiles)]
        ghosts = gathers(q, x, hot, None, None)
        for t in range(tiles):
            cur_ref[q, :, span[t]] = pull(
                q, t, x, ghosts, ghosts[0], bits_ref[:, span[t]], post(OPP[q], t), pop_ref[q, :, span[t]]
            )


def current_kernel(cur_ref, outer_ref, code_ref, spread_ref, take_ref, sb_ref, ra_ref, rb_ref, now_ref, post_ref, fine_ref, ghost_ref, codes_ref, got_ref, *, count):
    position = lax.axis_index("blk")
    blocks, cells = cur_ref.shape[1:]
    tiles = cells // LANES
    even = position % 2 == 0
    half, j, k = lanes(blocks)
    span = [slice(LANES * t, LANES * (t + 1)) for t in range(tiles)]
    n = ra_ref.shape[0]

    for s in range(n):
        got_ref[0, s] = dot(take_ref[0], split(jnp.where(even, ra_ref[s], rb_ref[s])))
        got_ref[1, s] = dot(take_ref[1], split(jnp.where(even, rb_ref[s], ra_ref[s])))

    def from_next(s):
        return got_ref[0, s // 2] if s % 2 == 0 else roll(got_ref[0, s // 2], 64)

    def from_prev(s):
        return got_ref[1, s // 2] if s % 2 == 1 else roll(got_ref[1, s // 2], 64)

    up_face, up_layer = side_slots(1)
    low_face, low_layer = side_slots(0)
    up = {q: from_next(s) for s, q in enumerate(up_face)}
    low = {q: from_prev(s) for s, q in enumerate(low_face)}
    code = code_ref[...]
    up_code = both_halves(from_next(2 * n - 1), False)
    low_code = both_halves(from_prev(2 * n - 1), True)
    codes_ref[0] = up_code
    codes_ref[1] = low_code
    near = jnp.where(even, sb_ref[n + 1], rb_ref[n])

    rows = coarse_rows(code, both_halves(near, False), count)
    for t in range(tiles):
        for s, v in enumerate(coarse_tile(rows, spread_ref[t])):
            fine_ref[s, :, span[t]] = v
    for q in range(Q):
        ex, ey, ez = VEL[q]
        for t in range(tiles):
            v = cur_ref[q, :, span[t]]
            cx, cy, cz = edges(q, t, tiles, half, j, k)
            if ey < 0:
                f = [fine_ref[CROSSING[2].index(q), :, span[m]] for m in range(tiles)]
                g = roll(sources(q, t, f, f[t], half), 64 * abs(ex) - 56 * ey + ez)
                ok = cy
                if cx is not None:
                    ok = ok & jnp.logical_not(cx)
                if cz is not None:
                    ok = ok & jnp.logical_not(cz)
                v = v + jnp.where(ok, g, 0.0)
            if cx is not None:
                ok = cx
                for c in (cy, cz):
                    if c is not None:
                        ok = ok & jnp.logical_not(c)
                v = v + jnp.where(ok, roll(up[q] if ex < 0 else low[q], 64 + 8 * ey + ez), 0.0)
            now_ref[q, :, span[t]] = v

    low_rows = coarse_rows(low_code, both_halves(sb_ref[n], False), count)
    low_fine = coarse_tile(low_rows, spread_ref[tiles])
    for q in range(Q):
        ex, ey, ez = VEL[q]
        _, cy, cz = edges(q, 0, tiles, half, j, k)
        corner = cy if cz is None else (cz if cy is None else cy | cz)
        sides = []
        for e, layer, face, take, mine in (
            (-1, up_layer, up, from_next, outer_ref.at[0]),
            (1, low_layer, low, from_prev, outer_ref.at[1]),
        ):
            if ex == -e:
                v = roll(mine[q], 64 + 8 * ey + ez)
                if corner is not None:
                    v = jnp.where(corner, face[OPP[q]], v)
            else:
                v = take(5 + layer.index(q))
                if ey < 0 and e > 0:
                    ok = cy if cz is None else cy & jnp.logical_not(cz)
                    v = v + jnp.where(ok, roll(low_fine[CROSSING[2].index(q)], ez), 0.0)
            sides.append(v)
        ghost_ref[q] = jnp.where(half, sides[1], sides[0])

    def step(i, carry):
        r = pl.ds(pl.multiple_of(8 * (i // tiles), 8), 8)
        l = pl.ds(pl.multiple_of(LANES * (i % tiles), LANES), LANES)
        out = collide([now_ref[q, r, l] for q in range(Q)])
        for q in range(Q):
            post_ref[q, r, l] = out[q]
        return carry

    lax.fori_loop(0, blocks // 8 * tiles, step, 0)

    rows = coarse_rows(code, both_halves(near, True), count)
    for t in range(tiles):
        for s, v in enumerate(coarse_tile(rows, spread_ref[t])):
            fine_ref[s, :, span[t]] = v


def final_kernel(now_ref, post_ref, fine_ref, half_ref, codes_ref, bits_ref, spread_ref, rb_ref, relay_ref, nbr_ref, out_ref, buf_ref, ghost_ref, sem, *, count):
    position = lax.axis_index("blk")
    blocks, cells = bits_ref.shape
    tiles = cells // LANES
    first = position * blocks
    half, j, k = lanes(blocks)
    span = [slice(LANES * t, LANES * (t + 1)) for t in range(tiles)]
    hot = local_hots(nbr_ref, first)
    copies = []

    def emit(q, remote):
        x = [post_ref[q, :, span[t]] for t in range(tiles)]
        ghosts = gathers(q, x, hot, lambda s, t: fine_ref[s, :, span[t]], remote)
        for t in range(tiles):
            buf_ref[q, :, span[t]] = pull(
                q, t, x, ghosts, ghosts[0], bits_ref[:, span[t]], post_ref[OPP[q], :, span[t]], now_ref[q, :, span[t]]
            )
        copy = pltpu.make_async_copy(buf_ref.at[q], out_ref.at[q], sem.at[q])
        copy.start()
        copies.append(copy)

    for q in range(Q):
        if VEL[q][0] == 0:
            emit(q, None)
    n = rb_ref.shape[0] - 2
    far = jnp.where(position % 2 == 0, relay_ref[n], rb_ref[n + 1])
    up_rows = coarse_rows(codes_ref[0], both_halves(far, False), count)
    up_fine = coarse_tile(up_rows, spread_ref[tiles])
    for q in range(Q):
        v = half_ref[q]
        if VEL[q][1] < 0 and VEL[q][0] <= 0:
            _, cy, cz = edges(q, 0, tiles, half, j, k)
            ok = cy & jnp.logical_not(half)
            if cz is not None:
                ok = ok & jnp.logical_not(cz)
            v = v + jnp.where(ok, roll(up_fine[CROSSING[2].index(q)], VEL[q][2]), 0.0)
        ghost_ref[q] = v

    def layer_step(g, carry):
        r = pl.ds(pl.multiple_of(8 * g, 8), 8)
        out = collide([ghost_ref[q, r, :] for q in range(Q)])
        for q in range(Q):
            if VEL[q][0]:
                ghost_ref[q, r, :] = out[q]
        return carry

    lax.fori_loop(0, blocks // 8, layer_step, 0)
    remote = {}
    for q in range(Q):
        if VEL[q][0]:
            there = codes_ref[0 if VEL[q][0] < 0 else 1] > 0.5
            remote[q] = jnp.where(there, ghost_ref[q], 0.0)
    for q in range(Q):
        if VEL[q][0]:
            emit(q, remote)
    for copy in copies:
        copy.wait()


def swapped(x, off):
    n = lax.axis_size("blk")
    low = [(i, i + 1) for i in range(off, n - 1, 2)]
    return lax.ppermute(x, "blk", low + [(b, a) for a, b in low])


def held(x):
    return pltpu.with_memory_space_constraint(x, pltpu.VMEM)


def body(populations, coarse_faces, neighbors, interface, solid):
    pop = populations.transpose(1, 0, 2)
    co = coarse_faces.transpose(0, 2, 1, 3)
    nbr, ifc = neighbors.T, interface.T
    blocks, cells = pop.shape[1:]
    count = co.shape[0]
    tiles = cells // LANES
    dense = pl.BlockSpec(memory_space=pltpu.VMEM)
    away = pl.BlockSpec(memory_space=pl.ANY)
    cap = blocks // 2
    room = pltpu.CompilerParams(vmem_limit_bytes=20 << 20)
    sides = pltpu.VMEM((2, Q, blocks, LANES), F32)
    payload = pltpu.VMEM((10, cap, LANES), F32)
    small = (nbr, ifc, solid)
    far_co = swapped(co, 0)
    outer = pl.pallas_call(
        outer_kernel,
        in_specs=[away] * 5,
        out_shape=(sides, pltpu.VMEM((blocks, LANES), I32), pltpu.VMEM(co.shape, F32), payload),
        scratch_shapes=[
            pltpu.VMEM((Q, blocks, LANES), F32),
            *(pltpu.VMEM(a.shape, a.dtype) for a in small),
            pltpu.SemaphoreType.DMA((5,)),
        ],
        compiler_params=pltpu.CompilerParams(vmem_limit_bytes=56 << 20),
        cost_estimate=pl.CostEstimate(flops=20_000_000, bytes_accessed=1_000_000, transcendentals=0),
        name="outer",
    )
    ahead, abits, co, part = outer(pop, *small, co)
    sb = pl.pallas_call(
        pack_kernel,
        in_specs=[dense] * 3,
        out_shape=pltpu.VMEM((12, cap, LANES), F32),
        compiler_params=room,
        name="pack",
    )(held(part), held(co), held(far_co))
    rb = swapped(sb, 1)
    pop, nbr, ifc, solid, ahead = lax.optimization_barrier((pop, nbr, ifc, solid, ahead))
    ahead, abits = held(ahead), held(abits)
    inner = pl.pallas_call(
        functools.partial(inner_kernel, count=count),
        in_specs=[dense] * 6,
        out_shape=(
            pltpu.VMEM((Q, blocks, cells), F32),
            sides,
            pltpu.VMEM((blocks, cells), I32),
            pltpu.VMEM((blocks, LANES), F32),
            pltpu.VMEM((tiles + 1, 256, LANES), BF16),
            pltpu.VMEM((2, blocks, 2 * cap), BF16),
            payload,
        ),
        scratch_shapes=[pltpu.VMEM((tiles - 2, Q, blocks, LANES), F32)],
        compiler_params=room,
        cost_estimate=pl.CostEstimate(flops=100_000_000, bytes_accessed=4_000_000, transcendentals=0),
        name="inner",
    )
    cur, outer, bits, code, spread, take, sa = inner(pop, nbr, ifc, solid, ahead, abits)
    ra = swapped(sa, 0)
    relay = swapped(rb, 0)
    state = pltpu.VMEM((Q, blocks, cells), F32)
    layer = pltpu.VMEM((Q, blocks, LANES), F32)
    current = pl.pallas_call(
        functools.partial(current_kernel, count=count),
        in_specs=[dense] * 8,
        out_shape=(state, state, pltpu.VMEM((5, blocks, cells), F32), layer, pltpu.VMEM((2, blocks, LANES), F32)),
        scratch_shapes=[pltpu.VMEM((2, 10, blocks, LANES), F32)],
        compiler_params=room,
        cost_estimate=pl.CostEstimate(flops=100_000_000, bytes_accessed=4_000_000, transcendentals=0),
        name="current",
    )
    given = [held(x) for x in (cur, outer, code, spread, take, sb, ra, rb)]
    now, post, fine, ghost, codes = current(*given)
    out = pl.pallas_call(
        functools.partial(final_kernel, count=count),
        in_specs=[dense] * 10,
        out_specs=away,
        out_shape=jax.ShapeDtypeStruct(pop.shape, F32),
        scratch_shapes=[state, layer, pltpu.SemaphoreType.DMA((Q,))],
        compiler_params=room,
        name="final",
    )(*(held(x) for x in (now, post, fine, ghost, codes, bits, spread, rb, relay)), nbr)
    return out.transpose(1, 0, 2)


def solution(mesh):
    placed = (P("blk", None, None), P("blk", None, None, None), P("blk", None), P("blk", None), P("blk", None))
    return jax.shard_map(body, mesh=mesh, in_specs=placed, out_specs=P("blk", None, None), check_vma=False)
```

```python
import functools

import jax
import jax.numpy as jnp
import numpy as np
from jax import lax
from jax.experimental import pallas as pl
from jax.experimental.pallas import tpu as pltpu
from jax.sharding import PartitionSpec as P


F32, BF16, I32 = jnp.float32, jnp.bfloat16, jnp.int32
LANES = 128
VEL = [
    (0, 0, 0),
    (1, 0, 0), (-1, 0, 0), (0, 1, 0), (0, -1, 0), (0, 0, 1), (0, 0, -1),
    (1, 1, 0), (-1, -1, 0), (1, -1, 0), (-1, 1, 0),
    (1, 0, 1), (-1, 0, -1), (1, 0, -1), (-1, 0, 1),
    (0, 1, 1), (0, -1, -1), (0, 1, -1), (0, -1, 1),
]
Q = len(VEL)
OPP = [VEL.index((-x, -y, -z)) for x, y, z in VEL]
CROSSING = [
    [q for q in range(Q) if VEL[q][d // 2] == (-1 if d % 2 == 0 else 1)] for d in range(6)
]


def rates():
    v = np.array(VEL) * 1.0
    x, y, z = v[:, 0], v[:, 1], v[:, 2]
    s = x * x + y * y + z * z
    rows = [
        np.ones(19), 19 * s - 30, (21 * s * s - 53 * s + 24) / 2,
        x, (5 * s - 9) * x, y, (5 * s - 9) * y, z, (5 * s - 9) * z,
        3 * x * x - s, (3 * s - 5) * (3 * x * x - s),
        y * y - z * z, (3 * s - 5) * (y * y - z * z),
        x * y, y * z, x * z,
        (y * y - z * z) * x, (z * z - x * x) * y, (x * x - y * y) * z,
    ]
    norms = (np.stack(rows) ** 2).sum(1)
    w = 1.0 / 0.6
    relax = np.array([0, 1.19, 1.4, 0, 1.2, 0, 1.2, 0, 1.2, w, 1.4, w, 1.4, w, w, w, 1.98, 1.98, 1.98])
    return [float(c) for c in relax / norms]


def collide(f):
    c = rates()
    s = {q: f[q] + f[q + 1] for q in range(1, 19, 2)}
    d = {q: f[q] - f[q + 1] for q in range(1, 19, 2)}
    a, b, g = s[7] + s[9], s[11] + s[13], s[15] + s[17]
    s1, s2 = s[1] + (s[3] + s[5]), a + b + g
    rho = f[0] + s1 + s2
    ax1, ax2 = d[7] + d[9], d[11] + d[13]
    ay1, ay2 = d[7] - d[9], d[15] + d[17]
    az1, az2 = d[11] - d[13], d[15] - d[17]
    ax, ay, az = ax1 + ax2, ay1 + ay2, az1 + az2
    jx, jy, jz = d[1] + ax, d[3] + ay, d[5] + az
    inv = 1.0 / rho
    ux, uy, uz = jx * inv, jy * inv, jz * inv
    xx, yy, zz = jx * ux, jy * uy, jz * uz
    jj = xx + yy + zz
    r1 = (19 * c[1]) * (s2 - f[0] - jj)
    r2 = c[2] * (9 * f[0] - 7 * s1 - 2 * s2 + 5.5 * jj)
    t1, t2, pe = 2 * s[1] - (s[3] + s[5]), a + b - 2 * g, 3 * xx - jj
    v1, v2, we = s[3] - s[5], a - b, yy - zz
    r9, r10 = c[9] * (t1 + t2 - pe), c[10] * (t2 - 2 * t1 + 0.5 * pe)
    r11, r12 = c[11] * (v1 + v2 - we), c[12] * (v2 - 2 * v1 + 0.5 * we)
    r13 = c[13] * (s[7] - s[9] - jx * uy)
    r14 = c[14] * (s[15] - s[17] - jy * uz)
    r15 = c[15] * (s[11] - s[13] - jx * uz)
    r4 = (c[4] * 5 / 3) * (ax - 2 * d[1])
    r6 = (c[6] * 5 / 3) * (ay - 2 * d[3])
    r8 = (c[8] * 5 / 3) * (az - 2 * d[5])
    r16, r17, r18 = c[16] * (ax1 - ax2), c[17] * (ay2 - ay1), c[18] * (az1 - az2)
    ea, eb = -11 * r1 - 4 * r2, 8 * r1 + r2
    a9, a11 = r9 - 2 * r10, r11 - 2 * r12
    b9, b11 = r9 + r10, r11 + r12
    exy, exz, eyz = eb + b9 + b11, eb + b9 - b11, eb - 2 * b9
    even = {
        1: ea + 2 * a9, 3: ea - a9 + a11, 5: ea - a9 - a11,
        7: exy + r13, 9: exy - r13, 11: exz + r15, 13: exz - r15, 15: eyz + r14, 17: eyz - r14,
    }
    odd = {
        1: -4 * r4, 3: -4 * r6, 5: -4 * r8,
        7: (r4 + r6) + (r16 - r17), 9: (r4 - r6) + (r16 + r17),
        11: (r4 + r8) - (r16 - r18), 13: (r4 - r8) - (r16 + r18),
        15: (r6 + r8) + (r17 - r18), 17: (r6 - r8) + (r17 + r18),
    }
    out = [f[0] + 30 * r1 - 12 * r2]
    for q in range(1, 19, 2):
        out += [f[q] - even[q] - odd[q], f[q + 1] - even[q] + odd[q]]
    return out


def feq(h):
    rho = h[0]
    for q in range(1, Q):
        rho = rho + h[q]
    safe = jnp.where(rho > 0, rho, 1.0)
    u = []
    for axis in range(3):
        m = None
        for q in range(Q):
            if VEL[q][axis]:
                t = h[q] if VEL[q][axis] > 0 else -h[q]
                m = t if m is None else m + t
        u.append(m / safe)
    sq = u[0] * u[0] + u[1] * u[1] + u[2] * u[2]
    out = {}
    for q in CROSSING[2]:
        p = None
        for axis in range(3):
            if VEL[q][axis]:
                t = u[axis] if VEL[q][axis] > 0 else -u[axis]
                p = t if p is None else p + t
        n = sum(abs(e) for e in VEL[q])
        w = 1.0 / 18.0 if n == 1 else 1.0 / 36.0
        out[q] = w * rho * (1.0 + 3.0 * p + 4.5 * p * p - 1.5 * sq)
    return out


def lanes(rows):
    l = lax.broadcasted_iota(I32, (rows, LANES), 1)
    return l >= 64, (l >> 3) & 7, l & 7


def split(x):
    hi = x.astype(BF16)
    lo = (x - hi.astype(F32)).astype(BF16)
    return jnp.concatenate([hi, lo], axis=0)


def dot(a, b):
    return jnp.dot(a, b, preferred_element_type=F32)


def select_rows(row, offset, count):
    r = lax.broadcasted_iota(I32, (count, row.shape[1]), 0)
    hot = jnp.where(r == row - offset, 1.0, 0.0).astype(BF16)
    return jnp.concatenate([hot, hot], axis=1)


def spread_rows(flags):
    n = flags.shape[1]
    eye = lax.broadcasted_iota(I32, (n, n), 0) == lax.broadcasted_iota(I32, (n, n), 1)
    diag = jnp.where(eye, flags.astype(F32), 0.0).astype(BF16)
    return dot(diag, jnp.ones((n, LANES), BF16))


def sources(q, t, tiles, outer, half):
    ex = VEL[q][0]
    if ex == 0:
        return tiles[t]
    n = t - ex
    other = tiles[n] if 0 <= n < len(tiles) else outer
    return jnp.where(half, other, tiles[t]) if ex > 0 else jnp.where(half, tiles[t], other)


def roll(x, by):
    by %= LANES
    return pltpu.roll(x, by, 1) if by else x


def edges(q, t, count, half, j, k):
    ex, ey, ez = VEL[q]
    cx = None
    if ex > 0 and t == 0:
        cx = jnp.logical_not(half)
    if ex < 0 and t == count - 1:
        cx = half
    cy = None if ey == 0 else (j == (0 if ey > 0 else 7))
    cz = None if ez == 0 else (k == (0 if ez > 0 else 7))
    return cx, cy, cz


def face_of(axis, e):
    return 2 * axis + (1 if e > 0 else 0)


def bounce_bits(t, solid, absent):
    half, j, k = lanes(solid[0].shape[0])
    acc = jnp.where(solid[t] != 0, 1, 0)
    for q in range(1, Q):
        ex, ey, ez = VEL[q]
        v = roll(sources(q, t, solid, solid[t], half), 64 * abs(ex) + 8 * ey + ez)
        sides = zip(edges(q, t, len(solid), half, j, k), (ex, ey, ez), range(3))
        crossed = [c for c in sides if c[0] is not None]
        for c, e, axis in crossed:
            v = jnp.where(c, absent[face_of(axis, e)], v)
        for i in range(len(crossed)):
            for m in range(i):
                v = jnp.where(crossed[i][0] & crossed[m][0], 1, v)
        acc = acc | (jnp.where(v != 0, 1, 0) << q)
    return acc


def absences(nbr_ref, ifc_ref):
    out = []
    for d in range(6):
        there = nbr_ref[d : d + 1, :] >= 0
        if d == 2:
            there = there | (ifc_ref[0:1, :] >= 0)
        out.append((1.0 - spread_rows(jnp.where(there, 1.0, 0.0))).astype(I32))
    return out


def local_hots(nbr_ref, first):
    n = nbr_ref.shape[1]
    return [select_rows(nbr_ref[(d ^ 1) : (d ^ 1) + 1, :], first, n) for d in range(6)]


def send_rows(row, first, count, cap):
    rel = row - first
    gone = (rel >= 0) & (rel < count)
    rel = jnp.where(gone, rel, 255)
    ahead = spread_rows(rel)[:, :count] < rel.astype(F32)
    rank = jnp.sum(jnp.where(ahead, 1.0, 0.0), axis=0, keepdims=True)
    r = lax.broadcasted_iota(I32, (cap, count), 0).astype(F32)
    hot = jnp.where((r == rank) & gone, 1.0, 0.0).astype(BF16)
    return jnp.concatenate([hot, hot], axis=1)


def take_rows(row, first, count, cap):
    rel = row - first
    gone = jnp.where((rel >= 0) & (rel < count), 1.0, 0.0)
    b = lax.broadcasted_iota(I32, (count, count), 0)
    a = lax.broadcasted_iota(I32, (count, count), 1)
    rank = dot(jnp.where(a < b, gone, 0.0).astype(BF16), jnp.ones((count, LANES), BF16))[:, :cap]
    there = spread_rows(gone)[:, :cap] > 0.5
    r = lax.broadcasted_iota(I32, (count, cap), 1).astype(F32)
    hot = jnp.where((r == rank) & there, 1.0, 0.0).astype(BF16)
    return jnp.concatenate([hot, hot], axis=1)


def coarse_code(ifc_ref, position, count):
    c = ifc_ref[0:1, :]
    code = jnp.where(c >= 0, 2 + 4 * (c - (position + 1) * count) + ifc_ref[1:2, :], 1)
    return spread_rows(code)


def far_row(c, s, count):
    return 5 * count + 5 * (c // 2) + s


def pack_kernel(part_ref, co_ref, far_co_ref, send_ref, near_ref):
    refs = (co_ref, far_co_ref)
    count = co_ref.shape[0]
    n = part_ref.shape[0]
    send_ref[:n] = part_ref[...]
    h = []
    for q in range(Q):
        h0 = jnp.concatenate([r[:, q, 0, :] for r in refs], axis=0)
        h1 = (1.0 - 0.5) * h0 + 0.5 * jnp.concatenate([r[:, q, 1, :] for r in refs], axis=0)
        h.append(jnp.concatenate([h0, h1], axis=1))
    e = feq(h)
    send_ref[n] = jnp.zeros_like(send_ref[n])
    near_ref[...] = jnp.zeros_like(near_ref)
    upper = lanes(1)[0]
    for s, q in enumerate(CROSSING[2]):
        v = e[q] + (0.6 / 1.1) * (h[q] - e[q])
        for c in range(count):
            send_ref[n, 5 * c + s : 5 * c + s + 1, :] = v[c : c + 1]
            near_ref[5 * c + s : 5 * c + s + 1, :] = v[count + c : count + c + 1]
        turned = roll(v, 64)
        for c in range(0, count, 2):
            other = min(c + 1, count - 1)
            to = far_row(c, s, count)
            send_ref[n, to : to + 1, :] = jnp.where(upper, turned[count + other : count + other + 1], v[count + c : count + c + 1])


def both_halves(x, upper):
    half = lanes(x.shape[0])[0]
    return jnp.where(half, x, roll(x, 64)) if upper else jnp.where(half, roll(x, 64), x)


def spread_matrix(tiles):
    kk = lax.broadcasted_iota(I32, (256, LANES), 0)
    ll = lax.broadcasted_iota(I32, (256, LANES), 1)
    w, m, k = kk >> 6, kk & 63, ll & 7
    out = []
    for t in range(tiles + 1):
        i = (ll >> 6) * 7 if t == tiles else 2 * t + (ll >> 6)
        want = 8 * (4 * (w >> 1) + (i >> 1)) + 4 * (w & 1) + (k >> 1)
        out.append(jnp.where(m == want, 1.0, 0.0).astype(BF16))
    return out


def rows_of(cg):
    return lambda c, s: cg[5 * c + s : 5 * c + s + 1, :]


def coarse_rows(code, cg, count):
    half = lanes(code.shape[0])[0]
    hi, lo = [], []
    for s in range(5):
        parts = []
        for pair in (0, 2):
            acc = jnp.zeros_like(code)
            for c in range(count):
                want = jnp.where(half, 3.0 + 4 * c + pair, 2.0 + 4 * c + pair)
                acc = jnp.where(code == want, cg(c, s), acc)
            parts.append(acc)
        x = jnp.concatenate(parts, axis=1)
        h = x.astype(BF16)
        hi.append(h)
        lo.append((x - h.astype(F32)).astype(BF16))
    return jnp.concatenate(hi + lo, axis=0)


def coarse_tile(rows, matrix):
    g = dot(rows, matrix)
    n = g.shape[0] // 2
    g = g[:n] + g[n:]
    b = n // 5
    return [g[b * s : b * (s + 1)] for s in range(5)]


def pull(q, t, x, parts, gx, bits, bounced, init):
    if q == 0:
        return jnp.where((bits & 1) != 0, init, x[t])
    half, j, k = lanes(bits.shape[0])
    ex, ey, ez = VEL[q]
    turn = 64 * abs(ex)
    out = roll(sources(q, t, x, gx, half), turn + 8 * ey + ez)
    _, cy, cz = edges(q, t, len(x), half, j, k)
    if ey:
        g = parts[1]
        out = jnp.where(cy, roll(sources(q, t, g, g[t], half), turn - 56 * ey + ez), out)
    if ez:
        g = parts[2]
        out = jnp.where(cz, roll(sources(q, t, g, g[t], half), turn + 8 * ey - 7 * ez), out)
    out = jnp.where((bits & (1 << q)) != 0, bounced, out)
    return jnp.where((bits & 1) != 0, init, out)


def gathers(q, x, hot, fine, remote):
    ex, ey, ez = VEL[q]
    gx, gy, gz = None, None, None
    if q:
        parts = [split(v) for v in x]
    if ex:
        gx = dot(hot[face_of(0, ex)], parts[0 if ex < 0 else len(x) - 1])
        if remote is not None:
            gx = gx + remote[q]
    if ey:
        gy = [dot(hot[face_of(1, ey)], p) for p in parts]
        if ey < 0 and fine is not None:
            s = CROSSING[2].index(q)
            gy = [g + fine(s, t) for t, g in enumerate(gy)]
    if ez:
        gz = [dot(hot[face_of(2, ez)], p) for p in parts]
    return gx, gy, gz


def side_slots(d):
    e = 1 if d == 0 else -1
    return [q for q in range(Q) if VEL[q][0] == e], [q for q in range(Q) if VEL[q][0] != -e]


def groups(blocks):
    return [slice(g, g + 8) for g in range(0, blocks, 8)]


def prepare_side(side, load, nbr_ref, solid, bits_put, post_ref, send_ref, hot, absent, code, first, ready=None):
    tiles = len(solid)
    blocks = solid[0].shape[0]
    t = tiles - 1 if side == 0 else 0
    half, j, k = lanes(blocks)
    bits = bounce_bits(t, solid, absent)
    bits_put(t, bits)
    if ready is not None:
        ready()

    for r in groups(blocks):
        out = collide([load(q, r, t) for q in range(Q)])
        for q in range(Q):
            post_ref[side, q, r, :] = out[q]
    to = send_rows(nbr_ref[side : side + 1, :], first + (blocks if side == 0 else -blocks), blocks, send_ref.shape[1])
    face, layer = side_slots(side)
    slots = [post_ref[side, q] for q in face]
    for q in layer:
        ex, ey, ez = VEL[q]
        x = post_ref[side, q]
        turn = 64 * abs(ex)
        out = roll(x, turn + 8 * ey + ez)
        _, cy, cz = edges(q, t, tiles, half, j, k)
        if ey or ez:
            parts = split(x)
        if ey:
            out = jnp.where(cy, roll(dot(hot[face_of(1, ey)], parts), turn - 56 * ey + ez), out)
        if ez:
            out = jnp.where(cz, roll(dot(hot[face_of(2, ez)], parts), turn + 8 * ey - 7 * ez), out)
        if q:
            out = jnp.where((bits & (1 << q)) != 0, post_ref[side, OPP[q]], out)
        slots.append(out)
    slots.append(code)
    for s in range(0, len(slots), 2):
        a, b = slots[s], slots[s + 1]
        packed = jnp.where(half, b, roll(a, 64)) if side == 0 else jnp.where(half, roll(b, 64), a)
        send_ref[s // 2] = dot(to, split(packed))


def outer_kernel(pop_hbm, *refs):
    given, (post_ref, bits_ref, co_ref, send_ref), (tile_ref, *small_refs, sem) = refs[:4], refs[4:8], refs[8:]
    nbr_ref, ifc_ref, solid_ref = small_refs
    position = lax.axis_index("blk")
    blocks = solid_ref.shape[0]
    tiles = solid_ref.shape[1] // LANES
    even = position % 2 == 0
    mine = pl.ds(pl.multiple_of(jnp.where(even, 0, LANES * (tiles - 1)), LANES), LANES)
    pairs = [(pop_hbm.at[:, :, mine], tile_ref), *zip(given, (*small_refs, co_ref))]
    copies = [pltpu.make_async_copy(a, b, sem.at[i]) for i, (a, b) in enumerate(pairs)]
    for copy in copies[1:] + copies[:1]:
        copy.start()
    for copy in copies[1:]:
        copy.wait()
    first = position * blocks
    code = coarse_code(ifc_ref, position, co_ref.shape[0])
    absent = absences(nbr_ref, ifc_ref)
    hot = local_hots(nbr_ref, first)
    solid = [solid_ref[:, LANES * t : LANES * (t + 1)] for t in range(tiles)]

    def load(q, r, t):
        return tile_ref[q, r, :]

    def put(t, bits):
        bits_ref[...] = bits

    for side in (0, 1):

        @pl.when(position % 2 == 1 - side)
        def _(side=side):
            prepare_side(side, load, nbr_ref, solid, put, post_ref, send_ref, hot, absent, code, first, copies[0].wait)


def inner_kernel(pop_ref, nbr_ref, ifc_ref, solid_ref, ahead_ref, abits_ref, cur_ref, outer_ref, bits_ref, code_ref, spread_ref, take_ref, send_ref, mid_ref, *, count):
    position = lax.axis_index("blk")
    blocks = solid_ref.shape[0]
    tiles = solid_ref.shape[1] // LANES
    first = position * blocks
    span = [slice(LANES * t, LANES * (t + 1)) for t in range(tiles)]
    code = coarse_code(ifc_ref, position, count)
    code_ref[...] = code
    absent = absences(nbr_ref, ifc_ref)
    hot = local_hots(nbr_ref, first)
    solid = [solid_ref[:, span[t]] for t in range(tiles)]

    def load(q, r, t):
        return pop_ref[q, r, span[t]]

    def put(t, bits):
        bits_ref[:, span[t]] = bits

    for t, m in enumerate(spread_matrix(tiles)):
        spread_ref[t] = m
    cap = take_ref.shape[2] // 2
    take_ref[0] = take_rows(nbr_ref[0:1, :], first + blocks, blocks, cap)
    take_ref[1] = take_rows(nbr_ref[1:2, :], first - blocks, blocks, cap)
    for t in range(1, tiles - 1):
        put(t, bounce_bits(t, solid, absent))
    for side in (0, 1):

        @pl.when(position % 2 == side)
        def _(side=side):
            prepare_side(side, load, nbr_ref, solid, put, outer_ref, send_ref, hot, absent, code, first)
            outer_ref[1 - side] = ahead_ref[1 - side]
            put(0 if side == 0 else tiles - 1, abits_ref[...])

    for t in range(1, tiles - 1):
        for r in groups(blocks):
            out = collide([pop_ref[q, r, span[t]] for q in range(Q)])
            for q in range(Q):
                mid_ref[t - 1, q, r, :] = out[q]

    def post(q, t):
        if t == 0:
            return outer_ref[1, q]
        return outer_ref[0, q] if t == tiles - 1 else mid_ref[t - 1, q]

    for q in range(Q):
        x = [post(q, t) for t in range(tiles)]
        ghosts = gathers(q, x, hot, None, None)
        for t in range(tiles):
            cur_ref[q, :, span[t]] = pull(
                q, t, x, ghosts, ghosts[0], bits_ref[:, span[t]], post(OPP[q], t), pop_ref[q, :, span[t]]
            )


def current_kernel(cur_ref, outer_ref, code_ref, spread_ref, take_ref, sb_ref, near_ref, ra_ref, rb_ref, now_ref, post_ref, fine_ref, ghost_ref, codes_ref, got_ref, *, count):
    position = lax.axis_index("blk")
    blocks, cells = cur_ref.shape[1:]
    tiles = cells // LANES
    even = position % 2 == 0
    half, j, k = lanes(blocks)
    span = [slice(LANES * t, LANES * (t + 1)) for t in range(tiles)]
    n = ra_ref.shape[0]

    for s in range(n):
        got_ref[0, s] = dot(take_ref[0], split(jnp.where(even, ra_ref[s], rb_ref[s])))
        got_ref[1, s] = dot(take_ref[1], split(jnp.where(even, rb_ref[s], ra_ref[s])))

    def from_next(s):
        return got_ref[0, s // 2] if s % 2 == 0 else roll(got_ref[0, s // 2], 64)

    def from_prev(s):
        return got_ref[1, s // 2] if s % 2 == 1 else roll(got_ref[1, s // 2], 64)

    up_face, up_layer = side_slots(1)
    low_face, low_layer = side_slots(0)
    up = {q: from_next(s) for s, q in enumerate(up_face)}
    low = {q: from_prev(s) for s, q in enumerate(low_face)}
    code = code_ref[...]
    up_code = both_halves(from_next(2 * n - 1), False)
    low_code = both_halves(from_prev(2 * n - 1), True)
    codes_ref[0] = up_code
    codes_ref[1] = low_code
    near = jnp.where(even, near_ref[...], rb_ref[n])

    rows = coarse_rows(code, rows_of(both_halves(near, False)), count)
    for t in range(tiles):
        for s, v in enumerate(coarse_tile(rows, spread_ref[t])):
            fine_ref[s, :, span[t]] = v
    for q in range(Q):
        ex, ey, ez = VEL[q]
        for t in range(tiles):
            v = cur_ref[q, :, span[t]]
            cx, cy, cz = edges(q, t, tiles, half, j, k)
            if ey < 0:
                f = [fine_ref[CROSSING[2].index(q), :, span[m]] for m in range(tiles)]
                g = roll(sources(q, t, f, f[t], half), 64 * abs(ex) - 56 * ey + ez)
                ok = cy
                if cx is not None:
                    ok = ok & jnp.logical_not(cx)
                if cz is not None:
                    ok = ok & jnp.logical_not(cz)
                v = v + jnp.where(ok, g, 0.0)
            if cx is not None:
                ok = cx
                for c in (cy, cz):
                    if c is not None:
                        ok = ok & jnp.logical_not(c)
                v = v + jnp.where(ok, roll(up[q] if ex < 0 else low[q], 64 + 8 * ey + ez), 0.0)
            now_ref[q, :, span[t]] = v

    low_rows = coarse_rows(low_code, rows_of(both_halves(sb_ref[n], False)), count)
    low_fine = coarse_tile(low_rows, spread_ref[tiles])
    for q in range(Q):
        ex, ey, ez = VEL[q]
        _, cy, cz = edges(q, 0, tiles, half, j, k)
        corner = cy if cz is None else (cz if cy is None else cy | cz)
        sides = []
        for e, layer, face, take, mine in (
            (-1, up_layer, up, from_next, outer_ref.at[0]),
            (1, low_layer, low, from_prev, outer_ref.at[1]),
        ):
            if ex == -e:
                v = roll(mine[q], 64 + 8 * ey + ez)
                if corner is not None:
                    v = jnp.where(corner, face[OPP[q]], v)
            else:
                v = take(5 + layer.index(q))
                if ey < 0 and e > 0:
                    ok = cy if cz is None else cy & jnp.logical_not(cz)
                    v = v + jnp.where(ok, roll(low_fine[CROSSING[2].index(q)], ez), 0.0)
            sides.append(v)
        ghost_ref[q] = jnp.where(half, sides[1], sides[0])

    for t in range(tiles):
        for r in groups(blocks):
            out = collide([now_ref[q, r, span[t]] for q in range(Q)])
            for q in range(Q):
                post_ref[q, r, span[t]] = out[q]

    rows = coarse_rows(code, rows_of(both_halves(near, True)), count)
    for t in range(tiles):
        for s, v in enumerate(coarse_tile(rows, spread_ref[t])):
            fine_ref[s, :, span[t]] = v


def final_kernel(now_ref, post_ref, fine_ref, half_ref, codes_ref, bits_ref, spread_ref, rb_ref, relay_ref, nbr_ref, out_ref, buf_ref, ghost_ref, sem, *, count):
    position = lax.axis_index("blk")
    blocks, cells = bits_ref.shape
    tiles = cells // LANES
    first = position * blocks
    half, j, k = lanes(blocks)
    span = [slice(LANES * t, LANES * (t + 1)) for t in range(tiles)]
    hot = local_hots(nbr_ref, first)
    copies = []

    def emit(q, remote):
        x = [post_ref[q, :, span[t]] for t in range(tiles)]
        ghosts = gathers(q, x, hot, lambda s, t: fine_ref[s, :, span[t]], remote)
        for t in range(tiles):
            buf_ref[q, :, span[t]] = pull(
                q, t, x, ghosts, ghosts[0], bits_ref[:, span[t]], post_ref[OPP[q], :, span[t]], now_ref[q, :, span[t]]
            )
        copy = pltpu.make_async_copy(buf_ref.at[q], out_ref.at[q], sem.at[q])
        copy.start()
        copies.append(copy)

    for q in range(Q):
        if VEL[q][0] == 0:
            emit(q, None)
    n = rb_ref.shape[0] - 1
    handed = rows_of(both_halves(relay_ref[n], False))
    direct = [both_halves(rb_ref[n], u) for u in (False, True)]

    def far(c, s):
        row = far_row(c, s, count)
        return jnp.where(position % 2 == 0, handed(c, s), direct[c % 2][row : row + 1])

    up_rows = coarse_rows(codes_ref[0], far, count)
    up_fine = coarse_tile(up_rows, spread_ref[tiles])
    for q in range(Q):
        v = half_ref[q]
        if VEL[q][1] < 0 and VEL[q][0] <= 0:
            _, cy, cz = edges(q, 0, tiles, half, j, k)
            ok = cy & jnp.logical_not(half)
            if cz is not None:
                ok = ok & jnp.logical_not(cz)
            v = v + jnp.where(ok, roll(up_fine[CROSSING[2].index(q)], VEL[q][2]), 0.0)
        ghost_ref[q] = v

    for r in groups(blocks):
        out = collide([ghost_ref[q, r, :] for q in range(Q)])
        for q in range(Q):
            if VEL[q][0]:
                ghost_ref[q, r, :] = out[q]
    remote = {}
    for q in range(Q):
        if VEL[q][0]:
            there = codes_ref[0 if VEL[q][0] < 0 else 1] > 0.5
            remote[q] = jnp.where(there, ghost_ref[q], 0.0)
    for q in range(Q):
        if VEL[q][0]:
            emit(q, remote)
    for copy in copies:
        copy.wait()


def swapped(x, off):
    n = lax.axis_size("blk")
    low = [(i, i + 1) for i in range(off, n - 1, 2)]
    return lax.ppermute(x, "blk", low + [(b, a) for a, b in low])


def held(x):
    return pltpu.with_memory_space_constraint(x, pltpu.VMEM)


def body(populations, coarse_faces, neighbors, interface, solid):
    pop = populations.transpose(1, 0, 2)
    co = coarse_faces.transpose(0, 2, 1, 3)
    nbr, ifc = neighbors.T, interface.T
    blocks, cells = pop.shape[1:]
    count = co.shape[0]
    tiles = cells // LANES
    dense = pl.BlockSpec(memory_space=pltpu.VMEM)
    away = pl.BlockSpec(memory_space=pl.ANY)
    cap = blocks // 2
    room = pltpu.CompilerParams(vmem_limit_bytes=20 << 20)
    sides = pltpu.VMEM((2, Q, blocks, LANES), F32)
    payload = pltpu.VMEM((10, cap, LANES), F32)
    small = (nbr, ifc, solid)
    far_co = swapped(co, 0)
    outer = pl.pallas_call(
        outer_kernel,
        in_specs=[away] * 5,
        out_shape=(sides, pltpu.VMEM((blocks, LANES), I32), pltpu.VMEM(co.shape, F32), payload),
        scratch_shapes=[
            pltpu.VMEM((Q, blocks, LANES), F32),
            *(pltpu.VMEM(a.shape, a.dtype) for a in small),
            pltpu.SemaphoreType.DMA((5,)),
        ],
        compiler_params=pltpu.CompilerParams(vmem_limit_bytes=56 << 20),
        cost_estimate=pl.CostEstimate(flops=20_000_000, bytes_accessed=1_000_000, transcendentals=0),
        name="outer",
    )
    ahead, abits, co, part = outer(pop, *small, co)
    sb, near = pl.pallas_call(
        pack_kernel,
        in_specs=[dense] * 3,
        out_shape=(pltpu.VMEM((11, cap, LANES), F32), pltpu.VMEM((cap, LANES), F32)),
        compiler_params=room,
        name="pack",
    )(held(part), held(co), held(far_co))
    rb = swapped(sb, 1)
    ahead, abits = held(ahead), held(abits)
    inner = pl.pallas_call(
        functools.partial(inner_kernel, count=count),
        in_specs=[dense] * 6,
        out_shape=(
            pltpu.VMEM((Q, blocks, cells), F32),
            sides,
            pltpu.VMEM((blocks, cells), I32),
            pltpu.VMEM((blocks, LANES), F32),
            pltpu.VMEM((tiles + 1, 256, LANES), BF16),
            pltpu.VMEM((2, blocks, 2 * cap), BF16),
            payload,
        ),
        scratch_shapes=[pltpu.VMEM((tiles - 2, Q, blocks, LANES), F32)],
        compiler_params=room,
        cost_estimate=pl.CostEstimate(flops=100_000_000, bytes_accessed=4_000_000, transcendentals=0),
        name="inner",
    )
    cur, outer, bits, code, spread, take, sa = inner(pop, nbr, ifc, solid, ahead, abits)
    ra = swapped(sa, 0)
    relay = swapped(rb, 0)
    state = pltpu.VMEM((Q, blocks, cells), F32)
    layer = pltpu.VMEM((Q, blocks, LANES), F32)
    current = pl.pallas_call(
        functools.partial(current_kernel, count=count),
        in_specs=[dense] * 9,
        out_shape=(state, state, pltpu.VMEM((5, blocks, cells), F32), layer, pltpu.VMEM((2, blocks, LANES), F32)),
        scratch_shapes=[pltpu.VMEM((2, 10, blocks, LANES), F32)],
        compiler_params=room,
        cost_estimate=pl.CostEstimate(flops=100_000_000, bytes_accessed=4_000_000, transcendentals=0),
        name="current",
    )
    given = [held(x) for x in (cur, outer, code, spread, take, sb, near, ra, rb)]
    now, post, fine, ghost, codes = current(*given)
    out = pl.pallas_call(
        functools.partial(final_kernel, count=count),
        in_specs=[dense] * 10,
        out_specs=away,
        out_shape=jax.ShapeDtypeStruct(pop.shape, F32),
        scratch_shapes=[state, layer, pltpu.SemaphoreType.DMA((Q,))],
        compiler_params=room,
        name="final",
    )(*(held(x) for x in (now, post, fine, ghost, codes, bits, spread, rb, relay)), nbr)
    return out.transpose(1, 0, 2)


def solution(mesh):
    placed = (P("blk", None, None), P("blk", None, None, None), P("blk", None), P("blk", None), P("blk", None))
    return jax.shard_map(body, mesh=mesh, in_specs=placed, out_specs=P("blk", None, None), check_vma=False)
```

```python
import functools

import jax
import jax.numpy as jnp
import numpy as np
from jax import lax
from jax.experimental import pallas as pl
from jax.experimental.pallas import tpu as pltpu
from jax.sharding import PartitionSpec as P


F32, BF16, I32 = jnp.float32, jnp.bfloat16, jnp.int32
LANES = 128
VEL = [
    (0, 0, 0),
    (1, 0, 0), (-1, 0, 0), (0, 1, 0), (0, -1, 0), (0, 0, 1), (0, 0, -1),
    (1, 1, 0), (-1, -1, 0), (1, -1, 0), (-1, 1, 0),
    (1, 0, 1), (-1, 0, -1), (1, 0, -1), (-1, 0, 1),
    (0, 1, 1), (0, -1, -1), (0, 1, -1), (0, -1, 1),
]
Q = len(VEL)
OPP = [VEL.index((-x, -y, -z)) for x, y, z in VEL]
CROSSING = [
    [q for q in range(Q) if VEL[q][d // 2] == (-1 if d % 2 == 0 else 1)] for d in range(6)
]


MIRROR = [VEL.index((-x, y, z)) for x, y, z in VEL]
FACE = CROSSING[0]
LAYER = [q for q in range(Q) if VEL[q][0] <= 0]
MIXED = [q for q in LAYER if VEL[q][1] < 0]


def moments():
    v = np.array(VEL) * 1.0
    x, y, z = v[:, 0], v[:, 1], v[:, 2]
    s = x * x + y * y + z * z
    rows = [
        np.ones(19), 19 * s - 30, (21 * s * s - 53 * s + 24) / 2,
        x, (5 * s - 9) * x, y, (5 * s - 9) * y, z, (5 * s - 9) * z,
        3 * x * x - s, (3 * s - 5) * (3 * x * x - s),
        y * y - z * z, (3 * s - 5) * (y * y - z * z),
        x * y, y * z, x * z,
        (y * y - z * z) * x, (z * z - x * x) * y, (x * x - y * y) * z,
    ]
    return np.stack(rows)


def rates():
    norms = (moments() ** 2).sum(1)
    w = 1.0 / 0.6
    relax = np.array([0, 1.19, 1.4, 0, 1.2, 0, 1.2, 0, 1.2, w, 1.4, w, 1.4, w, w, w, 1.98, 1.98, 1.98])
    return [float(c) for c in relax / norms]


def linear(p, items):
    m = moments()
    row = np.eye(Q)[p] - (m.T @ (np.array(rates())[:, None] * m))[p]
    same = {}
    for q, v in items:
        if abs(row[q]) > 1e-12:
            same.setdefault(round(abs(float(row[q])), 10), []).append((row[q] > 0, abs(float(row[q])), v))
    total = None
    for terms in same.values():
        part = None
        for plus, _, v in terms:
            if part is None:
                part = v if plus else -v
            else:
                part = part + v if plus else part - v
        part = terms[0][1] * part
        total = part if total is None else total + part
    return total


def shares(items):
    out = [linear(p, items) for p in FACE]
    total = None
    for _, v in items:
        total = v if total is None else total + v
    out.append(total)
    for axis in range(3):
        total = None
        for q, v in items:
            if VEL[q][axis]:
                v = v if VEL[q][axis] > 0 else -v
                total = v if total is None else total + v
        out.append(total)
    return out


def finish(parts):
    c = rates()
    rho, jx, jy, jz = parts[5:]
    inv = 1.0 / rho
    ux, uy, uz = jx * inv, jy * inv, jz * inv
    xx, yy, zz = jx * ux, jy * uy, jz * uz
    jj = xx + yy + zz
    pe, we = 3 * xx - jj, yy - zz
    r1, r2 = c[1] * (19 * jj - 11 * rho), c[2] * (3 * rho - 5.5 * jj)
    r4, r6, r8 = (c[4] * -2 / 3) * jx, (c[6] * -2 / 3) * jy, (c[8] * -2 / 3) * jz
    r13, r15 = c[13] * (jx * uy), c[15] * (jx * uz)
    ea, eb = -11 * r1 - 4 * r2, 8 * r1 + r2
    b9, b11 = (c[9] - 0.5 * c[10]) * pe, (c[11] - 0.5 * c[12]) * we
    exy, exz = eb + b9 + b11, eb + b9 - b11
    own = {
        (-1, 0, 0): ea + (2 * (c[9] + c[10])) * pe + 4 * r4,
        (-1, -1, 0): exy + r13 - (r4 + r6), (-1, 1, 0): exy - r13 - (r4 - r6),
        (-1, 0, -1): exz + r15 - (r4 + r8), (-1, 0, 1): exz - r15 - (r4 - r8),
    }
    return {p: parts[i] + own[VEL[p]] for i, p in enumerate(FACE)}


def collide(f):
    c = rates()
    s = {q: f[q] + f[q + 1] for q in range(1, 19, 2)}
    d = {q: f[q] - f[q + 1] for q in range(1, 19, 2)}
    a, b, g = s[7] + s[9], s[11] + s[13], s[15] + s[17]
    s1, s2 = s[1] + (s[3] + s[5]), a + b + g
    rho = f[0] + s1 + s2
    ax1, ax2 = d[7] + d[9], d[11] + d[13]
    ay1, ay2 = d[7] - d[9], d[15] + d[17]
    az1, az2 = d[11] - d[13], d[15] - d[17]
    ax, ay, az = ax1 + ax2, ay1 + ay2, az1 + az2
    jx, jy, jz = d[1] + ax, d[3] + ay, d[5] + az
    inv = 1.0 / rho
    ux, uy, uz = jx * inv, jy * inv, jz * inv
    xx, yy, zz = jx * ux, jy * uy, jz * uz
    jj = xx + yy + zz
    r1 = (19 * c[1]) * (s2 - f[0] - jj)
    r2 = c[2] * (9 * f[0] - 7 * s1 - 2 * s2 + 5.5 * jj)
    t1, t2, pe = 2 * s[1] - (s[3] + s[5]), a + b - 2 * g, 3 * xx - jj
    v1, v2, we = s[3] - s[5], a - b, yy - zz
    r9, r10 = c[9] * (t1 + t2 - pe), c[10] * (t2 - 2 * t1 + 0.5 * pe)
    r11, r12 = c[11] * (v1 + v2 - we), c[12] * (v2 - 2 * v1 + 0.5 * we)
    r13 = c[13] * (s[7] - s[9] - jx * uy)
    r14 = c[14] * (s[15] - s[17] - jy * uz)
    r15 = c[15] * (s[11] - s[13] - jx * uz)
    r4 = (c[4] * 5 / 3) * (ax - 2 * d[1])
    r6 = (c[6] * 5 / 3) * (ay - 2 * d[3])
    r8 = (c[8] * 5 / 3) * (az - 2 * d[5])
    r16, r17, r18 = c[16] * (ax1 - ax2), c[17] * (ay2 - ay1), c[18] * (az1 - az2)
    ea, eb = -11 * r1 - 4 * r2, 8 * r1 + r2
    a9, a11 = r9 - 2 * r10, r11 - 2 * r12
    b9, b11 = r9 + r10, r11 + r12
    exy, exz, eyz = eb + b9 + b11, eb + b9 - b11, eb - 2 * b9
    even = {
        1: ea + 2 * a9, 3: ea - a9 + a11, 5: ea - a9 - a11,
        7: exy + r13, 9: exy - r13, 11: exz + r15, 13: exz - r15, 15: eyz + r14, 17: eyz - r14,
    }
    odd = {
        1: -4 * r4, 3: -4 * r6, 5: -4 * r8,
        7: (r4 + r6) + (r16 - r17), 9: (r4 - r6) + (r16 + r17),
        11: (r4 + r8) - (r16 - r18), 13: (r4 - r8) - (r16 + r18),
        15: (r6 + r8) + (r17 - r18), 17: (r6 - r8) + (r17 + r18),
    }
    out = [f[0] + 30 * r1 - 12 * r2]
    for q in range(1, 19, 2):
        out += [f[q] - even[q] - odd[q], f[q + 1] - even[q] + odd[q]]
    return out


def feq(h):
    rho = h[0]
    for q in range(1, Q):
        rho = rho + h[q]
    safe = jnp.where(rho > 0, rho, 1.0)
    u = []
    for axis in range(3):
        m = None
        for q in range(Q):
            if VEL[q][axis]:
                t = h[q] if VEL[q][axis] > 0 else -h[q]
                m = t if m is None else m + t
        u.append(m / safe)
    sq = u[0] * u[0] + u[1] * u[1] + u[2] * u[2]
    out = {}
    for q in CROSSING[2]:
        p = None
        for axis in range(3):
            if VEL[q][axis]:
                t = u[axis] if VEL[q][axis] > 0 else -u[axis]
                p = t if p is None else p + t
        n = sum(abs(e) for e in VEL[q])
        w = 1.0 / 18.0 if n == 1 else 1.0 / 36.0
        out[q] = w * rho * (1.0 + 3.0 * p + 4.5 * p * p - 1.5 * sq)
    return out


def lanes(rows):
    l = lax.broadcasted_iota(I32, (rows, LANES), 1)
    return l >= 64, (l >> 3) & 7, l & 7


def split(x):
    hi = x.astype(BF16)
    lo = (x - hi.astype(F32)).astype(BF16)
    return jnp.concatenate([hi, lo], axis=0)


def dot(a, b):
    return jnp.dot(a, b, preferred_element_type=F32)


def select_rows(row, offset, count):
    r = lax.broadcasted_iota(I32, (count, row.shape[1]), 0)
    hot = jnp.where(r == row - offset, 1.0, 0.0).astype(BF16)
    return jnp.concatenate([hot, hot], axis=1)


def spread_rows(flags):
    n = flags.shape[1]
    eye = lax.broadcasted_iota(I32, (n, n), 0) == lax.broadcasted_iota(I32, (n, n), 1)
    diag = jnp.where(eye, flags.astype(F32), 0.0).astype(BF16)
    return dot(diag, jnp.ones((n, LANES), BF16))


def sources(q, t, tiles, outer, half):
    ex = VEL[q][0]
    if ex == 0:
        return tiles[t]
    n = t - ex
    other = tiles[n] if 0 <= n < len(tiles) else outer
    return jnp.where(half, other, tiles[t]) if ex > 0 else jnp.where(half, tiles[t], other)


def roll(x, by):
    by %= LANES
    return pltpu.roll(x, by, 1) if by else x


def edges(q, t, count, half, j, k):
    ex, ey, ez = VEL[q]
    cx = None
    if ex > 0 and t == 0:
        cx = jnp.logical_not(half)
    if ex < 0 and t == count - 1:
        cx = half
    cy = None if ey == 0 else (j == (0 if ey > 0 else 7))
    cz = None if ez == 0 else (k == (0 if ez > 0 else 7))
    return cx, cy, cz


def face_of(axis, e):
    return 2 * axis + (1 if e > 0 else 0)


def bounce_bits(t, solid, absent):
    half, j, k = lanes(solid[0].shape[0])
    acc = jnp.where(solid[t] != 0, 1, 0)
    for q in range(1, Q):
        ex, ey, ez = VEL[q]
        v = roll(sources(q, t, solid, solid[t], half), 64 * abs(ex) + 8 * ey + ez)
        sides = zip(edges(q, t, len(solid), half, j, k), (ex, ey, ez), range(3))
        crossed = [c for c in sides if c[0] is not None]
        for c, e, axis in crossed:
            v = jnp.where(c, absent[face_of(axis, e)], v)
        for i in range(len(crossed)):
            for m in range(i):
                v = jnp.where(crossed[i][0] & crossed[m][0], 1, v)
        acc = acc | (jnp.where(v != 0, 1, 0) << q)
    return acc


def absences(nbr_ref, ifc_ref):
    out = []
    for d in range(6):
        there = nbr_ref[d : d + 1, :] >= 0
        if d == 2:
            there = there | (ifc_ref[0:1, :] >= 0)
        out.append((1.0 - spread_rows(jnp.where(there, 1.0, 0.0))).astype(I32))
    return out


def local_hots(nbr_ref, first):
    n = nbr_ref.shape[1]
    return [select_rows(nbr_ref[(d ^ 1) : (d ^ 1) + 1, :], first, n) for d in range(6)]


def send_rows(row, first, count, cap):
    rel = row - first
    gone = (rel >= 0) & (rel < count)
    rel = jnp.where(gone, rel, 255)
    ahead = spread_rows(rel)[:, :count] < rel.astype(F32)
    rank = jnp.sum(jnp.where(ahead, 1.0, 0.0), axis=0, keepdims=True)
    r = lax.broadcasted_iota(I32, (cap, count), 0).astype(F32)
    hot = jnp.where((r == rank) & gone, 1.0, 0.0).astype(BF16)
    return jnp.concatenate([hot, hot], axis=1)


def take_rows(row, first, count, cap):
    rel = row - first
    gone = jnp.where((rel >= 0) & (rel < count), 1.0, 0.0)
    b = lax.broadcasted_iota(I32, (count, count), 0)
    a = lax.broadcasted_iota(I32, (count, count), 1)
    rank = dot(jnp.where(a < b, gone, 0.0).astype(BF16), jnp.ones((count, LANES), BF16))[:, :cap]
    there = spread_rows(gone)[:, :cap] > 0.5
    r = lax.broadcasted_iota(I32, (count, cap), 1).astype(F32)
    hot = jnp.where((r == rank) & there, 1.0, 0.0).astype(BF16)
    return jnp.concatenate([hot, hot], axis=1)


def coarse_code(ifc_ref, position, count):
    c = ifc_ref[0:1, :]
    code = jnp.where(c >= 0, 2 + 4 * (c - (position + 1) * count) + ifc_ref[1:2, :], 1)
    return spread_rows(code)


def far_row(c, s, count):
    return 5 * count + 5 * (c // 2) + s


def pack_kernel(part_ref, co_ref, far_co_ref, send_ref, near_ref):
    refs = (co_ref, far_co_ref)
    count = co_ref.shape[0]
    n = part_ref.shape[0]
    send_ref[:n] = part_ref[...]
    h = []
    for q in range(Q):
        h0 = jnp.concatenate([r[:, q, 0, :] for r in refs], axis=0)
        h1 = (1.0 - 0.5) * h0 + 0.5 * jnp.concatenate([r[:, q, 1, :] for r in refs], axis=0)
        h.append(jnp.concatenate([h0, h1], axis=1))
    e = feq(h)
    send_ref[n] = jnp.zeros_like(send_ref[n])
    near_ref[...] = jnp.zeros_like(near_ref)
    upper = lanes(1)[0]
    for s, q in enumerate(CROSSING[2]):
        v = e[q] + (0.6 / 1.1) * (h[q] - e[q])
        for c in range(count):
            send_ref[n, 5 * c + s : 5 * c + s + 1, :] = v[c : c + 1]
            near_ref[5 * c + s : 5 * c + s + 1, :] = v[count + c : count + c + 1]
        turned = roll(v, 64)
        for c in range(0, count, 2):
            other = min(c + 1, count - 1)
            to = far_row(c, s, count)
            send_ref[n, to : to + 1, :] = jnp.where(upper, turned[count + other : count + other + 1], v[count + c : count + c + 1])


def both_halves(x, upper):
    half = lanes(x.shape[0])[0]
    return jnp.where(half, x, roll(x, 64)) if upper else jnp.where(half, roll(x, 64), x)


def spread_matrix(tiles):
    kk = lax.broadcasted_iota(I32, (256, LANES), 0)
    ll = lax.broadcasted_iota(I32, (256, LANES), 1)
    w, m, k = kk >> 6, kk & 63, ll & 7
    out = []
    for t in range(tiles + 1):
        i = (ll >> 6) * 7 if t == tiles else 2 * t + (ll >> 6)
        want = 8 * (4 * (w >> 1) + (i >> 1)) + 4 * (w & 1) + (k >> 1)
        out.append(jnp.where(m == want, 1.0, 0.0).astype(BF16))
    return out


def rows_of(cg):
    return lambda c, s: cg[5 * c + s : 5 * c + s + 1, :]


def coarse_rows(code, cg, count):
    half = lanes(code.shape[0])[0]
    hi, lo = [], []
    for s in range(5):
        parts = []
        for pair in (0, 2):
            acc = jnp.zeros_like(code)
            for c in range(count):
                want = jnp.where(half, 3.0 + 4 * c + pair, 2.0 + 4 * c + pair)
                acc = jnp.where(code == want, cg(c, s), acc)
            parts.append(acc)
        x = jnp.concatenate(parts, axis=1)
        h = x.astype(BF16)
        hi.append(h)
        lo.append((x - h.astype(F32)).astype(BF16))
    return jnp.concatenate(hi + lo, axis=0)


def coarse_tile(rows, matrix):
    g = dot(rows, matrix)
    n = g.shape[0] // 2
    g = g[:n] + g[n:]
    b = n // 5
    return [g[b * s : b * (s + 1)] for s in range(5)]


def pull(q, t, x, parts, gx, bits, bounced, init):
    if q == 0:
        return jnp.where((bits & 1) != 0, init, x[t])
    half, j, k = lanes(bits.shape[0])
    ex, ey, ez = VEL[q]
    turn = 64 * abs(ex)
    out = roll(sources(q, t, x, gx, half), turn + 8 * ey + ez)
    _, cy, cz = edges(q, t, len(x), half, j, k)
    if ey:
        g = parts[1]
        out = jnp.where(cy, roll(sources(q, t, g, g[t], half), turn - 56 * ey + ez), out)
    if ez:
        g = parts[2]
        out = jnp.where(cz, roll(sources(q, t, g, g[t], half), turn + 8 * ey - 7 * ez), out)
    out = jnp.where((bits & (1 << q)) != 0, bounced, out)
    return jnp.where((bits & 1) != 0, init, out)


def gathers(q, x, hot, fine, remote):
    ex, ey, ez = VEL[q]
    gx, gy, gz = None, None, None
    if q:
        parts = [split(v) for v in x]
    if ex:
        gx = dot(hot[face_of(0, ex)], parts[0 if ex < 0 else len(x) - 1])
        if remote is not None:
            gx = gx + remote[q]
    if ey:
        gy = [dot(hot[face_of(1, ey)], p) for p in parts]
        if ey < 0 and fine is not None:
            s = CROSSING[2].index(q)
            gy = [g + fine(s, t) for t, g in enumerate(gy)]
    if ez:
        gz = [dot(hot[face_of(2, ez)], p) for p in parts]
    return gx, gy, gz


def corners(q, half, j, k):
    _, cy, cz = edges(q, 0, 0, half, j, k)
    return cy if cz is None else (cz if cy is None else cy | cz)


def groups(blocks):
    return [slice(g, g + 8) for g in range(0, blocks, 8)]


def prepare_side(side, load, nbr_ref, solid, bits_put, post_ref, send_ref, hot, absent, code, first, ready=None):
    tiles = len(solid)
    blocks = solid[0].shape[0]
    t = tiles - 1 if side == 0 else 0
    half, j, k = lanes(blocks)
    bits = bounce_bits(t, solid, absent)
    bits_put(t, bits)
    if ready is not None:
        ready()

    for r in groups(blocks):
        out = collide([load(q, r, t) for q in range(Q)])
        for q in range(Q):
            post_ref[side, q, r, :] = out[q]
    to = send_rows(nbr_ref[side : side + 1, :], first + (blocks if side == 0 else -blocks), blocks, send_ref.shape[1])
    actual = list(range(Q)) if side == 1 else MIRROR
    streamed = []
    for c in LAYER:
        q = actual[c]
        ex, ey, ez = VEL[q]
        x = post_ref[side, q]
        turn = 64 * abs(ex)
        out = roll(x, turn + 8 * ey + ez)
        _, cy, cz = edges(q, t, tiles, half, j, k)
        if ey or ez:
            parts = split(x)
        if ey:
            out = jnp.where(cy, roll(dot(hot[face_of(1, ey)], parts), turn - 56 * ey + ez), out)
        if ez:
            out = jnp.where(cz, roll(dot(hot[face_of(2, ez)], parts), turn + 8 * ey - 7 * ez), out)
        if q:
            out = jnp.where((bits & (1 << q)) != 0, post_ref[side, OPP[q]], out)
        streamed.append((c, out))
    for c in range(Q):
        corner = corners(c, half, j, k)
        if VEL[c][0] > 0 and corner is not None:
            streamed.append((c, jnp.where(corner, post_ref[side, OPP[actual[c]]], 0.0)))
    slots = [post_ref[side, actual[c]] for c in FACE] + shares(streamed) + [code]
    for s in range(0, len(slots), 2):
        a, b = slots[s], slots[min(s + 1, len(slots) - 1)]
        packed = jnp.where(half, b, roll(a, 64)) if side == 0 else jnp.where(half, roll(b, 64), a)
        send_ref[s // 2] = dot(to, split(packed))


def outer_kernel(pop_hbm, *refs):
    given, (post_ref, bits_ref, co_ref, send_ref), (tile_ref, *small_refs, sem) = refs[:4], refs[4:8], refs[8:]
    nbr_ref, ifc_ref, solid_ref = small_refs
    position = lax.axis_index("blk")
    blocks = solid_ref.shape[0]
    tiles = solid_ref.shape[1] // LANES
    even = position % 2 == 0
    mine = pl.ds(pl.multiple_of(jnp.where(even, 0, LANES * (tiles - 1)), LANES), LANES)
    pairs = [(pop_hbm.at[:, :, mine], tile_ref), *zip(given, (*small_refs, co_ref))]
    copies = [pltpu.make_async_copy(a, b, sem.at[i]) for i, (a, b) in enumerate(pairs)]
    for copy in copies[1:] + copies[:1]:
        copy.start()
    for copy in copies[1:]:
        copy.wait()
    first = position * blocks
    code = coarse_code(ifc_ref, position, co_ref.shape[0])
    absent = absences(nbr_ref, ifc_ref)
    hot = local_hots(nbr_ref, first)
    solid = [solid_ref[:, LANES * t : LANES * (t + 1)] for t in range(tiles)]

    def load(q, r, t):
        return tile_ref[q, r, :]

    def put(t, bits):
        bits_ref[...] = bits

    for side in (0, 1):

        @pl.when(position % 2 == 1 - side)
        def _(side=side):
            prepare_side(side, load, nbr_ref, solid, put, post_ref, send_ref, hot, absent, code, first, copies[0].wait)


def inner_kernel(pop_ref, nbr_ref, ifc_ref, solid_ref, ahead_ref, abits_ref, cur_ref, bits_ref, code_ref, spread_ref, take_ref, send_ref, own_ref, mid_ref, outer_ref, *, count):
    position = lax.axis_index("blk")
    blocks = solid_ref.shape[0]
    tiles = solid_ref.shape[1] // LANES
    first = position * blocks
    span = [slice(LANES * t, LANES * (t + 1)) for t in range(tiles)]
    code = coarse_code(ifc_ref, position, count)
    code_ref[...] = code
    absent = absences(nbr_ref, ifc_ref)
    hot = local_hots(nbr_ref, first)
    solid = [solid_ref[:, span[t]] for t in range(tiles)]

    def load(q, r, t):
        return pop_ref[q, r, span[t]]

    def put(t, bits):
        bits_ref[:, span[t]] = bits

    for t, m in enumerate(spread_matrix(tiles)):
        spread_ref[t] = m
    cap = take_ref.shape[2] // 2
    take_ref[0] = take_rows(nbr_ref[0:1, :], first + blocks, blocks, cap)
    take_ref[1] = take_rows(nbr_ref[1:2, :], first - blocks, blocks, cap)
    for t in range(1, tiles - 1):
        put(t, bounce_bits(t, solid, absent))
    for side in (0, 1):

        @pl.when(position % 2 == side)
        def _(side=side):
            prepare_side(side, load, nbr_ref, solid, put, outer_ref, send_ref, hot, absent, code, first)
            outer_ref[1 - side] = ahead_ref[1 - side]
            put(0 if side == 0 else tiles - 1, abits_ref[...])

    for t in range(1, tiles - 1):
        for r in groups(blocks):
            out = collide([pop_ref[q, r, span[t]] for q in range(Q)])
            for q in range(Q):
                mid_ref[t - 1, q, r, :] = out[q]

    half, j, k = lanes(blocks)
    items = []
    for q in range(Q):
        if VEL[q][0] > 0:
            turn = 64 + 8 * VEL[q][1] + VEL[q][2]
            v = jnp.where(half, roll(outer_ref[1, MIRROR[q]], turn), roll(outer_ref[0, q], turn))
            corner = corners(q, half, j, k)
            items.append((q, v if corner is None else jnp.where(corner, 0.0, v)))
    for i, v in enumerate(shares(items)):
        own_ref[i] = v

    def post(q, t):
        if t == 0:
            return outer_ref[1, q]
        return outer_ref[0, q] if t == tiles - 1 else mid_ref[t - 1, q]

    for q in range(Q):
        x = [post(q, t) for t in range(tiles)]
        ghosts = gathers(q, x, hot, None, None)
        for t in range(tiles):
            cur_ref[q, :, span[t]] = pull(
                q, t, x, ghosts, ghosts[0], bits_ref[:, span[t]], post(OPP[q], t), pop_ref[q, :, span[t]]
            )


def current_kernel(cur_ref, own_ref, code_ref, spread_ref, take_ref, near_ref, ra_ref, rb_ref, now_ref, post_ref, fine_ref, ghost_ref, codes_ref, got_ref, *, count):
    position = lax.axis_index("blk")
    blocks, cells = cur_ref.shape[1:]
    tiles = cells // LANES
    even = position % 2 == 0
    half, j, k = lanes(blocks)
    span = [slice(LANES * t, LANES * (t + 1)) for t in range(tiles)]
    n = ra_ref.shape[0]

    for s in range(n):
        got_ref[0, s] = dot(take_ref[0], split(jnp.where(even, ra_ref[s], rb_ref[s])))
        got_ref[1, s] = dot(take_ref[1], split(jnp.where(even, rb_ref[s], ra_ref[s])))

    def from_next(s):
        return got_ref[0, s // 2] if s % 2 == 0 else roll(got_ref[0, s // 2], 64)

    def from_prev(s):
        return got_ref[1, s // 2] if s % 2 == 1 else roll(got_ref[1, s // 2], 64)

    up = {q: from_next(s) for s, q in enumerate(FACE)}
    low = {MIRROR[q]: from_prev(s) for s, q in enumerate(FACE)}
    code = code_ref[...]
    up_code = both_halves(from_next(14), False)
    low_code = both_halves(from_prev(14), True)
    codes_ref[0] = up_code
    codes_ref[1] = low_code
    near = jnp.where(even, near_ref[...], rb_ref[n])

    rows = coarse_rows(code, rows_of(both_halves(near, False)), count)
    for t in range(tiles):
        for s, v in enumerate(coarse_tile(rows, spread_ref[t])):
            fine_ref[s, :, span[t]] = v
    for q in range(Q):
        ex, ey, ez = VEL[q]
        for t in range(tiles):
            v = cur_ref[q, :, span[t]]
            cx, cy, cz = edges(q, t, tiles, half, j, k)
            if ey < 0:
                f = [fine_ref[CROSSING[2].index(q), :, span[m]] for m in range(tiles)]
                g = roll(sources(q, t, f, f[t], half), 64 * abs(ex) - 56 * ey + ez)
                ok = cy
                if cx is not None:
                    ok = ok & jnp.logical_not(cx)
                if cz is not None:
                    ok = ok & jnp.logical_not(cz)
                v = v + jnp.where(ok, g, 0.0)
            if cx is not None:
                ok = cx
                for c in (cy, cz):
                    if c is not None:
                        ok = ok & jnp.logical_not(c)
                v = v + jnp.where(ok, roll(up[q] if ex < 0 else low[q], 64 + 8 * ey + ez), 0.0)
            now_ref[q, :, span[t]] = v

    for i in range(9):
        ghost_ref[i] = own_ref[i] + jnp.where(half, from_prev(5 + i), from_next(5 + i))

    for t in range(tiles):
        for r in groups(blocks):
            out = collide([now_ref[q, r, span[t]] for q in range(Q)])
            for q in range(Q):
                post_ref[q, r, span[t]] = out[q]

    rows = coarse_rows(code, rows_of(both_halves(near, True)), count)
    for t in range(tiles):
        for s, v in enumerate(coarse_tile(rows, spread_ref[t])):
            fine_ref[s, :, span[t]] = v


def final_kernel(now_ref, post_ref, fine_ref, half_ref, codes_ref, bits_ref, spread_ref, sb_ref, rb_ref, relay_ref, nbr_ref, out_ref, buf_ref, sem, *, count):
    position = lax.axis_index("blk")
    blocks, cells = bits_ref.shape
    tiles = cells // LANES
    first = position * blocks
    half, j, k = lanes(blocks)
    span = [slice(LANES * t, LANES * (t + 1)) for t in range(tiles)]
    hot = local_hots(nbr_ref, first)
    copies = []

    def emit(q, remote):
        x = [post_ref[q, :, span[t]] for t in range(tiles)]
        ghosts = gathers(q, x, hot, lambda s, t: fine_ref[s, :, span[t]], remote)
        for t in range(tiles):
            buf_ref[q, :, span[t]] = pull(
                q, t, x, ghosts, ghosts[0], bits_ref[:, span[t]], post_ref[OPP[q], :, span[t]], now_ref[q, :, span[t]]
            )
        copy = pltpu.make_async_copy(buf_ref.at[q], out_ref.at[q], sem.at[q])
        copy.start()
        copies.append(copy)

    for q in range(Q):
        if VEL[q][0] == 0:
            emit(q, None)
    n = rb_ref.shape[0] - 1
    handed = rows_of(both_halves(relay_ref[n], False))
    direct = [both_halves(rb_ref[n], u) for u in (False, True)]

    def far(c, s):
        row = far_row(c, s, count)
        return jnp.where(position % 2 == 0, handed(c, s), direct[c % 2][row : row + 1])

    up_rows = coarse_rows(codes_ref[0], far, count)
    up_fine = coarse_tile(up_rows, spread_ref[tiles])
    low_rows = coarse_rows(codes_ref[1], rows_of(both_halves(sb_ref[n], False)), count)
    low_fine = coarse_tile(low_rows, spread_ref[tiles])
    items = []
    for q in MIXED:
        _, cy, cz = edges(q, 0, tiles, half, j, k)
        ok = cy if cz is None else cy & jnp.logical_not(cz)
        v = jnp.where(half, low_fine[CROSSING[2].index(MIRROR[q])], up_fine[CROSSING[2].index(q)])
        items.append((q, jnp.where(ok, roll(v, VEL[q][2]), 0.0)))
    parts = [half_ref[i] + v for i, v in enumerate(shares(items))]
    remote = {}
    for q, v in finish(parts).items():
        remote[q] = jnp.where(codes_ref[0] > 0.5, v, 0.0)
        remote[MIRROR[q]] = jnp.where(codes_ref[1] > 0.5, v, 0.0)
    for q in range(Q):
        if VEL[q][0]:
            emit(q, remote)
    for copy in copies:
        copy.wait()


def swapped(x, off):
    n = lax.axis_size("blk")
    low = [(i, i + 1) for i in range(off, n - 1, 2)]
    return lax.ppermute(x, "blk", low + [(b, a) for a, b in low])


def held(x):
    return pltpu.with_memory_space_constraint(x, pltpu.VMEM)


def body(populations, coarse_faces, neighbors, interface, solid):
    pop = populations.transpose(1, 0, 2)
    co = coarse_faces.transpose(0, 2, 1, 3)
    nbr, ifc = neighbors.T, interface.T
    blocks, cells = pop.shape[1:]
    count = co.shape[0]
    tiles = cells // LANES
    dense = pl.BlockSpec(memory_space=pltpu.VMEM)
    away = pl.BlockSpec(memory_space=pl.ANY)
    cap = blocks // 2
    room = pltpu.CompilerParams(vmem_limit_bytes=20 << 20)
    sides = pltpu.VMEM((2, Q, blocks, LANES), F32)
    payload = pltpu.VMEM((8, cap, LANES), F32)
    small = (nbr, ifc, solid)
    far_co = swapped(co, 0)
    outer = pl.pallas_call(
        outer_kernel,
        in_specs=[away] * 5,
        out_shape=(sides, pltpu.VMEM((blocks, LANES), I32), pltpu.VMEM(co.shape, F32), payload),
        scratch_shapes=[
            pltpu.VMEM((Q, blocks, LANES), F32),
            *(pltpu.VMEM(a.shape, a.dtype) for a in small),
            pltpu.SemaphoreType.DMA((5,)),
        ],
        compiler_params=pltpu.CompilerParams(vmem_limit_bytes=56 << 20),
        cost_estimate=pl.CostEstimate(flops=20_000_000, bytes_accessed=1_000_000, transcendentals=0),
        name="outer",
    )
    ahead, abits, co, part = outer(pop, *small, co)
    sb, near = pl.pallas_call(
        pack_kernel,
        in_specs=[dense] * 3,
        out_shape=(pltpu.VMEM((9, cap, LANES), F32), pltpu.VMEM((cap, LANES), F32)),
        compiler_params=room,
        name="pack",
    )(held(part), held(co), held(far_co))
    rb = swapped(sb, 1)
    ahead, abits = held(ahead), held(abits)
    inner = pl.pallas_call(
        functools.partial(inner_kernel, count=count),
        in_specs=[dense] * 6,
        out_shape=(
            pltpu.VMEM((Q, blocks, cells), F32),
            pltpu.VMEM((blocks, cells), I32),
            pltpu.VMEM((blocks, LANES), F32),
            pltpu.VMEM((tiles + 1, 256, LANES), BF16),
            pltpu.VMEM((2, blocks, 2 * cap), BF16),
            payload,
            pltpu.VMEM((9, blocks, LANES), F32),
        ),
        scratch_shapes=[pltpu.VMEM((tiles - 2, Q, blocks, LANES), F32), sides],
        compiler_params=room,
        cost_estimate=pl.CostEstimate(flops=100_000_000, bytes_accessed=4_000_000, transcendentals=0),
        name="inner",
    )
    cur, bits, code, spread, take, sa, own = inner(pop, nbr, ifc, solid, ahead, abits)
    ra = swapped(sa, 0)
    relay = swapped(rb, 0)
    state = pltpu.VMEM((Q, blocks, cells), F32)
    layer = pltpu.VMEM((9, blocks, LANES), F32)
    current = pl.pallas_call(
        functools.partial(current_kernel, count=count),
        in_specs=[dense] * 8,
        out_shape=(state, state, pltpu.VMEM((5, blocks, cells), F32), layer, pltpu.VMEM((2, blocks, LANES), F32)),
        scratch_shapes=[pltpu.VMEM((2, 8, blocks, LANES), F32)],
        compiler_params=room,
        cost_estimate=pl.CostEstimate(flops=100_000_000, bytes_accessed=4_000_000, transcendentals=0),
        name="current",
    )
    given = [held(x) for x in (cur, own, code, spread, take, near, ra, rb)]
    now, post, fine, ghost, codes = current(*given)
    out = pl.pallas_call(
        functools.partial(final_kernel, count=count),
        in_specs=[dense] * 11,
        out_specs=away,
        out_shape=jax.ShapeDtypeStruct(pop.shape, F32),
        scratch_shapes=[state, pltpu.SemaphoreType.DMA((Q,))],
        compiler_params=room,
        name="final",
    )(*(held(x) for x in (now, post, fine, ghost, codes, bits, spread, sb, rb, relay)), nbr)
    return out.transpose(1, 0, 2)


def solution(mesh):
    placed = (P("blk", None, None), P("blk", None, None, None), P("blk", None), P("blk", None), P("blk", None))
    return jax.shard_map(body, mesh=mesh, in_specs=placed, out_specs=P("blk", None, None), check_vma=False)
```

```python
import functools

import jax
import jax.numpy as jnp
import numpy as np
from jax import lax
from jax.experimental import pallas as pl
from jax.experimental.pallas import tpu as pltpu
from jax.sharding import PartitionSpec as P


F32, BF16, I32 = jnp.float32, jnp.bfloat16, jnp.int32
LANES = 128
VEL = [
    (0, 0, 0),
    (1, 0, 0), (-1, 0, 0), (0, 1, 0), (0, -1, 0), (0, 0, 1), (0, 0, -1),
    (1, 1, 0), (-1, -1, 0), (1, -1, 0), (-1, 1, 0),
    (1, 0, 1), (-1, 0, -1), (1, 0, -1), (-1, 0, 1),
    (0, 1, 1), (0, -1, -1), (0, 1, -1), (0, -1, 1),
]
Q = len(VEL)
OPP = [VEL.index((-x, -y, -z)) for x, y, z in VEL]
CROSSING = [
    [q for q in range(Q) if VEL[q][d // 2] == (-1 if d % 2 == 0 else 1)] for d in range(6)
]


MIRROR = [VEL.index((-x, y, z)) for x, y, z in VEL]
FACE = CROSSING[0]
LAYER = [q for q in range(Q) if VEL[q][0] <= 0]
MIXED = [q for q in LAYER if VEL[q][1] < 0]


def moments():
    v = np.array(VEL) * 1.0
    x, y, z = v[:, 0], v[:, 1], v[:, 2]
    s = x * x + y * y + z * z
    rows = [
        np.ones(19), 19 * s - 30, (21 * s * s - 53 * s + 24) / 2,
        x, (5 * s - 9) * x, y, (5 * s - 9) * y, z, (5 * s - 9) * z,
        3 * x * x - s, (3 * s - 5) * (3 * x * x - s),
        y * y - z * z, (3 * s - 5) * (y * y - z * z),
        x * y, y * z, x * z,
        (y * y - z * z) * x, (z * z - x * x) * y, (x * x - y * y) * z,
    ]
    return np.stack(rows)


def rates():
    norms = (moments() ** 2).sum(1)
    w = 1.0 / 0.6
    relax = np.array([0, 1.19, 1.4, 0, 1.2, 0, 1.2, 0, 1.2, w, 1.4, w, 1.4, w, w, w, 1.98, 1.98, 1.98])
    return [float(c) for c in relax / norms]


def kept(f, wall):
    out = collide(f)
    return [jnp.where(wall, f[OPP[q]], out[q]) for q in range(Q)]


def linear(p, items):
    m = moments()
    row = np.eye(Q)[p] - (m.T @ (np.array(rates())[:, None] * m))[p]
    same = {}
    for q, v in items:
        if abs(row[q]) > 1e-12:
            same.setdefault(round(abs(float(row[q])), 10), []).append((row[q] > 0, abs(float(row[q])), v))
    total = None
    for terms in same.values():
        part = None
        for plus, _, v in terms:
            if part is None:
                part = v if plus else -v
            else:
                part = part + v if plus else part - v
        part = terms[0][1] * part
        total = part if total is None else total + part
    return total


def shares(items):
    out = [linear(p, items) for p in FACE]
    total = None
    for _, v in items:
        total = v if total is None else total + v
    out.append(total)
    for axis in range(3):
        total = None
        for q, v in items:
            if VEL[q][axis]:
                v = v if VEL[q][axis] > 0 else -v
                total = v if total is None else total + v
        out.append(total)
    return out


def finish(parts):
    c = rates()
    rho, jx, jy, jz = parts[5:]
    inv = 1.0 / rho
    ux, uy, uz = jx * inv, jy * inv, jz * inv
    xx, yy, zz = jx * ux, jy * uy, jz * uz
    jj = xx + yy + zz
    pe, we = 3 * xx - jj, yy - zz
    r1, r2 = c[1] * (19 * jj - 11 * rho), c[2] * (3 * rho - 5.5 * jj)
    r4, r6, r8 = (c[4] * -2 / 3) * jx, (c[6] * -2 / 3) * jy, (c[8] * -2 / 3) * jz
    r13, r15 = c[13] * (jx * uy), c[15] * (jx * uz)
    ea, eb = -11 * r1 - 4 * r2, 8 * r1 + r2
    b9, b11 = (c[9] - 0.5 * c[10]) * pe, (c[11] - 0.5 * c[12]) * we
    exy, exz = eb + b9 + b11, eb + b9 - b11
    own = {
        (-1, 0, 0): ea + (2 * (c[9] + c[10])) * pe + 4 * r4,
        (-1, -1, 0): exy + r13 - (r4 + r6), (-1, 1, 0): exy - r13 - (r4 - r6),
        (-1, 0, -1): exz + r15 - (r4 + r8), (-1, 0, 1): exz - r15 - (r4 - r8),
    }
    return {p: parts[i] + own[VEL[p]] for i, p in enumerate(FACE)}


def collide(f):
    c = rates()
    s = {q: f[q] + f[q + 1] for q in range(1, 19, 2)}
    d = {q: f[q] - f[q + 1] for q in range(1, 19, 2)}
    a, b, g = s[7] + s[9], s[11] + s[13], s[15] + s[17]
    s1, s2 = s[1] + (s[3] + s[5]), a + b + g
    rho = f[0] + s1 + s2
    ax1, ax2 = d[7] + d[9], d[11] + d[13]
    ay1, ay2 = d[7] - d[9], d[15] + d[17]
    az1, az2 = d[11] - d[13], d[15] - d[17]
    ax, ay, az = ax1 + ax2, ay1 + ay2, az1 + az2
    jx, jy, jz = d[1] + ax, d[3] + ay, d[5] + az
    inv = 1.0 / rho
    ux, uy, uz = jx * inv, jy * inv, jz * inv
    xx, yy, zz = jx * ux, jy * uy, jz * uz
    jj = xx + yy + zz
    r1 = (19 * c[1]) * (s2 - f[0] - jj)
    r2 = c[2] * (9 * f[0] - 7 * s1 - 2 * s2 + 5.5 * jj)
    t1, t2, pe = 2 * s[1] - (s[3] + s[5]), a + b - 2 * g, 3 * xx - jj
    v1, v2, we = s[3] - s[5], a - b, yy - zz
    r9, r10 = c[9] * (t1 + t2 - pe), c[10] * (t2 - 2 * t1 + 0.5 * pe)
    r11, r12 = c[11] * (v1 + v2 - we), c[12] * (v2 - 2 * v1 + 0.5 * we)
    r13 = c[13] * (s[7] - s[9] - jx * uy)
    r14 = c[14] * (s[15] - s[17] - jy * uz)
    r15 = c[15] * (s[11] - s[13] - jx * uz)
    r4 = (c[4] * 5 / 3) * (ax - 2 * d[1])
    r6 = (c[6] * 5 / 3) * (ay - 2 * d[3])
    r8 = (c[8] * 5 / 3) * (az - 2 * d[5])
    r16, r17, r18 = c[16] * (ax1 - ax2), c[17] * (ay2 - ay1), c[18] * (az1 - az2)
    ea, eb = -11 * r1 - 4 * r2, 8 * r1 + r2
    a9, a11 = r9 - 2 * r10, r11 - 2 * r12
    b9, b11 = r9 + r10, r11 + r12
    exy, exz, eyz = eb + b9 + b11, eb + b9 - b11, eb - 2 * b9
    even = {
        1: ea + 2 * a9, 3: ea - a9 + a11, 5: ea - a9 - a11,
        7: exy + r13, 9: exy - r13, 11: exz + r15, 13: exz - r15, 15: eyz + r14, 17: eyz - r14,
    }
    odd = {
        1: -4 * r4, 3: -4 * r6, 5: -4 * r8,
        7: (r4 + r6) + (r16 - r17), 9: (r4 - r6) + (r16 + r17),
        11: (r4 + r8) - (r16 - r18), 13: (r4 - r8) - (r16 + r18),
        15: (r6 + r8) + (r17 - r18), 17: (r6 - r8) + (r17 + r18),
    }
    out = [f[0] + 30 * r1 - 12 * r2]
    for q in range(1, 19, 2):
        out += [f[q] - even[q] - odd[q], f[q + 1] - even[q] + odd[q]]
    return out


def feq(h):
    rho = h[0]
    for q in range(1, Q):
        rho = rho + h[q]
    safe = jnp.where(rho > 0, rho, 1.0)
    u = []
    for axis in range(3):
        m = None
        for q in range(Q):
            if VEL[q][axis]:
                t = h[q] if VEL[q][axis] > 0 else -h[q]
                m = t if m is None else m + t
        u.append(m / safe)
    sq = u[0] * u[0] + u[1] * u[1] + u[2] * u[2]
    out = {}
    for q in CROSSING[2]:
        p = None
        for axis in range(3):
            if VEL[q][axis]:
                t = u[axis] if VEL[q][axis] > 0 else -u[axis]
                p = t if p is None else p + t
        n = sum(abs(e) for e in VEL[q])
        w = 1.0 / 18.0 if n == 1 else 1.0 / 36.0
        out[q] = w * rho * (1.0 + 3.0 * p + 4.5 * p * p - 1.5 * sq)
    return out


def lanes(rows):
    l = lax.broadcasted_iota(I32, (rows, LANES), 1)
    return l >= 64, (l >> 3) & 7, l & 7


def split(x):
    hi = x.astype(BF16)
    lo = (x - hi.astype(F32)).astype(BF16)
    return jnp.concatenate([hi, lo], axis=0)


def dot(a, b):
    return jnp.dot(a, b, preferred_element_type=F32)


def select_rows(row, offset, count):
    r = lax.broadcasted_iota(I32, (count, row.shape[1]), 0)
    hot = jnp.where(r == row - offset, 1.0, 0.0).astype(BF16)
    return jnp.concatenate([hot, hot], axis=1)


def spread_rows(flags):
    n = flags.shape[1]
    eye = lax.broadcasted_iota(I32, (n, n), 0) == lax.broadcasted_iota(I32, (n, n), 1)
    diag = jnp.where(eye, flags.astype(F32), 0.0).astype(BF16)
    return dot(diag, jnp.ones((n, LANES), BF16))


def sources(q, t, tiles, outer, half):
    ex = VEL[q][0]
    if ex == 0:
        return tiles[t]
    n = t - ex
    other = tiles[n] if 0 <= n < len(tiles) else outer
    return jnp.where(half, other, tiles[t]) if ex > 0 else jnp.where(half, tiles[t], other)


def roll(x, by):
    by %= LANES
    return pltpu.roll(x, by, 1) if by else x


def edges(q, t, count, half, j, k):
    ex, ey, ez = VEL[q]
    cx = None
    if ex > 0 and t == 0:
        cx = jnp.logical_not(half)
    if ex < 0 and t == count - 1:
        cx = half
    cy = None if ey == 0 else (j == (0 if ey > 0 else 7))
    cz = None if ez == 0 else (k == (0 if ez > 0 else 7))
    return cx, cy, cz


def face_of(axis, e):
    return 2 * axis + (1 if e > 0 else 0)


def bounce_bits(t, solid, absent):
    half, j, k = lanes(solid[0].shape[0])
    acc = jnp.where(solid[t] != 0, (1 << Q) - 1, 0)
    for q in range(1, Q):
        ex, ey, ez = VEL[q]
        v = roll(sources(q, t, solid, solid[t], half), 64 * abs(ex) + 8 * ey + ez)
        sides = zip(edges(q, t, len(solid), half, j, k), (ex, ey, ez), range(3))
        crossed = [c for c in sides if c[0] is not None]
        for c, e, axis in crossed:
            v = jnp.where(c, absent[face_of(axis, e)], v)
        for i in range(len(crossed)):
            for m in range(i):
                v = jnp.where(crossed[i][0] & crossed[m][0], 1, v)
        acc = acc | (jnp.where(v != 0, 1, 0) << q)
    return acc


def absences(nbr_ref, ifc_ref):
    out = []
    for d in range(6):
        there = nbr_ref[d : d + 1, :] >= 0
        if d == 2:
            there = there | (ifc_ref[0:1, :] >= 0)
        out.append((1.0 - spread_rows(jnp.where(there, 1.0, 0.0))).astype(I32))
    return out


def local_hots(nbr_ref, first):
    n = nbr_ref.shape[1]
    return [select_rows(nbr_ref[(d ^ 1) : (d ^ 1) + 1, :], first, n) for d in range(6)]


def send_rows(row, first, count, cap):
    rel = row - first
    gone = (rel >= 0) & (rel < count)
    rel = jnp.where(gone, rel, 255)
    ahead = spread_rows(rel)[:, :count] < rel.astype(F32)
    rank = jnp.sum(jnp.where(ahead, 1.0, 0.0), axis=0, keepdims=True)
    r = lax.broadcasted_iota(I32, (cap, count), 0).astype(F32)
    hot = jnp.where((r == rank) & gone, 1.0, 0.0).astype(BF16)
    return jnp.concatenate([hot, hot], axis=1)


def take_rows(row, first, count, cap):
    rel = row - first
    gone = jnp.where((rel >= 0) & (rel < count), 1.0, 0.0)
    b = lax.broadcasted_iota(I32, (count, count), 0)
    a = lax.broadcasted_iota(I32, (count, count), 1)
    rank = dot(jnp.where(a < b, gone, 0.0).astype(BF16), jnp.ones((count, LANES), BF16))[:, :cap]
    there = spread_rows(gone)[:, :cap] > 0.5
    r = lax.broadcasted_iota(I32, (count, cap), 1).astype(F32)
    hot = jnp.where((r == rank) & there, 1.0, 0.0).astype(BF16)
    return jnp.concatenate([hot, hot], axis=1)


def coarse_code(ifc_ref, position, count):
    c = ifc_ref[0:1, :]
    code = jnp.where(c >= 0, 2 + 4 * (c - (position + 1) * count) + ifc_ref[1:2, :], 1)
    return spread_rows(code)


def far_row(c, s, count):
    return 5 * count + 5 * (c // 2) + s


def pack_kernel(part_ref, co_ref, far_co_ref, send_ref, near_ref):
    refs = (co_ref, far_co_ref)
    count = co_ref.shape[0]
    n = part_ref.shape[0]
    send_ref[:n] = part_ref[...]
    h = []
    for q in range(Q):
        h0 = jnp.concatenate([r[:, q, 0, :] for r in refs], axis=0)
        h1 = (1.0 - 0.5) * h0 + 0.5 * jnp.concatenate([r[:, q, 1, :] for r in refs], axis=0)
        h.append(jnp.concatenate([h0, h1], axis=1))
    e = feq(h)
    send_ref[n] = jnp.zeros_like(send_ref[n])
    near_ref[...] = jnp.zeros_like(near_ref)
    upper = lanes(1)[0]
    for s, q in enumerate(CROSSING[2]):
        v = e[q] + (0.6 / 1.1) * (h[q] - e[q])
        for c in range(count):
            send_ref[n, 5 * c + s : 5 * c + s + 1, :] = v[c : c + 1]
            near_ref[5 * c + s : 5 * c + s + 1, :] = v[count + c : count + c + 1]
        turned = roll(v, 64)
        for c in range(0, count, 2):
            other = min(c + 1, count - 1)
            to = far_row(c, s, count)
            send_ref[n, to : to + 1, :] = jnp.where(upper, turned[count + other : count + other + 1], v[count + c : count + c + 1])


def both_halves(x, upper):
    half = lanes(x.shape[0])[0]
    return jnp.where(half, x, roll(x, 64)) if upper else jnp.where(half, roll(x, 64), x)


def spread_matrix(tiles):
    kk = lax.broadcasted_iota(I32, (256, LANES), 0)
    ll = lax.broadcasted_iota(I32, (256, LANES), 1)
    w, m, k = kk >> 6, kk & 63, ll & 7
    out = []
    for t in range(tiles + 1):
        i = (ll >> 6) * 7 if t == tiles else 2 * t + (ll >> 6)
        want = 8 * (4 * (w >> 1) + (i >> 1)) + 4 * (w & 1) + (k >> 1)
        out.append(jnp.where(m == want, 1.0, 0.0).astype(BF16))
    return out


def rows_of(cg):
    return lambda c, s: cg[5 * c + s : 5 * c + s + 1, :]


def coarse_rows(code, cg, count):
    half = lanes(code.shape[0])[0]
    hi, lo = [], []
    for s in range(5):
        parts = []
        for pair in (0, 2):
            acc = jnp.zeros_like(code)
            for c in range(count):
                want = jnp.where(half, 3.0 + 4 * c + pair, 2.0 + 4 * c + pair)
                acc = jnp.where(code == want, cg(c, s), acc)
            parts.append(acc)
        x = jnp.concatenate(parts, axis=1)
        h = x.astype(BF16)
        hi.append(h)
        lo.append((x - h.astype(F32)).astype(BF16))
    return jnp.concatenate(hi + lo, axis=0)


def coarse_tile(rows, matrix):
    g = dot(rows, matrix)
    n = g.shape[0] // 2
    g = g[:n] + g[n:]
    b = n // 5
    return [g[b * s : b * (s + 1)] for s in range(5)]


def pull(q, t, x, parts, gx, bits, bounced):
    if q == 0:
        return x[t]
    half, j, k = lanes(bits.shape[0])
    ex, ey, ez = VEL[q]
    turn = 64 * abs(ex)
    out = roll(sources(q, t, x, gx, half), turn + 8 * ey + ez)
    _, cy, cz = edges(q, t, len(x), half, j, k)
    if ey:
        g = parts[1]
        out = jnp.where(cy, roll(sources(q, t, g, g[t], half), turn - 56 * ey + ez), out)
    if ez:
        g = parts[2]
        out = jnp.where(cz, roll(sources(q, t, g, g[t], half), turn + 8 * ey - 7 * ez), out)
    return jnp.where((bits & (1 << q)) != 0, bounced, out)


def gathers(q, x, hot, fine, remote):
    ex, ey, ez = VEL[q]
    gx, gy, gz = None, None, None
    if q:
        parts = [split(v) for v in x]
    if ex:
        gx = dot(hot[face_of(0, ex)], parts[0 if ex < 0 else len(x) - 1])
        if remote is not None:
            gx = gx + remote[q]
    if ey:
        gy = [dot(hot[face_of(1, ey)], p) for p in parts]
        if ey < 0 and fine is not None:
            s = CROSSING[2].index(q)
            gy = [g + fine(s, t) for t, g in enumerate(gy)]
    if ez:
        gz = [dot(hot[face_of(2, ez)], p) for p in parts]
    return gx, gy, gz


def corners(q, half, j, k):
    _, cy, cz = edges(q, 0, 0, half, j, k)
    return cy if cz is None else (cz if cy is None else cy | cz)


def groups(blocks):
    return [slice(g, g + 8) for g in range(0, blocks, 8)]


def prepare_side(side, load, nbr_ref, solid, bits_put, post_ref, send_ref, hot, absent, code, first, ready=None):
    tiles = len(solid)
    blocks = solid[0].shape[0]
    t = tiles - 1 if side == 0 else 0
    half, j, k = lanes(blocks)
    bits = bounce_bits(t, solid, absent)
    bits_put(t, bits)
    if ready is not None:
        ready()

    for r in groups(blocks):
        out = kept([load(q, r, t) for q in range(Q)], solid[t][r] != 0)
        for q in range(Q):
            post_ref[side, q, r, :] = out[q]
    to = send_rows(nbr_ref[side : side + 1, :], first + (blocks if side == 0 else -blocks), blocks, send_ref.shape[1])
    actual = list(range(Q)) if side == 1 else MIRROR
    streamed = []
    for c in LAYER:
        q = actual[c]
        ex, ey, ez = VEL[q]
        x = post_ref[side, q]
        turn = 64 * abs(ex)
        out = roll(x, turn + 8 * ey + ez)
        _, cy, cz = edges(q, t, tiles, half, j, k)
        if ey or ez:
            parts = split(x)
        if ey:
            out = jnp.where(cy, roll(dot(hot[face_of(1, ey)], parts), turn - 56 * ey + ez), out)
        if ez:
            out = jnp.where(cz, roll(dot(hot[face_of(2, ez)], parts), turn + 8 * ey - 7 * ez), out)
        if q:
            out = jnp.where((bits & (1 << q)) != 0, post_ref[side, OPP[q]], out)
        streamed.append((c, out))
    for c in range(Q):
        corner = corners(c, half, j, k)
        if VEL[c][0] > 0 and corner is not None:
            streamed.append((c, jnp.where(corner, post_ref[side, OPP[actual[c]]], 0.0)))
    slots = [post_ref[side, actual[c]] for c in FACE] + shares(streamed) + [code]
    for s in range(0, len(slots), 2):
        a, b = slots[s], slots[min(s + 1, len(slots) - 1)]
        packed = jnp.where(half, b, roll(a, 64)) if side == 0 else jnp.where(half, roll(b, 64), a)
        send_ref[s // 2] = dot(to, split(packed))


def outer_kernel(pop_hbm, *refs):
    given, (post_ref, bits_ref, co_ref, send_ref), (tile_ref, *small_refs, sem) = refs[:4], refs[4:8], refs[8:]
    nbr_ref, ifc_ref, solid_ref = small_refs
    position = lax.axis_index("blk")
    blocks = solid_ref.shape[0]
    tiles = solid_ref.shape[1] // LANES
    even = position % 2 == 0
    mine = pl.ds(pl.multiple_of(jnp.where(even, 0, LANES * (tiles - 1)), LANES), LANES)
    pairs = [(pop_hbm.at[:, :, mine], tile_ref), *zip(given, (*small_refs, co_ref))]
    copies = [pltpu.make_async_copy(a, b, sem.at[i]) for i, (a, b) in enumerate(pairs)]
    for copy in copies[1:] + copies[:1]:
        copy.start()
    for copy in copies[1:]:
        copy.wait()
    first = position * blocks
    code = coarse_code(ifc_ref, position, co_ref.shape[0])
    absent = absences(nbr_ref, ifc_ref)
    hot = local_hots(nbr_ref, first)
    solid = [solid_ref[:, LANES * t : LANES * (t + 1)] for t in range(tiles)]

    def load(q, r, t):
        return tile_ref[q, r, :]

    def put(t, bits):
        bits_ref[...] = bits

    for side in (0, 1):

        @pl.when(position % 2 == 1 - side)
        def _(side=side):
            prepare_side(side, load, nbr_ref, solid, put, post_ref, send_ref, hot, absent, code, first, copies[0].wait)


def inner_kernel(pop_ref, nbr_ref, ifc_ref, solid_ref, ahead_ref, abits_ref, cur_ref, bits_ref, code_ref, spread_ref, take_ref, send_ref, own_ref, hot_ref, mid_ref, outer_ref, *, count):
    position = lax.axis_index("blk")
    blocks = solid_ref.shape[0]
    tiles = solid_ref.shape[1] // LANES
    first = position * blocks
    span = [slice(LANES * t, LANES * (t + 1)) for t in range(tiles)]
    code = coarse_code(ifc_ref, position, count)
    code_ref[...] = code
    absent = absences(nbr_ref, ifc_ref)
    hot = local_hots(nbr_ref, first)
    solid = [solid_ref[:, span[t]] for t in range(tiles)]

    def load(q, r, t):
        return pop_ref[q, r, span[t]]

    def put(t, bits):
        bits_ref[:, span[t]] = bits

    for t, m in enumerate(spread_matrix(tiles)):
        spread_ref[t] = m
    cap = take_ref.shape[2] // 2
    take_ref[0] = take_rows(nbr_ref[0:1, :], first + blocks, blocks, cap)
    take_ref[1] = take_rows(nbr_ref[1:2, :], first - blocks, blocks, cap)
    for t in range(1, tiles - 1):
        put(t, bounce_bits(t, solid, absent))
    for side in (0, 1):

        @pl.when(position % 2 == side)
        def _(side=side):
            prepare_side(side, load, nbr_ref, solid, put, outer_ref, send_ref, hot, absent, code, first)
            outer_ref[1 - side] = ahead_ref[1 - side]
            put(0 if side == 0 else tiles - 1, abits_ref[...])

    for t in range(1, tiles - 1):
        for r in groups(blocks):
            out = kept([pop_ref[q, r, span[t]] for q in range(Q)], solid[t][r] != 0)
            for q in range(Q):
                mid_ref[t - 1, q, r, :] = out[q]

    for d in range(6):
        hot_ref[d] = hot[d]
    half, j, k = lanes(blocks)
    items = []
    for q in range(Q):
        if VEL[q][0] > 0:
            turn = 64 + 8 * VEL[q][1] + VEL[q][2]
            v = jnp.where(half, roll(outer_ref[1, MIRROR[q]], turn), roll(outer_ref[0, q], turn))
            corner = corners(q, half, j, k)
            items.append((q, v if corner is None else jnp.where(corner, 0.0, v)))
    for i, v in enumerate(shares(items)):
        own_ref[i] = v

    def post(q, t):
        if t == 0:
            return outer_ref[1, q]
        return outer_ref[0, q] if t == tiles - 1 else mid_ref[t - 1, q]

    for q in range(Q):
        x = [post(q, t) for t in range(tiles)]
        ghosts = gathers(q, x, hot, None, None)
        for t in range(tiles):
            cur_ref[q, :, span[t]] = pull(
                q, t, x, ghosts, ghosts[0], bits_ref[:, span[t]], post(OPP[q], t)
            )


def current_kernel(cur_ref, own_ref, code_ref, spread_ref, take_ref, near_ref, bits_ref, ra_ref, rb_ref, post_ref, fine_ref, ghost_ref, codes_ref, got_ref, now_ref, *, count):
    position = lax.axis_index("blk")
    blocks, cells = cur_ref.shape[1:]
    tiles = cells // LANES
    even = position % 2 == 0
    half, j, k = lanes(blocks)
    span = [slice(LANES * t, LANES * (t + 1)) for t in range(tiles)]
    n = ra_ref.shape[0]

    for s in range(n):
        got_ref[0, s] = dot(take_ref[0], split(jnp.where(even, ra_ref[s], rb_ref[s])))
        got_ref[1, s] = dot(take_ref[1], split(jnp.where(even, rb_ref[s], ra_ref[s])))

    def from_next(s):
        return got_ref[0, s // 2] if s % 2 == 0 else roll(got_ref[0, s // 2], 64)

    def from_prev(s):
        return got_ref[1, s // 2] if s % 2 == 1 else roll(got_ref[1, s // 2], 64)

    up = {q: from_next(s) for s, q in enumerate(FACE)}
    low = {MIRROR[q]: from_prev(s) for s, q in enumerate(FACE)}
    code = code_ref[...]
    up_code = both_halves(from_next(14), False)
    low_code = both_halves(from_prev(14), True)
    codes_ref[0] = up_code
    codes_ref[1] = low_code
    near = jnp.where(even, near_ref[...], rb_ref[n])

    rows = coarse_rows(code, rows_of(both_halves(near, False)), count)
    for t in range(tiles):
        for s, v in enumerate(coarse_tile(rows, spread_ref[t])):
            fine_ref[s, :, span[t]] = v
    for q in range(Q):
        ex, ey, ez = VEL[q]
        for t in range(tiles):
            v = cur_ref[q, :, span[t]]
            cx, cy, cz = edges(q, t, tiles, half, j, k)
            if ey < 0:
                f = [fine_ref[CROSSING[2].index(q), :, span[m]] for m in range(tiles)]
                g = roll(sources(q, t, f, f[t], half), 64 * abs(ex) - 56 * ey + ez)
                ok = cy
                if cx is not None:
                    ok = ok & jnp.logical_not(cx)
                if cz is not None:
                    ok = ok & jnp.logical_not(cz)
                v = v + jnp.where(ok, g, 0.0)
            if cx is not None:
                ok = cx
                for c in (cy, cz):
                    if c is not None:
                        ok = ok & jnp.logical_not(c)
                v = v + jnp.where(ok, roll(up[q] if ex < 0 else low[q], 64 + 8 * ey + ez), 0.0)
            now_ref[q, :, span[t]] = v

    for i in range(9):
        ghost_ref[i] = own_ref[i] + jnp.where(half, from_prev(5 + i), from_next(5 + i))

    for t in range(tiles):
        for r in groups(blocks):
            out = kept([now_ref[q, r, span[t]] for q in range(Q)], (bits_ref[r, span[t]] & 1) != 0)
            for q in range(Q):
                post_ref[q, r, span[t]] = out[q]

    rows = coarse_rows(code, rows_of(both_halves(near, True)), count)
    for t in range(tiles):
        for s, v in enumerate(coarse_tile(rows, spread_ref[t])):
            fine_ref[s, :, span[t]] = v


def final_kernel(post_ref, fine_ref, half_ref, codes_ref, bits_ref, spread_ref, sb_ref, rb_ref, relay_ref, hot_ref, out_ref, buf_ref, sem, *, count):
    position = lax.axis_index("blk")
    blocks, cells = bits_ref.shape
    tiles = cells // LANES
    half, j, k = lanes(blocks)
    span = [slice(LANES * t, LANES * (t + 1)) for t in range(tiles)]
    hot = [hot_ref[d] for d in range(6)]
    copies = []

    def emit(q, remote):
        x = [post_ref[q, :, span[t]] for t in range(tiles)]
        ghosts = gathers(q, x, hot, lambda s, t: fine_ref[s, :, span[t]], remote)
        for t in range(tiles):
            buf_ref[q, :, span[t]] = pull(
                q, t, x, ghosts, ghosts[0], bits_ref[:, span[t]], post_ref[OPP[q], :, span[t]]
            )
        copy = pltpu.make_async_copy(buf_ref.at[q], out_ref.at[q], sem.at[q])
        copy.start()
        copies.append(copy)

    for q in range(Q):
        if VEL[q][0] == 0:
            emit(q, None)
    n = rb_ref.shape[0] - 1
    handed = rows_of(both_halves(relay_ref[0], False))
    direct = [both_halves(rb_ref[n], u) for u in (False, True)]

    def far(c, s):
        row = far_row(c, s, count)
        return jnp.where(position % 2 == 0, handed(c, s), direct[c % 2][row : row + 1])

    up_rows = coarse_rows(codes_ref[0], far, count)
    up_fine = coarse_tile(up_rows, spread_ref[tiles])
    low_rows = coarse_rows(codes_ref[1], rows_of(both_halves(sb_ref[n], False)), count)
    low_fine = coarse_tile(low_rows, spread_ref[tiles])
    items = []
    for q in MIXED:
        _, cy, cz = edges(q, 0, tiles, half, j, k)
        ok = cy if cz is None else cy & jnp.logical_not(cz)
        v = jnp.where(half, low_fine[CROSSING[2].index(MIRROR[q])], up_fine[CROSSING[2].index(q)])
        items.append((q, jnp.where(ok, roll(v, VEL[q][2]), 0.0)))
    parts = [half_ref[i] + v for i, v in enumerate(shares(items))]
    remote = {}
    for q, v in finish(parts).items():
        remote[q] = jnp.where(codes_ref[0] > 0.5, v, 0.0)
        remote[MIRROR[q]] = jnp.where(codes_ref[1] > 0.5, v, 0.0)
    for q in range(Q):
        if VEL[q][0]:
            emit(q, remote)
    for copy in copies:
        copy.wait()


def swapped(x, off):
    n = lax.axis_size("blk")
    low = [(i, i + 1) for i in range(off, n - 1, 2)]
    return lax.ppermute(x, "blk", low + [(b, a) for a, b in low])


def held(x):
    return pltpu.with_memory_space_constraint(x, pltpu.VMEM)


def body(populations, coarse_faces, neighbors, interface, solid):
    pop = populations.transpose(1, 0, 2)
    co = coarse_faces.transpose(0, 2, 1, 3)
    nbr, ifc = neighbors.T, interface.T
    blocks, cells = pop.shape[1:]
    count = co.shape[0]
    tiles = cells // LANES
    dense = pl.BlockSpec(memory_space=pltpu.VMEM)
    away = pl.BlockSpec(memory_space=pl.ANY)
    cap = blocks // 2
    room = pltpu.CompilerParams(vmem_limit_bytes=20 << 20)
    sides = pltpu.VMEM((2, Q, blocks, LANES), F32)
    payload = pltpu.VMEM((8, cap, LANES), F32)
    small = (nbr, ifc, solid)
    far_co = swapped(co, 0)
    outer = pl.pallas_call(
        outer_kernel,
        in_specs=[away] * 5,
        out_shape=(sides, pltpu.VMEM((blocks, LANES), I32), pltpu.VMEM(co.shape, F32), payload),
        scratch_shapes=[
            pltpu.VMEM((Q, blocks, LANES), F32),
            *(pltpu.VMEM(a.shape, a.dtype) for a in small),
            pltpu.SemaphoreType.DMA((5,)),
        ],
        compiler_params=pltpu.CompilerParams(vmem_limit_bytes=56 << 20),
        cost_estimate=pl.CostEstimate(flops=20_000_000, bytes_accessed=1_000_000, transcendentals=0),
        name="outer",
    )
    ahead, abits, co, part = outer(pop, *small, co)
    sb, near = pl.pallas_call(
        pack_kernel,
        in_specs=[dense] * 3,
        out_shape=(pltpu.VMEM((9, cap, LANES), F32), pltpu.VMEM((cap, LANES), F32)),
        compiler_params=room,
        name="pack",
    )(held(part), held(co), held(far_co))
    rb = swapped(sb, 1)
    ahead, abits = held(ahead), held(abits)
    inner = pl.pallas_call(
        functools.partial(inner_kernel, count=count),
        in_specs=[dense] * 6,
        out_shape=(
            pltpu.VMEM((Q, blocks, cells), F32),
            pltpu.VMEM((blocks, cells), I32),
            pltpu.VMEM((blocks, LANES), F32),
            pltpu.VMEM((tiles + 1, 256, LANES), BF16),
            pltpu.VMEM((2, blocks, 2 * cap), BF16),
            payload,
            pltpu.VMEM((9, blocks, LANES), F32),
            pltpu.VMEM((6, blocks, 2 * blocks), BF16),
        ),
        scratch_shapes=[pltpu.VMEM((tiles - 2, Q, blocks, LANES), F32), sides],
        compiler_params=room,
        cost_estimate=pl.CostEstimate(flops=100_000_000, bytes_accessed=4_000_000, transcendentals=0),
        name="inner",
    )
    cur, bits, code, spread, take, sa, own, hots = inner(pop, nbr, ifc, solid, ahead, abits)
    ra = swapped(sa, 0)
    relay = swapped(rb[-1:], 0)
    state = pltpu.VMEM((Q, blocks, cells), F32)
    layer = pltpu.VMEM((9, blocks, LANES), F32)
    current = pl.pallas_call(
        functools.partial(current_kernel, count=count),
        in_specs=[dense] * 9,
        out_shape=(state, pltpu.VMEM((5, blocks, cells), F32), layer, pltpu.VMEM((2, blocks, LANES), F32)),
        scratch_shapes=[pltpu.VMEM((2, 8, blocks, LANES), F32), state],
        compiler_params=room,
        cost_estimate=pl.CostEstimate(flops=100_000_000, bytes_accessed=4_000_000, transcendentals=0),
        name="current",
    )
    given = [held(x) for x in (cur, own, code, spread, take, near, bits, ra, rb)]
    post, fine, ghost, codes = current(*given)
    out = pl.pallas_call(
        functools.partial(final_kernel, count=count),
        in_specs=[dense] * 10,
        out_specs=away,
        out_shape=jax.ShapeDtypeStruct(pop.shape, F32),
        scratch_shapes=[state, pltpu.SemaphoreType.DMA((Q,))],
        compiler_params=room,
        name="final",
    )(*(held(x) for x in (post, fine, ghost, codes, bits, spread, sb, rb, relay, hots)))
    return out.transpose(1, 0, 2)


def solution(mesh):
    placed = (P("blk", None, None), P("blk", None, None, None), P("blk", None), P("blk", None), P("blk", None))
    return jax.shard_map(body, mesh=mesh, in_specs=placed, out_specs=P("blk", None, None), check_vma=False)
```

```python
import functools

import jax
import jax.numpy as jnp
import numpy as np
from jax import lax
from jax.experimental import pallas as pl
from jax.experimental.pallas import tpu as pltpu
from jax.sharding import PartitionSpec as P


F32, BF16, I32 = jnp.float32, jnp.bfloat16, jnp.int32
LANES = 128
VEL = [
    (0, 0, 0),
    (1, 0, 0), (-1, 0, 0), (0, 1, 0), (0, -1, 0), (0, 0, 1), (0, 0, -1),
    (1, 1, 0), (-1, -1, 0), (1, -1, 0), (-1, 1, 0),
    (1, 0, 1), (-1, 0, -1), (1, 0, -1), (-1, 0, 1),
    (0, 1, 1), (0, -1, -1), (0, 1, -1), (0, -1, 1),
]
Q = len(VEL)
OPP = [VEL.index((-x, -y, -z)) for x, y, z in VEL]
CROSSING = [
    [q for q in range(Q) if VEL[q][d // 2] == (-1 if d % 2 == 0 else 1)] for d in range(6)
]


MIRROR = [VEL.index((-x, y, z)) for x, y, z in VEL]
FACE = CROSSING[0]
LAYER = [q for q in range(Q) if VEL[q][0] <= 0]
CODED = VEL.index((-1, -1, 0))
MIXED = [q for q in LAYER if VEL[q][1] < 0]


def moments():
    v = np.array(VEL) * 1.0
    x, y, z = v[:, 0], v[:, 1], v[:, 2]
    s = x * x + y * y + z * z
    rows = [
        np.ones(19), 19 * s - 30, (21 * s * s - 53 * s + 24) / 2,
        x, (5 * s - 9) * x, y, (5 * s - 9) * y, z, (5 * s - 9) * z,
        3 * x * x - s, (3 * s - 5) * (3 * x * x - s),
        y * y - z * z, (3 * s - 5) * (y * y - z * z),
        x * y, y * z, x * z,
        (y * y - z * z) * x, (z * z - x * x) * y, (x * x - y * y) * z,
    ]
    return np.stack(rows)


def rates():
    norms = (moments() ** 2).sum(1)
    w = 1.0 / 0.6
    relax = np.array([0, 1.19, 1.4, 0, 1.2, 0, 1.2, 0, 1.2, w, 1.4, w, 1.4, w, w, w, 1.98, 1.98, 1.98])
    return [float(c) for c in relax / norms]


def kept(f, wall):
    out = collide(f)
    return [jnp.where(wall, f[OPP[q]], out[q]) for q in range(Q)]


def linear(p, items):
    m = moments()
    row = np.eye(Q)[p] - (m.T @ (np.array(rates())[:, None] * m))[p]
    same = {}
    for q, v in items:
        if abs(row[q]) > 1e-12:
            same.setdefault(round(abs(float(row[q])), 10), []).append((row[q] > 0, abs(float(row[q])), v))
    total = None
    for terms in same.values():
        part = None
        for plus, _, v in terms:
            if part is None:
                part = v if plus else -v
            else:
                part = part + v if plus else part - v
        part = terms[0][1] * part
        total = part if total is None else total + part
    return total


def shares(items):
    out = [linear(p, items) for p in FACE]
    total = None
    for _, v in items:
        total = v if total is None else total + v
    out.append(total)
    for axis in range(3):
        total = None
        for q, v in items:
            if VEL[q][axis]:
                v = v if VEL[q][axis] > 0 else -v
                total = v if total is None else total + v
        out.append(total)
    return out


def finish(parts):
    c = rates()
    rho, jx, jy, jz = parts[5:]
    inv = 1.0 / rho
    ux, uy, uz = jx * inv, jy * inv, jz * inv
    xx, yy, zz = jx * ux, jy * uy, jz * uz
    jj = xx + yy + zz
    pe, we = 3 * xx - jj, yy - zz
    r1, r2 = c[1] * (19 * jj - 11 * rho), c[2] * (3 * rho - 5.5 * jj)
    r4, r6, r8 = (c[4] * -2 / 3) * jx, (c[6] * -2 / 3) * jy, (c[8] * -2 / 3) * jz
    r13, r15 = c[13] * (jx * uy), c[15] * (jx * uz)
    ea, eb = -11 * r1 - 4 * r2, 8 * r1 + r2
    b9, b11 = (c[9] - 0.5 * c[10]) * pe, (c[11] - 0.5 * c[12]) * we
    exy, exz = eb + b9 + b11, eb + b9 - b11
    own = {
        (-1, 0, 0): ea + (2 * (c[9] + c[10])) * pe + 4 * r4,
        (-1, -1, 0): exy + r13 - (r4 + r6), (-1, 1, 0): exy - r13 - (r4 - r6),
        (-1, 0, -1): exz + r15 - (r4 + r8), (-1, 0, 1): exz - r15 - (r4 - r8),
    }
    return {p: parts[i] + own[VEL[p]] for i, p in enumerate(FACE)}


def collide(f):
    c = rates()
    s = {q: f[q] + f[q + 1] for q in range(1, 19, 2)}
    d = {q: f[q] - f[q + 1] for q in range(1, 19, 2)}
    a, b, g = s[7] + s[9], s[11] + s[13], s[15] + s[17]
    s1, s2 = s[1] + (s[3] + s[5]), a + b + g
    rho = f[0] + s1 + s2
    ax1, ax2 = d[7] + d[9], d[11] + d[13]
    ay1, ay2 = d[7] - d[9], d[15] + d[17]
    az1, az2 = d[11] - d[13], d[15] - d[17]
    ax, ay, az = ax1 + ax2, ay1 + ay2, az1 + az2
    jx, jy, jz = d[1] + ax, d[3] + ay, d[5] + az
    inv = 1.0 / rho
    ux, uy, uz = jx * inv, jy * inv, jz * inv
    xx, yy, zz = jx * ux, jy * uy, jz * uz
    jj = xx + yy + zz
    r1 = (19 * c[1]) * (s2 - f[0] - jj)
    r2 = c[2] * (9 * f[0] - 7 * s1 - 2 * s2 + 5.5 * jj)
    t1, t2, pe = 2 * s[1] - (s[3] + s[5]), a + b - 2 * g, 3 * xx - jj
    v1, v2, we = s[3] - s[5], a - b, yy - zz
    r9, r10 = c[9] * (t1 + t2 - pe), c[10] * (t2 - 2 * t1 + 0.5 * pe)
    r11, r12 = c[11] * (v1 + v2 - we), c[12] * (v2 - 2 * v1 + 0.5 * we)
    r13 = c[13] * (s[7] - s[9] - jx * uy)
    r14 = c[14] * (s[15] - s[17] - jy * uz)
    r15 = c[15] * (s[11] - s[13] - jx * uz)
    r4 = (c[4] * 5 / 3) * (ax - 2 * d[1])
    r6 = (c[6] * 5 / 3) * (ay - 2 * d[3])
    r8 = (c[8] * 5 / 3) * (az - 2 * d[5])
    r16, r17, r18 = c[16] * (ax1 - ax2), c[17] * (ay2 - ay1), c[18] * (az1 - az2)
    ea, eb = -11 * r1 - 4 * r2, 8 * r1 + r2
    a9, a11 = r9 - 2 * r10, r11 - 2 * r12
    b9, b11 = r9 + r10, r11 + r12
    exy, exz, eyz = eb + b9 + b11, eb + b9 - b11, eb - 2 * b9
    even = {
        1: ea + 2 * a9, 3: ea - a9 + a11, 5: ea - a9 - a11,
        7: exy + r13, 9: exy - r13, 11: exz + r15, 13: exz - r15, 15: eyz + r14, 17: eyz - r14,
    }
    odd = {
        1: -4 * r4, 3: -4 * r6, 5: -4 * r8,
        7: (r4 + r6) + (r16 - r17), 9: (r4 - r6) + (r16 + r17),
        11: (r4 + r8) - (r16 - r18), 13: (r4 - r8) - (r16 + r18),
        15: (r6 + r8) + (r17 - r18), 17: (r6 - r8) + (r17 + r18),
    }
    out = [f[0] + 30 * r1 - 12 * r2]
    for q in range(1, 19, 2):
        out += [f[q] - even[q] - odd[q], f[q + 1] - even[q] + odd[q]]
    return out


def feq(h):
    rho = h[0]
    for q in range(1, Q):
        rho = rho + h[q]
    inv = 1.0 / jnp.where(rho > 0, rho, 1.0)
    u = []
    for axis in range(3):
        m = None
        for q in range(Q):
            if VEL[q][axis]:
                t = h[q] if VEL[q][axis] > 0 else -h[q]
                m = t if m is None else m + t
        u.append(m * inv)
    sq = u[0] * u[0] + u[1] * u[1] + u[2] * u[2]
    out = {}
    for q in CROSSING[2]:
        p = None
        for axis in range(3):
            if VEL[q][axis]:
                t = u[axis] if VEL[q][axis] > 0 else -u[axis]
                p = t if p is None else p + t
        n = sum(abs(e) for e in VEL[q])
        w = 1.0 / 18.0 if n == 1 else 1.0 / 36.0
        out[q] = w * rho * (1.0 + 3.0 * p + 4.5 * p * p - 1.5 * sq)
    return out


def lanes(rows):
    l = lax.broadcasted_iota(I32, (rows, LANES), 1)
    return l >= 64, (l >> 3) & 7, l & 7


def split(x):
    hi = x.astype(BF16)
    lo = (x - hi.astype(F32)).astype(BF16)
    return jnp.concatenate([hi, lo], axis=0)


def dot(a, b):
    return jnp.dot(a, b, preferred_element_type=F32)


def select_rows(row, offset, count):
    r = lax.broadcasted_iota(I32, (count, row.shape[1]), 0)
    hot = jnp.where(r == row - offset, 1.0, 0.0).astype(BF16)
    return jnp.concatenate([hot, hot], axis=1)


def spread_rows(flags):
    n = flags.shape[1]
    eye = lax.broadcasted_iota(I32, (n, n), 0) == lax.broadcasted_iota(I32, (n, n), 1)
    diag = jnp.where(eye, flags.astype(F32), 0.0).astype(BF16)
    return dot(diag, jnp.ones((n, LANES), BF16))


def sources(q, t, tiles, outer, half):
    ex = VEL[q][0]
    if ex == 0:
        return tiles[t]
    n = t - ex
    other = tiles[n] if 0 <= n < len(tiles) else outer
    return jnp.where(half, other, tiles[t]) if ex > 0 else jnp.where(half, tiles[t], other)


def roll(x, by):
    by %= LANES
    return pltpu.roll(x, by, 1) if by else x


def edges(q, t, count, half, j, k):
    ex, ey, ez = VEL[q]
    cx = None
    if ex > 0 and t == 0:
        cx = jnp.logical_not(half)
    if ex < 0 and t == count - 1:
        cx = half
    cy = None if ey == 0 else (j == (0 if ey > 0 else 7))
    cz = None if ez == 0 else (k == (0 if ez > 0 else 7))
    return cx, cy, cz


def face_of(axis, e):
    return 2 * axis + (1 if e > 0 else 0)


def bounce_bits(t, solid, absent):
    half, j, k = lanes(solid[0].shape[0])
    acc = jnp.where(solid[t] != 0, (1 << Q) - 1, 0)
    for q in range(1, Q):
        ex, ey, ez = VEL[q]
        v = roll(sources(q, t, solid, solid[t], half), 64 * abs(ex) + 8 * ey + ez)
        sides = zip(edges(q, t, len(solid), half, j, k), (ex, ey, ez), range(3))
        crossed = [c for c in sides if c[0] is not None]
        for c, e, axis in crossed:
            v = jnp.where(c, absent[face_of(axis, e)], v)
        for i in range(len(crossed)):
            for m in range(i):
                v = jnp.where(crossed[i][0] & crossed[m][0], 1, v)
        acc = acc | (jnp.where(v != 0, 1, 0) << q)
    return acc


def absences(nbr_ref, ifc_ref):
    out = []
    for d in range(6):
        there = nbr_ref[d : d + 1, :] >= 0
        if d == 2:
            there = there | (ifc_ref[0:1, :] >= 0)
        out.append((1.0 - spread_rows(jnp.where(there, 1.0, 0.0))).astype(I32))
    return out


def local_hots(nbr_ref, first):
    n = nbr_ref.shape[1]
    return [select_rows(nbr_ref[(d ^ 1) : (d ^ 1) + 1, :], first, n) for d in range(6)]


def send_rows(row, first, count, cap):
    rel = row - first
    gone = (rel >= 0) & (rel < count)
    rel = jnp.where(gone, rel, 255)
    ahead = spread_rows(rel)[:, :count] < rel.astype(F32)
    rank = jnp.sum(jnp.where(ahead, 1.0, 0.0), axis=0, keepdims=True)
    r = lax.broadcasted_iota(I32, (cap, count), 0).astype(F32)
    hot = jnp.where((r == rank) & gone, 1.0, 0.0).astype(BF16)
    return jnp.concatenate([hot, hot], axis=1)


def take_rows(row, first, count, cap):
    rel = row - first
    gone = jnp.where((rel >= 0) & (rel < count), 1.0, 0.0)
    b = lax.broadcasted_iota(I32, (count, count), 0)
    a = lax.broadcasted_iota(I32, (count, count), 1)
    rank = dot(jnp.where(a < b, gone, 0.0).astype(BF16), jnp.ones((count, LANES), BF16))[:, :cap]
    there = spread_rows(gone)[:, :cap] > 0.5
    r = lax.broadcasted_iota(I32, (count, cap), 1).astype(F32)
    hot = jnp.where((r == rank) & there, 1.0, 0.0).astype(BF16)
    return jnp.concatenate([hot, hot], axis=1)


def coarse_code(ifc_ref, position, count):
    c = ifc_ref[0:1, :]
    code = jnp.where(c >= 0, 2 + 4 * (c - (position + 1) * count) + ifc_ref[1:2, :], 1)
    return spread_rows(code)


def far_row(c, s, count):
    return 5 * count + 5 * (c // 2) + s


def pack_kernel(part_ref, co_ref, far_co_ref, send_ref, near_ref):
    refs = (co_ref, far_co_ref)
    count = co_ref.shape[0]
    n = part_ref.shape[0]
    send_ref[:n] = part_ref[...]
    h = []
    for q in range(Q):
        h0 = jnp.concatenate([r[:, q, 0, :] for r in refs], axis=0)
        h1 = (1.0 - 0.5) * h0 + 0.5 * jnp.concatenate([r[:, q, 1, :] for r in refs], axis=0)
        h.append(jnp.concatenate([h0, h1], axis=1))
    e = feq(h)
    send_ref[n] = jnp.zeros_like(send_ref[n])
    near_ref[...] = jnp.zeros_like(near_ref)
    upper = lanes(1)[0]
    for s, q in enumerate(CROSSING[2]):
        v = e[q] + (0.6 / 1.1) * (h[q] - e[q])
        for c in range(count):
            send_ref[n, 5 * c + s : 5 * c + s + 1, :] = v[c : c + 1]
            near_ref[5 * c + s : 5 * c + s + 1, :] = v[count + c : count + c + 1]
        turned = roll(v, 64)
        for c in range(0, count, 2):
            other = min(c + 1, count - 1)
            to = far_row(c, s, count)
            send_ref[n, to : to + 1, :] = jnp.where(upper, turned[count + other : count + other + 1], v[count + c : count + c + 1])


def both_halves(x, upper):
    half = lanes(x.shape[0])[0]
    return jnp.where(half, x, roll(x, 64)) if upper else jnp.where(half, roll(x, 64), x)


def spread_matrix(tiles):
    kk = lax.broadcasted_iota(I32, (256, LANES), 0)
    ll = lax.broadcasted_iota(I32, (256, LANES), 1)
    w, m, k = kk >> 6, kk & 63, ll & 7
    out = []
    for t in range(tiles + 1):
        i = (ll >> 6) * 7 if t == tiles else 2 * t + (ll >> 6)
        want = 8 * (4 * (w >> 1) + (i >> 1)) + 4 * (w & 1) + (k >> 1)
        out.append(jnp.where(m == want, 1.0, 0.0).astype(BF16))
    return out


def rows_of(cg):
    return lambda c, s: cg[5 * c + s : 5 * c + s + 1, :]


def coarse_rows(code, cg, count):
    half = lanes(code.shape[0])[0]
    hi, lo = [], []
    for s in range(5):
        parts = []
        for pair in (0, 2):
            acc = jnp.zeros_like(code)
            for c in range(count):
                want = jnp.where(half, 3.0 + 4 * c + pair, 2.0 + 4 * c + pair)
                acc = jnp.where(code == want, cg(c, s), acc)
            parts.append(acc)
        x = jnp.concatenate(parts, axis=1)
        h = x.astype(BF16)
        hi.append(h)
        lo.append((x - h.astype(F32)).astype(BF16))
    return jnp.concatenate(hi + lo, axis=0)


def coarse_tile(rows, matrix):
    g = dot(rows, matrix)
    n = g.shape[0] // 2
    g = g[:n] + g[n:]
    b = n // 5
    return [g[b * s : b * (s + 1)] for s in range(5)]


def pull(q, t, x, parts, gx, bits, bounced):
    if q == 0:
        return x[t]
    half, j, k = lanes(bits.shape[0])
    ex, ey, ez = VEL[q]
    turn = 64 * abs(ex)
    out = roll(sources(q, t, x, gx, half), turn + 8 * ey + ez)
    _, cy, cz = edges(q, t, len(x), half, j, k)
    if ey:
        g = parts[1]
        out = jnp.where(cy, roll(sources(q, t, g, g[t], half), turn - 56 * ey + ez), out)
    if ez:
        g = parts[2]
        out = jnp.where(cz, roll(sources(q, t, g, g[t], half), turn + 8 * ey - 7 * ez), out)
    return jnp.where((bits & (1 << q)) != 0, bounced, out)


def gathers(q, x, hot, fine, remote):
    ex, ey, ez = VEL[q]
    gx, gy, gz = None, None, None
    if q:
        parts = [split(v) for v in x]
    if ex:
        gx = dot(hot[face_of(0, ex)], parts[0 if ex < 0 else len(x) - 1])
        if remote is not None:
            gx = gx + remote[q]
    if ey:
        gy = [dot(hot[face_of(1, ey)], p) for p in parts]
        if ey < 0 and fine is not None:
            s = CROSSING[2].index(q)
            gy = [g + fine(s, t) for t, g in enumerate(gy)]
    if ez:
        gz = [dot(hot[face_of(2, ez)], p) for p in parts]
    return gx, gy, gz


def corners(q, half, j, k):
    _, cy, cz = edges(q, 0, 0, half, j, k)
    return cy if cz is None else (cz if cy is None else cy | cz)


def groups(blocks):
    return [slice(g, g + 8) for g in range(0, blocks, 8)]


def prepare_side(side, load, nbr_ref, solid, bits_put, post_ref, send_ref, hot, absent, code, first, ready=None):
    tiles = len(solid)
    blocks = solid[0].shape[0]
    t = tiles - 1 if side == 0 else 0
    half, j, k = lanes(blocks)
    bits = bounce_bits(t, solid, absent)
    bits_put(t, bits)
    if ready is not None:
        ready()

    for r in groups(blocks):
        out = kept([load(q, r, t) for q in range(Q)], solid[t][r] != 0)
        for q in range(Q):
            post_ref[side, q, r, :] = out[q]
    to = send_rows(nbr_ref[side : side + 1, :], first + (blocks if side == 0 else -blocks), blocks, send_ref.shape[1])
    actual = list(range(Q)) if side == 1 else MIRROR
    streamed = []
    for c in LAYER:
        q = actual[c]
        ex, ey, ez = VEL[q]
        x = post_ref[side, q]
        turn = 64 * abs(ex)
        out = roll(x, turn + 8 * ey + ez)
        _, cy, cz = edges(q, t, tiles, half, j, k)
        if ey or ez:
            parts = split(x)
        if ey:
            out = jnp.where(cy, roll(dot(hot[face_of(1, ey)], parts), turn - 56 * ey + ez), out)
        if ez:
            out = jnp.where(cz, roll(dot(hot[face_of(2, ez)], parts), turn + 8 * ey - 7 * ez), out)
        if q:
            out = jnp.where((bits & (1 << q)) != 0, post_ref[side, OPP[q]], out)
        streamed.append((c, out))
    for c in range(Q):
        corner = corners(c, half, j, k)
        if VEL[c][0] > 0 and corner is not None:
            streamed.append((c, jnp.where(corner, post_ref[side, OPP[actual[c]]], 0.0)))
    faces = [post_ref[side, actual[c]] for c in FACE]
    faces[FACE.index(CODED)] = jnp.where(j == 0, code, faces[FACE.index(CODED)])
    slots = faces + shares(streamed)
    for s in range(0, len(slots), 2):
        a, b = slots[s], slots[min(s + 1, len(slots) - 1)]
        packed = jnp.where(half, b, roll(a, 64)) if side == 0 else jnp.where(half, roll(b, 64), a)
        send_ref[s // 2] = dot(to, split(packed))


def outer_kernel(pop_hbm, *refs):
    given, (post_ref, bits_ref, co_ref, send_ref), (tile_ref, *small_refs, sem) = refs[:4], refs[4:8], refs[8:]
    nbr_ref, ifc_ref, solid_ref = small_refs
    position = lax.axis_index("blk")
    blocks = solid_ref.shape[0]
    tiles = solid_ref.shape[1] // LANES
    even = position % 2 == 0
    mine = pl.ds(pl.multiple_of(jnp.where(even, 0, LANES * (tiles - 1)), LANES), LANES)
    pairs = [(pop_hbm.at[:, :, mine], tile_ref), *zip(given, (*small_refs, co_ref))]
    copies = [pltpu.make_async_copy(a, b, sem.at[i]) for i, (a, b) in enumerate(pairs)]
    for copy in copies[1:] + copies[:1]:
        copy.start()
    for copy in copies[1:]:
        copy.wait()
    first = position * blocks
    code = coarse_code(ifc_ref, position, co_ref.shape[0])
    absent = absences(nbr_ref, ifc_ref)
    hot = local_hots(nbr_ref, first)
    solid = [solid_ref[:, LANES * t : LANES * (t + 1)] for t in range(tiles)]

    def load(q, r, t):
        return tile_ref[q, r, :]

    def put(t, bits):
        bits_ref[...] = bits

    for side in (0, 1):

        @pl.when(position % 2 == 1 - side)
        def _(side=side):
            prepare_side(side, load, nbr_ref, solid, put, post_ref, send_ref, hot, absent, code, first, copies[0].wait)


def inner_kernel(pop_ref, nbr_ref, ifc_ref, solid_ref, ahead_ref, abits_ref, cur_ref, bits_ref, code_ref, spread_ref, take_ref, send_ref, own_ref, hot_ref, mid_ref, outer_ref, *, count):
    position = lax.axis_index("blk")
    blocks = solid_ref.shape[0]
    tiles = solid_ref.shape[1] // LANES
    first = position * blocks
    span = [slice(LANES * t, LANES * (t + 1)) for t in range(tiles)]
    code = coarse_code(ifc_ref, position, count)
    code_ref[...] = code
    absent = absences(nbr_ref, ifc_ref)
    hot = local_hots(nbr_ref, first)
    solid = [solid_ref[:, span[t]] for t in range(tiles)]

    def load(q, r, t):
        return pop_ref[q, r, span[t]]

    def put(t, bits):
        bits_ref[:, span[t]] = bits

    for t, m in enumerate(spread_matrix(tiles)):
        spread_ref[t] = m
    cap = take_ref.shape[2] // 2
    take_ref[0] = take_rows(nbr_ref[0:1, :], first + blocks, blocks, cap)
    take_ref[1] = take_rows(nbr_ref[1:2, :], first - blocks, blocks, cap)
    for t in range(1, tiles - 1):
        put(t, bounce_bits(t, solid, absent))
    for side in (0, 1):

        @pl.when(position % 2 == side)
        def _(side=side):
            prepare_side(side, load, nbr_ref, solid, put, outer_ref, send_ref, hot, absent, code, first)
            outer_ref[1 - side] = ahead_ref[1 - side]
            put(0 if side == 0 else tiles - 1, abits_ref[...])

    for t in range(1, tiles - 1):
        for r in groups(blocks):
            out = kept([pop_ref[q, r, span[t]] for q in range(Q)], solid[t][r] != 0)
            for q in range(Q):
                mid_ref[t - 1, q, r, :] = out[q]

    for d in range(6):
        hot_ref[d] = hot[d]
    half, j, k = lanes(blocks)
    items = []
    for q in range(Q):
        if VEL[q][0] > 0:
            turn = 64 + 8 * VEL[q][1] + VEL[q][2]
            v = jnp.where(half, roll(outer_ref[1, MIRROR[q]], turn), roll(outer_ref[0, q], turn))
            corner = corners(q, half, j, k)
            items.append((q, v if corner is None else jnp.where(corner, 0.0, v)))
    for i, v in enumerate(shares(items)):
        own_ref[i] = v

    def post(q, t):
        if t == 0:
            return outer_ref[1, q]
        return outer_ref[0, q] if t == tiles - 1 else mid_ref[t - 1, q]

    for q in range(Q):
        x = [post(q, t) for t in range(tiles)]
        ghosts = gathers(q, x, hot, None, None)
        for t in range(tiles):
            cur_ref[q, :, span[t]] = pull(
                q, t, x, ghosts, ghosts[0], bits_ref[:, span[t]], post(OPP[q], t)
            )


def current_kernel(cur_ref, own_ref, code_ref, spread_ref, take_ref, near_ref, bits_ref, ra_ref, rb_ref, post_ref, fine_ref, ghost_ref, codes_ref, got_ref, now_ref, *, count):
    position = lax.axis_index("blk")
    blocks, cells = cur_ref.shape[1:]
    tiles = cells // LANES
    even = position % 2 == 0
    half, j, k = lanes(blocks)
    span = [slice(LANES * t, LANES * (t + 1)) for t in range(tiles)]
    n = ra_ref.shape[0]

    for s in range(n):
        got_ref[0, s] = dot(take_ref[0], split(jnp.where(even, ra_ref[s], rb_ref[s])))
        got_ref[1, s] = dot(take_ref[1], split(jnp.where(even, rb_ref[s], ra_ref[s])))

    def from_next(s):
        return got_ref[0, s // 2] if s % 2 == 0 else roll(got_ref[0, s // 2], 64)

    def from_prev(s):
        return got_ref[1, s // 2] if s % 2 == 1 else roll(got_ref[1, s // 2], 64)

    up = {q: from_next(s) for s, q in enumerate(FACE)}
    low = {MIRROR[q]: from_prev(s) for s, q in enumerate(FACE)}
    code = code_ref[...]
    up_code = jnp.broadcast_to(up[CODED][:, 0:1], code.shape)
    low_code = jnp.broadcast_to(low[MIRROR[CODED]][:, 64:65], code.shape)
    codes_ref[0] = up_code
    codes_ref[1] = low_code
    near = jnp.where(even, near_ref[...], rb_ref[n])

    rows = coarse_rows(code, rows_of(both_halves(near, False)), count)
    for t in range(tiles):
        for s, v in enumerate(coarse_tile(rows, spread_ref[t])):
            fine_ref[s, :, span[t]] = v
    for q in range(Q):
        ex, ey, ez = VEL[q]
        for t in range(tiles):
            v = cur_ref[q, :, span[t]]
            cx, cy, cz = edges(q, t, tiles, half, j, k)
            if ey < 0:
                f = [fine_ref[CROSSING[2].index(q), :, span[m]] for m in range(tiles)]
                g = roll(sources(q, t, f, f[t], half), 64 * abs(ex) - 56 * ey + ez)
                ok = cy
                if cx is not None:
                    ok = ok & jnp.logical_not(cx)
                if cz is not None:
                    ok = ok & jnp.logical_not(cz)
                v = v + jnp.where(ok, g, 0.0)
            if cx is not None:
                ok = cx
                for c in (cy, cz):
                    if c is not None:
                        ok = ok & jnp.logical_not(c)
                v = v + jnp.where(ok, roll(up[q] if ex < 0 else low[q], 64 + 8 * ey + ez), 0.0)
            now_ref[q, :, span[t]] = v

    for i in range(9):
        ghost_ref[i] = own_ref[i] + jnp.where(half, from_prev(5 + i), from_next(5 + i))

    for t in range(tiles):
        for r in groups(blocks):
            out = kept([now_ref[q, r, span[t]] for q in range(Q)], (bits_ref[r, span[t]] & 1) != 0)
            for q in range(Q):
                post_ref[q, r, span[t]] = out[q]

    rows = coarse_rows(code, rows_of(both_halves(near, True)), count)
    for t in range(tiles):
        for s, v in enumerate(coarse_tile(rows, spread_ref[t])):
            fine_ref[s, :, span[t]] = v


def final_kernel(post_ref, fine_ref, half_ref, codes_ref, bits_ref, spread_ref, sb_ref, rb_ref, relay_ref, hot_ref, out_ref, buf_ref, sem, *, count):
    position = lax.axis_index("blk")
    blocks, cells = bits_ref.shape
    tiles = cells // LANES
    half, j, k = lanes(blocks)
    span = [slice(LANES * t, LANES * (t + 1)) for t in range(tiles)]
    hot = [hot_ref[d] for d in range(6)]
    copies = []

    def emit(q, remote):
        x = [post_ref[q, :, span[t]] for t in range(tiles)]
        ghosts = gathers(q, x, hot, lambda s, t: fine_ref[s, :, span[t]], remote)
        for t in range(tiles):
            buf_ref[q, :, span[t]] = pull(
                q, t, x, ghosts, ghosts[0], bits_ref[:, span[t]], post_ref[OPP[q], :, span[t]]
            )
        copy = pltpu.make_async_copy(buf_ref.at[q], out_ref.at[q], sem.at[q])
        copy.start()
        copies.append(copy)

    for q in range(Q):
        if VEL[q][0] == 0:
            emit(q, None)
    n = rb_ref.shape[0] - 1
    handed = rows_of(both_halves(relay_ref[0], False))
    direct = [both_halves(rb_ref[n], u) for u in (False, True)]

    def far(c, s):
        row = far_row(c, s, count)
        return jnp.where(position % 2 == 0, handed(c, s), direct[c % 2][row : row + 1])

    up_rows = coarse_rows(codes_ref[0], far, count)
    up_fine = coarse_tile(up_rows, spread_ref[tiles])
    low_rows = coarse_rows(codes_ref[1], rows_of(both_halves(sb_ref[n], False)), count)
    low_fine = coarse_tile(low_rows, spread_ref[tiles])
    items = []
    for q in MIXED:
        _, cy, cz = edges(q, 0, tiles, half, j, k)
        ok = cy if cz is None else cy & jnp.logical_not(cz)
        v = jnp.where(half, low_fine[CROSSING[2].index(MIRROR[q])], up_fine[CROSSING[2].index(q)])
        items.append((q, jnp.where(ok, roll(v, VEL[q][2]), 0.0)))
    parts = [half_ref[i] + v for i, v in enumerate(shares(items))]
    remote = {}
    for q, v in finish(parts).items():
        remote[q] = jnp.where(codes_ref[0] > 0.5, v, 0.0)
        remote[MIRROR[q]] = jnp.where(codes_ref[1] > 0.5, v, 0.0)
    for q in range(Q):
        if VEL[q][0]:
            emit(q, remote)
    for copy in copies:
        copy.wait()


def swapped(x, off):
    n = lax.axis_size("blk")
    low = [(i, i + 1) for i in range(off, n - 1, 2)]
    return lax.ppermute(x, "blk", low + [(b, a) for a, b in low])


def held(x):
    return pltpu.with_memory_space_constraint(x, pltpu.VMEM)


def body(populations, coarse_faces, neighbors, interface, solid):
    pop = populations.transpose(1, 0, 2)
    co = coarse_faces.transpose(0, 2, 1, 3)
    nbr, ifc = neighbors.T, interface.T
    blocks, cells = pop.shape[1:]
    count = co.shape[0]
    tiles = cells // LANES
    dense = pl.BlockSpec(memory_space=pltpu.VMEM)
    away = pl.BlockSpec(memory_space=pl.ANY)
    cap = blocks // 2
    room = pltpu.CompilerParams(vmem_limit_bytes=20 << 20)
    sides = pltpu.VMEM((2, Q, blocks, LANES), F32)
    payload = pltpu.VMEM((7, cap, LANES), F32)
    small = (nbr, ifc, solid)
    far_co = swapped(co, 0)
    outer = pl.pallas_call(
        outer_kernel,
        in_specs=[away] * 5,
        out_shape=(sides, pltpu.VMEM((blocks, LANES), I32), pltpu.VMEM(co.shape, F32), payload),
        scratch_shapes=[
            pltpu.VMEM((Q, blocks, LANES), F32),
            *(pltpu.VMEM(a.shape, a.dtype) for a in small),
            pltpu.SemaphoreType.DMA((5,)),
        ],
        compiler_params=pltpu.CompilerParams(vmem_limit_bytes=56 << 20),
        cost_estimate=pl.CostEstimate(flops=20_000_000, bytes_accessed=1_000_000, transcendentals=0),
        name="outer",
    )
    ahead, abits, co, part = outer(pop, *small, co)
    sb, near = pl.pallas_call(
        pack_kernel,
        in_specs=[dense] * 3,
        out_shape=(pltpu.VMEM((8, cap, LANES), F32), pltpu.VMEM((cap, LANES), F32)),
        compiler_params=room,
        name="pack",
    )(held(part), held(co), held(far_co))
    rb = swapped(sb, 1)
    ahead, abits = held(ahead), held(abits)
    inner = pl.pallas_call(
        functools.partial(inner_kernel, count=count),
        in_specs=[dense] * 6,
        out_shape=(
            pltpu.VMEM((Q, blocks, cells), F32),
            pltpu.VMEM((blocks, cells), I32),
            pltpu.VMEM((blocks, LANES), F32),
            pltpu.VMEM((tiles + 1, 256, LANES), BF16),
            pltpu.VMEM((2, blocks, 2 * cap), BF16),
            payload,
            pltpu.VMEM((9, blocks, LANES), F32),
            pltpu.VMEM((6, blocks, 2 * blocks), BF16),
        ),
        scratch_shapes=[pltpu.VMEM((tiles - 2, Q, blocks, LANES), F32), sides],
        compiler_params=room,
        cost_estimate=pl.CostEstimate(flops=100_000_000, bytes_accessed=4_000_000, transcendentals=0),
        name="inner",
    )
    cur, bits, code, spread, take, sa, own, hots = inner(pop, nbr, ifc, solid, ahead, abits)
    ra = swapped(sa, 0)
    relay = swapped(rb[-1:], 0)
    state = pltpu.VMEM((Q, blocks, cells), F32)
    layer = pltpu.VMEM((9, blocks, LANES), F32)
    current = pl.pallas_call(
        functools.partial(current_kernel, count=count),
        in_specs=[dense] * 9,
        out_shape=(state, pltpu.VMEM((5, blocks, cells), F32), layer, pltpu.VMEM((2, blocks, LANES), F32)),
        scratch_shapes=[pltpu.VMEM((2, 7, blocks, LANES), F32), state],
        compiler_params=room,
        cost_estimate=pl.CostEstimate(flops=100_000_000, bytes_accessed=4_000_000, transcendentals=0),
        name="current",
    )
    given = [held(x) for x in (cur, own, code, spread, take, near, bits, ra, rb)]
    post, fine, ghost, codes = current(*given)
    out = pl.pallas_call(
        functools.partial(final_kernel, count=count),
        in_specs=[dense] * 10,
        out_specs=away,
        out_shape=jax.ShapeDtypeStruct(pop.shape, F32),
        scratch_shapes=[state, pltpu.SemaphoreType.DMA((Q,))],
        compiler_params=room,
        name="final",
    )(*(held(x) for x in (post, fine, ghost, codes, bits, spread, sb, rb, relay, hots)))
    return out.transpose(1, 0, 2)


def solution(mesh):
    placed = (P("blk", None, None), P("blk", None, None, None), P("blk", None), P("blk", None), P("blk", None))
    return jax.shard_map(body, mesh=mesh, in_specs=placed, out_specs=P("blk", None, None), check_vma=False)
```
